512 devices in a mesh: seq: 64 (over z, x, core), chan: 8 (over y).
Axes of the slice: x: 4, y: 8, z: 8, core: 2. Of those that a mesh axis runs over, the one named last changes fastest.
Arguments:
- inner_acts: bfloat16 [32768, 4096], P('seq', 'chan')
- gate_input: bfloat16 [32768, 4096], P('seq', 'chan'), may hold values from -6 to 6
- forward_keys: bfloat16 [32768, 128], P('seq'), may hold values from -0.5 to 0.5
- forward_queries: bfloat16 [32768, 128], P('seq'), may hold values from -6 to 6
- backward_keys: bfloat16 [32768, 128], P('seq'), may hold values from -0.5 to 0.5
- backward_queries: bfloat16 [32768, 128], P('seq'), may hold values from -6 to 6
- decay_codes: int32 [2, 128, 64], P(None, 'seq', 'chan'), may hold values from 1 to 98304
- clip_start: int32 [32768], P('seq'), may hold values 0 or 1
- skip_gain: float32 [64], P('chan'), may hold values from 0.3 to 3
- norm_gain: float32 [4096], P('chan'), may hold values from 0.1 to 1.9
- out_weight: bfloat16 [4096, 2048], P('chan'), may hold values from -0.09375 to 0.09375
Outputs:
- mixed: bfloat16 [8192, 2048], P('seq')
The draws below stay inside these ranges and needn't reach their ends.
All inputs are finite; a program needn't handle non-finite values. No bound on the sum of `clip_start` on one device may be relied on, other than what follows from the above.
Results may differ from the reference program's by a relative error of at most 0.01.
Values may be sent and summed in bfloat16 or wider, within the bound.
A program may use at most 128 MiB of HBM per device.

```python
import math
import jax
import jax.numpy as jnp
from jax import lax

D = 2048
E = 4096
H = 64
N = 128
SPAN = 256
POOL = 4
TOK_DEV = 512
P_SIZE = 64
TOKENS = 32768
SPANS = 128
N_SEQ = 64


def draw_inner_acts(key, part):
    first, second = jax.random.split(key, 2)
    column = jnp.arange(E, dtype=jnp.float32) / E
    spread = jax.random.uniform(second, (1, E), jnp.float32, 0.5, 2.0)
    col_scale = 10.0 ** (column[None, :] - 0.5) * spread
    values = jax.random.normal(first, (TOKENS, E), jnp.float32) * col_scale
    return values.astype(jnp.bfloat16)


def draw_decay_codes(key, part):
    first, second, third = jax.random.split(jax.random.fold_in(key, 7), 3)
    slow = jax.random.randint(first, (2, 1, H), 0, 2)
    slow_codes = jax.random.randint(second, (2, SPANS, H), 1, 65)
    fast_codes = jax.random.randint(third, (2, SPANS, H), TOKENS, 3 * TOKENS + 1)
    return jnp.where(slow == 1, slow_codes, fast_codes).astype(jnp.int32)


def place_ends(values, own_key, smallest, top_value):
    longest = values.shape.index(max(values.shape))
    spots = []
    for shift in (0, 1):
        where = [jax.random.randint(jax.random.fold_in(own_key, axis), (), 0, length) for axis, length in enumerate(values.shape)]
        where[longest] = (where[longest] + shift) % values.shape[longest]
        spots.append(tuple(where))
    return values.at[spots[0]].set(smallest).at[spots[1]].set(top_value)


def block_scale(rng, shape, shards, low, top_value):
    level = 1.0
    for position, shards_of in shards:
        heights = jax.random.uniform(jax.random.fold_in(jax.random.fold_in(rng, 6), position), (shards_of,), jnp.float32, low / len(shards), top_value / len(shards))
        level = level * jnp.repeat(jnp.exp(heights), shape[position] // shards_of).reshape((-1,) + (1,) * (len(shape) - 1 - position))
    return level


def noise(rng, shape, width, most, shards=(), kind=jnp.bfloat16):
    values = width * jax.random.normal(rng, shape, jnp.float32)
    if shards:
        values = values * block_scale(rng, shape, shards, -0.22, 0.18)
    return jnp.clip(values, -most, most).astype(kind)


def setup_inputs(seed: int = 0) -> dict:
    arg_keys = jax.random.split(jax.random.key(seed), 12)
    inner_acts = draw_inner_acts(jax.random.fold_in(arg_keys[11], 71), 0)
    gate_input = noise(arg_keys[1], (TOKENS, E), 1.0, 6.0, ((0, 64), (1, 8)))
    forward_keys = noise(arg_keys[2], (TOKENS, N), N ** -0.5, 0.5, ((0, 64),))
    forward_queries = noise(arg_keys[3], (TOKENS, N), 1.0, 6.0, ((0, 64),))
    backward_keys = noise(arg_keys[4], (TOKENS, N), N ** -0.5, 0.5, ((0, 64),))
    backward_queries = noise(arg_keys[5], (TOKENS, N), 1.0, 6.0, ((0, 64),))
    decay_codes = draw_decay_codes(jax.random.fold_in(arg_keys[11], 71), 0)
    clip_start = place_ends((jax.random.randint(arg_keys[7], (TOKENS,), 0, TOKENS) < 4).astype(jnp.int32), jax.random.fold_in(arg_keys[7], 1), 0, 1)
    skip_gain = jnp.clip(jnp.exp(math.log(3.0) - 2.3025851 * jax.random.uniform(arg_keys[8], (H,), jnp.float32) ** block_scale(arg_keys[8], (H,), ((0, 8),), -0.2, 0.2)), 0.3, 3.0)
    norm_gain = jnp.clip(1.0 + 0.18 * jax.random.normal(arg_keys[9], (E,), jnp.float32), 0.1, 1.9)
    out_weight = noise(arg_keys[10], (E, D), E ** -0.5, 0.09375, ((0, 8),))
    return dict(inner_acts=inner_acts, gate_input=gate_input, forward_keys=forward_keys, forward_queries=forward_queries, backward_keys=backward_keys, backward_queries=backward_queries, decay_codes=decay_codes, clip_start=clip_start, skip_gain=skip_gain, norm_gain=norm_gain, out_weight=out_weight)


def block_terms(acts, keys, queries, logs, scal, starts, forward):
    seg = jnp.cumsum(starts).astype(jnp.int32)
    cum = jnp.cumsum(logs, axis=0)
    excl = cum - logs
    scores = jnp.dot(queries, keys.T, preferred_element_type=jnp.float32)
    length = keys.shape[0]
    rows_idx = lax.broadcasted_iota(jnp.int32, (length, length), 0)
    cols_idx = lax.broadcasted_iota(jnp.int32, (length, length), 1)
    same = seg[:, None] == seg[None, :]
    cumt = cum.T
    exct = excl.T
    if forward:
        inside = same & (cols_idx <= rows_idx)
        expo = cumt[:, :, None] - cumt[:, None, :]
    else:
        inside = same & (cols_idx >= rows_idx)
        expo = exct[:, None, :] - exct[:, :, None]
    factor = jnp.exp(jnp.where(inside[None], expo, -jnp.inf))
    weights = (factor * scores[None] * scal.T[:, None, :]).astype(jnp.bfloat16)
    final = seg[-1]
    top = cum[-1]
    if forward:
        state_w = jnp.exp(jnp.where((seg == final)[:, None], top[None, :] - cum, -jnp.inf))
        carry_w = jnp.exp(jnp.where((seg == 0)[:, None], cum, -jnp.inf))
    else:
        state_w = jnp.exp(jnp.where((seg == 0)[:, None], excl, -jnp.inf))
        carry_w = jnp.exp(jnp.where((seg == final)[:, None], top[None, :] - excl, -jnp.inf))
    keyed = ((state_w * scal).T[:, :, None] * keys.astype(jnp.float32)[None]).astype(jnp.bfloat16)
    passing = jnp.where(final == 0, jnp.exp(top), jnp.zeros_like(top))
    return (weights, keyed, passing, carry_w)

def direction(acts3, keys, queries, logs, scal, starts, forward):
    items = (acts3.reshape(N_SEQ, TOK_DEV, H, P_SIZE), keys.reshape(N_SEQ, TOK_DEV, N), queries.reshape(N_SEQ, TOK_DEV, N), logs.reshape(N_SEQ, TOK_DEV, H), scal.reshape(N_SEQ, TOK_DEV, H), starts.reshape(N_SEQ, TOK_DEV))

    def step(state, item):
        acts, kb, qb, lg, sc, st = item
        weights, keyed, passing, carry_w = block_terms(acts, kb, qb, lg, sc, st, forward)
        acts_f = acts.astype(jnp.float32)
        inner = jnp.einsum('gij,jgp->igp', weights.astype(jnp.float32), acts_f)
        entering = jnp.einsum('in,gnp->igp', qb.astype(jnp.float32), state, precision=lax.Precision.HIGHEST)
        out_rows = inner + carry_w[:, :, None] * entering
        local = jnp.einsum('gjn,jgp->gnp', keyed.astype(jnp.float32), acts_f)
        return (passing[:, None, None] * state + local, out_rows)
    init = jnp.zeros((H, N, P_SIZE), jnp.float32)
    _, outs = lax.scan(step, init, items, reverse=not forward)
    return outs.reshape(TOKENS, H, P_SIZE)

def reference(inner_acts, gate_input, forward_keys, forward_queries, backward_keys, backward_queries, decay_codes, clip_start, skip_gain, norm_gain, out_weight):
    rate = decay_codes.astype(jnp.float32) / (32.0 * TOKENS)
    rate = jnp.repeat(rate, SPAN, axis=1)
    logs = jnp.log1p(-rate)
    scal = jnp.sqrt(rate * (2.0 - rate))
    acts3 = inner_acts.reshape(TOKENS, H, P_SIZE)
    ahead = direction(acts3, forward_keys, forward_queries, logs[0], scal[0], clip_start, True)
    behind = direction(acts3, backward_keys, backward_queries, logs[1], scal[1], clip_start, False)
    total = ahead + behind + skip_gain[None, :, None] * acts3.astype(jnp.float32)
    gated = total.reshape(TOKENS, E) * jax.nn.silu(gate_input.astype(jnp.float32))
    meansq = lax.optimization_barrier(jnp.sum(gated * gated, axis=1)) / E
    hidden = (gated * lax.rsqrt(meansq + 1e-05)[:, None] * norm_gain[None, :]).astype(jnp.bfloat16)
    projected = jnp.dot(hidden, out_weight, preferred_element_type=jnp.float32)
    mixed = lax.optimization_barrier(jnp.sum(projected.reshape(TOKENS // POOL, POOL, D), axis=1)) * (1.0 / POOL)
    return mixed.astype(jnp.bfloat16)
```

```python
import functools

import jax
import jax.numpy as jnp
from jax import lax
from jax.experimental import pallas as pl
from jax.experimental.pallas import tpu as pltpu
from jax.sharding import Mesh
from jax.sharding import PartitionSpec as P

SPAN = 256
POOL = 4
CH = 128
HEAD = 64
LANES = 128
SEQ = ("seq_0", "seq_1", "seq_2")
MESH = pl.DeviceIdType.MESH
F32 = jnp.float32
BF = jnp.bfloat16


def log_keep(rate):
    acc = jnp.full_like(rate, 1.0 / 12)
    for n in range(11, 0, -1):
        acc = acc * rate + 1.0 / n
    return -rate * acc


def dot_t(a, b):
    return lax.dot_general(a, b, (((0,), (0,)), ((), ())), preferred_element_type=F32)


def dot_nt(a, b):
    return lax.dot_general(a, b, (((1,), (1,)), ((), ())), preferred_element_type=F32)


def dot(a, b):
    return jnp.dot(a, b, preferred_element_type=F32)


def chains(n_y):
    far, near = n_y // 2, n_y // 2 - 1
    return ((1, 0, far), (-1, 1, far), (-1, 0, near), (1, 1, near))


def layer_kernel(
    sizes,
    codes_ref,
    skip_ref,
    clip_ref,
    gain_ref,
    acts_hbm,
    gate_hbm,
    fk_hbm,
    fq_hbm,
    bk_hbm,
    bq_hbm,
    w_hbm,
    out_hbm,
    x_ref,
    z_ref,
    fk_ref,
    fq_ref,
    bk_ref,
    bq_ref,
    w_ref,
    y_scr,
    silu_scr,
    st_scr,
    carry_scr,
    cw_scr,
    sbuf,
    recv1,
    pbuf,
    recvp,
    a_scr,
    q_scr,
    zbuf,
    recvz,
    zpbuf,
    recvzp,
    ebuf,
    recv3,
    qbuf,
    recvq,
    part,
    rs_send,
    rs_recv,
    obuf,
    in_sem,
    p1s,
    p1r,
    pps,
    ppr,
    zs,
    zr,
    zps,
    zpr,
    p3s,
    p3r,
    sqs,
    sqr,
    rss,
    rsr,
    ags,
    agr,
    out_sem,
):
    n_z, n_x, n_c, n_y = sizes
    n_p = n_x * n_c
    tokens, width = x_ref.shape
    n_ch = tokens // CH
    n_sp = tokens // SPAN
    heads = width // HEAD
    tiles = width // LANES
    states = fk_ref.shape[1]
    prow = states // n_p
    total_tokens = n_z * n_x * n_c * tokens
    dim = w_ref.shape[1]
    half = dim // 2
    rows_out = tokens // POOL
    orow = rows_out // n_y

    iz = lax.axis_index("seq_0")
    ix = lax.axis_index("seq_1")
    ic = lax.axis_index("seq_2")
    iy = lax.axis_index("chan")
    me = ix * n_c + ic

    def plane_peer(k, sign=1):
        px = lax.rem(ix + sign * (k // n_c) + n_x, n_x)
        pc = lax.rem(ic + sign * (k % n_c) + n_c, n_c)
        return px, pc, px * n_c + pc

    def z_peer(k, sign=1):
        return lax.rem(iz + sign * k + n_z, n_z)

    def y_peer(k, sign=1):
        return lax.rem(iy + sign * k + 2 * n_y, n_y)

    barrier = pltpu.get_barrier_semaphore()
    for k in range(1, n_p):
        px, pc, _ = plane_peer(k)
        pl.semaphore_signal(
            barrier, inc=1, device_id={"seq_1": px, "seq_2": pc}, device_id_type=MESH
        )
    for k in range(1, n_z):
        pl.semaphore_signal(barrier, inc=1, device_id={"seq_0": z_peer(k)}, device_id_type=MESH)
    for k in range(1, n_y):
        pl.semaphore_signal(barrier, inc=1, device_id={"chan": y_peer(k)}, device_id_type=MESH)

    loads = [
        pltpu.make_async_copy(src, dst, in_sem.at[n])
        for n, (src, dst) in enumerate(
            (
                (acts_hbm, x_ref),
                (fk_hbm, fk_ref),
                (bk_hbm, bk_ref),
                (fq_hbm, fq_ref),
                (bq_hbm, bq_ref),
                (gate_hbm, z_ref),
                (w_hbm, w_ref),
            )
        )
    ]
    for load in loads:
        load.start()

    low = lax.broadcasted_iota(jnp.int32, (1, LANES), 1) < HEAD
    logs, scal = [], []
    for d in range(2):
        logs.append([])
        scal.append([])
        for s in range(n_sp):
            rates = [
                jnp.full((1, LANES), codes_ref[d, s, h].astype(F32)) * (1.0 / (32.0 * total_tokens))
                for h in range(heads)
            ]
            logs[d].append([log_keep(r) for r in rates])
            scal[d].append([jnp.sqrt(r * (2.0 - r)) for r in rates])

    def as_row(items):
        return jnp.concatenate(
            [jnp.where(low, items[2 * t], items[2 * t + 1]) for t in range(tiles)], axis=1
        )

    log_row = [[as_row(logs[d][s]) for s in range(n_sp)] for d in range(2)]
    scal_row = [[as_row(scal[d][s]) for s in range(n_sp)] for d in range(2)]

    rows = lax.broadcasted_iota(jnp.int32, (CH, CH), 0)
    cols = lax.broadcasted_iota(jnp.int32, (CH, CH), 1)
    lower = rows >= cols
    upper = rows <= cols
    starts = clip_ref[...].astype(F32).astype(BF)
    seg_row = dot(starts, upper.astype(F32).astype(BF))
    seg_col = dot_nt(lower.astype(F32).astype(BF), starts)
    seg_c = [seg_col[:, a : a + 1] for a in range(n_ch)]
    fin = [seg_row[a : a + 1, CH - 1 : CH] for a in range(n_ch)]
    first_m = [(seg_c[a] == 0.0).astype(F32) for a in range(n_ch)]
    last_m = [(seg_c[a] == fin[a]).astype(F32) for a in range(n_ch)]
    clear = [(fin[a] == 0.0).astype(F32) for a in range(n_ch)]
    passing = [
        [jnp.exp(float(CH) * log_row[d][a * CH // SPAN]) * clear[a] for a in range(n_ch)]
        for d in range(2)
    ]

    step_f = lax.broadcasted_iota(jnp.int32, (CH, width), 0).astype(F32)
    grow = (
        [jnp.exp(log_row[0][s] * (CH - 1.0 - step_f)) * scal_row[0][s] for s in range(n_sp)],
        [jnp.exp(log_row[1][s] * step_f) * scal_row[1][s] for s in range(n_sp)],
    )
    for n in range(3):
        loads[n].wait()

    def chunk(a):
        return pl.ds(a * CH, CH)

    total_pass = []
    for d in range(2):
        keys_ref = (fk_ref, bk_ref)[d]
        mask = (last_m, first_m)[d]
        order = range(n_ch) if d == 0 else range(n_ch - 1, -1, -1)
        state, through = None, None
        for a in order:
            if state is None:
                st_scr[d, a] = jnp.zeros((states, width), F32)
                carry_scr[d, a] = jnp.ones((8, width), F32)
            else:
                st_scr[d, a] = state
                carry_scr[d, a] = jnp.broadcast_to(through, (8, width))
            scaled = (x_ref[chunk(a), :].astype(F32) * (grow[d][a * CH // SPAN] * mask[a])).astype(BF)
            local = dot_t(keys_ref[chunk(a), :], scaled)
            state = local if state is None else passing[d][a] * state + local
            through = passing[d][a] if through is None else passing[d][a] * through
        for j in range(n_p):
            sbuf[j, d] = state[j * prow : (j + 1) * prow, :].astype(BF)
        for t in range(tiles):
            pbuf[d * tiles + t : d * tiles + t + 1, :] = through[:, t * LANES : (t + 1) * LANES]

    pl.semaphore_wait(barrier, (n_p - 1) + (n_z - 1) + (n_y - 1))

    def p1_copies(k):
        px, pc, pj = plane_peer(k)
        where = {"seq_1": px, "seq_2": pc}
        return (
            pltpu.make_async_remote_copy(
                pbuf, recvp.at[me], pps.at[k], ppr.at[k], device_id=where, device_id_type=MESH
            ),
            pltpu.make_async_remote_copy(
                sbuf.at[pj], recv1.at[me], p1s.at[k], p1r.at[k], device_id=where, device_id_type=MESH
            ),
        )

    def p1_arrivals(k):
        px, pc, pj = plane_peer(k, -1)
        where = {"seq_1": px, "seq_2": pc}
        return (
            pltpu.make_async_remote_copy(
                pbuf, recvp.at[pj], pps.at[k], ppr.at[k], device_id=where, device_id_type=MESH
            ),
            pltpu.make_async_remote_copy(
                sbuf.at[pj], recv1.at[pj], p1s.at[k], p1r.at[k], device_id=where, device_id_type=MESH
            ),
        )

    sent = []
    far_first = sorted(range(1, n_p), key=lambda k: -min(k // n_c, n_x - k // n_c))
    for k in far_first:
        for copy in p1_copies(k):
            copy.start()
            sent.append(copy)
    recv1[me] = sbuf[me]
    recvp[me] = pbuf[...]

    loads[3].wait()
    loads[4].wait()
    apart = jnp.abs(rows - cols).astype(F32)
    left_m = jnp.where(low, 1.0, 0.0).astype(BF)
    right_m = jnp.where(low, 0.0, 1.0).astype(BF)
    for s in range(n_sp):
        decay = [
            jnp.exp(apart * jnp.where(lower, logs[0][s][h], logs[1][s][h])) for h in range(heads)
        ]
        for a in range(s * SPAN // CH, (s + 1) * SPAN // CH):
            same = seg_c[a] == seg_row[a : a + 1, :]
            ahead = jnp.where(
                same & lower, dot_nt(fq_ref[chunk(a), :], fk_ref[chunk(a), :]), 0.0
            )
            behind = jnp.where(
                same & upper, dot_nt(bq_ref[chunk(a), :], bk_ref[chunk(a), :]), 0.0
            )
            for t in range(tiles):
                pair = jnp.concatenate(
                    [
                        (
                            decay[h] * (scal[0][s][h] * ahead + scal[1][s][h] * behind)
                        ).astype(BF)
                        for h in (2 * t, 2 * t + 1)
                    ],
                    axis=1,
                )
                lanes = pl.ds(t * LANES, LANES)
                xt = x_ref[chunk(a), lanes]
                both = jnp.concatenate([xt * left_m, xt * right_m], axis=0)
                skip = jnp.where(low, skip_ref[2 * t], skip_ref[2 * t + 1])
                y_scr[chunk(a), lanes] = dot(pair, both) + skip * xt.astype(F32)

    for k in range(1, n_p):
        for copy in p1_arrivals(k):
            copy.wait_recv()

    def pass_row(ref, d):
        return jnp.concatenate(
            [ref[d * tiles + t : d * tiles + t + 1, :] for t in range(tiles)], axis=1
        )

    for d in range(2):
        order = range(n_p) if d == 0 else range(n_p - 1, -1, -1)
        state = jnp.zeros((prow, width), F32)
        through = jnp.ones((1, width), F32)
        for q in order:
            a_scr[d, q] = state
            q_scr[d, q] = jnp.broadcast_to(through, (8, width))
            factor = pass_row(recvp.at[q], d)
            state = factor * state + recv1[q, d].astype(F32)
            through = factor * through
        zbuf[d] = state.astype(BF)
        for t in range(tiles):
            zpbuf[d * tiles + t : d * tiles + t + 1, :] = through[:, t * LANES : (t + 1) * LANES]

    def z_copies(k):
        pz = z_peer(k)
        where = {"seq_0": pz}
        d = jnp.where(pz > iz, 0, 1)
        return (
            pltpu.make_async_remote_copy(
                zpbuf, recvzp.at[iz], zps.at[k], zpr.at[k], device_id=where, device_id_type=MESH
            ),
            pltpu.make_async_remote_copy(
                zbuf.at[d], recvz.at[iz], zs.at[k], zr.at[k], device_id=where, device_id_type=MESH
            ),
        )

    def z_arrivals(k):
        pz = z_peer(k, -1)
        where = {"seq_0": pz}
        return (
            pltpu.make_async_remote_copy(
                zpbuf, recvzp.at[pz], zps.at[k], zpr.at[k], device_id=where, device_id_type=MESH
            ),
            pltpu.make_async_remote_copy(
                zbuf.at[0], recvz.at[pz], zs.at[k], zr.at[k], device_id=where, device_id_type=MESH
            ),
        )

    for k in sorted(range(1, n_z), key=lambda k: -min(k, n_z - k)):
        for copy in z_copies(k):
            copy.start()
            sent.append(copy)
    recvz[iz] = jnp.zeros((prow, width), BF)
    recvzp[iz] = zpbuf[...]

    loads[5].wait()
    for a in range(n_ch):
        v = z_ref[chunk(a), :].astype(F32)
        silu_scr[chunk(a), :] = v / (1.0 + jnp.exp(-v))
    for s in range(n_sp):
        cw_scr[0, s] = jnp.exp(log_row[0][s] * (step_f + 1.0))
        cw_scr[1, s] = jnp.exp(log_row[1][s] * (float(CH) - step_f))

    for k in range(1, n_z):
        for copy in z_arrivals(k):
            copy.wait_recv()

    for d in range(2):
        state = jnp.zeros((prow, width), F32)
        for q in range(n_z) if d == 0 else range(n_z - 1, -1, -1):
            new = pass_row(recvzp.at[q], d) * state + recvz[q].astype(F32)
            state = jnp.where(q < iz if d == 0 else q > iz, new, state)
        for q in range(n_p):
            ebuf[q, d] = (a_scr[d, q] + q_scr[d, q][0:1, :] * state).astype(BF)

    def p3_copy(k, sign=1):
        px, pc, pj = plane_peer(k, sign)
        return pltpu.make_async_remote_copy(
            ebuf.at[pj],
            recv3.at[me if sign == 1 else pj],
            p3s.at[k],
            p3r.at[k],
            device_id={"seq_1": px, "seq_2": pc},
            device_id_type=MESH,
        )

    for k in far_first:
        copy = p3_copy(k)
        copy.start()
        sent.append(copy)
    recv3[me] = ebuf[me]
    for k in range(1, n_p):
        p3_copy(k, -1).wait_recv()

    for a in range(n_ch):
        s = a * CH // SPAN
        for d in range(2):
            entering = jnp.concatenate([recv3[q, d] for q in range(n_p)], axis=0).astype(F32)
            state = st_scr[d, a] + carry_scr[d, a][0:1, :] * entering
            mask = (first_m, last_m)[d]
            queries = (fq_ref, bq_ref)[d][chunk(a), :]
            y_scr[chunk(a), :] += (cw_scr[d, s] * mask[a]) * dot(queries, state.astype(BF))
        gated = y_scr[chunk(a), :] * silu_scr[chunk(a), :]
        y_scr[chunk(a), :] = gated
        squares = gated * gated
        lanes_sum = squares[:, :LANES]
        for t in range(1, tiles):
            lanes_sum = lanes_sum + squares[:, t * LANES : (t + 1) * LANES]
        qbuf[a : a + 1, :] = jnp.sum(lanes_sum.T, axis=0, keepdims=True)

    def q_copy(k, sign=1):
        py = y_peer(k, sign)
        return pltpu.make_async_remote_copy(
            qbuf,
            recvq.at[iy if sign == 1 else py],
            sqs.at[k],
            sqr.at[k],
            device_id={"chan": py},
            device_id_type=MESH,
        )

    for k in sorted(range(1, n_y), key=lambda k: -min(k, n_y - k)):
        copy = q_copy(k)
        copy.start()
        sent.append(copy)
    recvq[iy] = qbuf[...]
    for k in range(1, n_y):
        q_copy(k, -1).wait_recv()
    squares = recvq[0]
    for k in range(1, n_y):
        squares = squares + recvq[k]
    inv = lax.rsqrt(squares / float(n_y * width) + 1e-05)

    pool = jnp.where(
        lax.broadcasted_iota(jnp.int32, (CH // POOL, CH), 0)
        == lax.broadcasted_iota(jnp.int32, (CH // POOL, CH), 1) // POOL,
        1.0 / POOL,
        0.0,
    ).astype(BF)
    gain = gain_ref[...]
    pooled = []
    for a in range(n_ch):
        inv_col = jnp.broadcast_to(inv[a : a + 1, :], (CH, LANES)).T
        inv_full = jnp.concatenate([inv_col] * tiles, axis=1)
        hidden = (y_scr[chunk(a), :] * inv_full * gain).astype(BF)
        pooled.append(dot(pool, hidden))
    pooled = jnp.concatenate(pooled, axis=0)
    high = pooled.astype(BF)
    rest = (pooled - high.astype(F32)).astype(BF)
    loads[6].wait()
    for c in range(2):
        cut = pl.ds(c * half, half)
        w = w_ref[:, cut]
        result = dot(high, w) + dot(rest, w)
        for p in range(n_y):
            part[p, :, cut] = result[p * orow : (p + 1) * orow, :]

    links = [c for c in enumerate(chains(n_y)) if c[1][2] > 0]

    def rs_copy(n, sign, s):
        return pltpu.make_async_remote_copy(
            rs_send.at[n, s],
            rs_recv.at[n, s],
            rss.at[n, s],
            rsr.at[n, s],
            device_id={"chan": y_peer(sign)},
            device_id_type=MESH,
        )

    for s in range(n_y // 2):
        for n, (sign, h, length) in links:
            if s >= length:
                continue
            cut = pl.ds(h * half, half)
            value = part[y_peer(sign * (length - s)), :, cut]
            if s > 0:
                rs_copy(n, sign, s - 1).wait_recv()
                value = value + rs_recv[n, s - 1].astype(F32)
            rs_send[n, s] = value.astype(BF)
            copy = rs_copy(n, sign, s)
            copy.start()
            sent.append(copy)

    def out_rows(p):
        return pl.ds(pl.multiple_of(p * orow, orow), orow)

    for h in range(2):
        cut = pl.ds(h * half, half)
        value = part[iy, :, cut]
        for n, (sign, hh, length) in links:
            if hh == h:
                rs_copy(n, sign, length - 1).wait_recv()
                value = value + rs_recv[n, length - 1].astype(F32)
        obuf[out_rows(iy), cut] = value.astype(BF)

    def ag_copy(n, sign, h, s, own):
        p = y_peer(-sign * s) if own else y_peer(-sign * (s + 1))
        view = obuf.at[out_rows(p), pl.ds(h * half, half)]
        return pltpu.make_async_remote_copy(
            view,
            view,
            ags.at[n, s],
            agr.at[n, s],
            device_id={"chan": y_peer(sign)},
            device_id_type=MESH,
        )

    for s in range(n_y // 2):
        for n, (sign, h, length) in links:
            if s >= length:
                continue
            if s > 0:
                ag_copy(n, sign, h, s - 1, False).wait_recv()
            copy = ag_copy(n, sign, h, s, True)
            copy.start()
            sent.append(copy)
    for n, (sign, h, length) in links:
        ag_copy(n, sign, h, length - 1, False).wait_recv()
    done = pltpu.make_async_copy(obuf, out_hbm, out_sem)
    done.start()
    for copy in sent:
        copy.wait_send()
    done.wait()


def body(
    inner_acts,
    gate_input,
    forward_keys,
    forward_queries,
    backward_keys,
    backward_queries,
    decay_codes,
    clip_start,
    skip_gain,
    norm_gain,
    out_weight,
):
    sizes = tuple(lax.axis_size(a) for a in SEQ) + (lax.axis_size("chan"),)
    n_z, n_x, n_c, n_y = sizes
    n_p = n_x * n_c
    tokens, width = inner_acts.shape
    states = forward_keys.shape[1]
    dim = out_weight.shape[1]
    n_ch, n_sp = tokens // CH, tokens // SPAN
    prow = states // n_p
    rows_out = tokens // POOL
    orow = rows_out // n_y
    steps = n_y // 2
    vmem = pltpu.VMEM
    dma = pltpu.SemaphoreType.DMA
    any_spec = pl.BlockSpec(memory_space=pl.ANY)
    smem_spec = pl.BlockSpec(memory_space=pltpu.SMEM)
    vmem_spec = pl.BlockSpec(memory_space=pltpu.VMEM)
    scratch = [
        vmem((tokens, width), BF),
        vmem((tokens, width), BF),
        vmem((tokens, states), BF),
        vmem((tokens, states), BF),
        vmem((tokens, states), BF),
        vmem((tokens, states), BF),
        vmem(out_weight.shape, BF),
        vmem((tokens, width), F32),
        vmem((tokens, width), F32),
        vmem((2, n_ch, states, width), F32),
        vmem((2, n_ch, 8, width), F32),
        vmem((2, n_sp, CH, width), F32),
        vmem((n_p, 2, prow, width), BF),
        vmem((n_p, 2, prow, width), BF),
        vmem((8, LANES), F32),
        vmem((n_p, 8, LANES), F32),
        vmem((2, n_p, prow, width), F32),
        vmem((2, n_p, 8, width), F32),
        vmem((2, prow, width), BF),
        vmem((n_z, prow, width), BF),
        vmem((8, LANES), F32),
        vmem((n_z, 8, LANES), F32),
        vmem((n_p, 2, prow, width), BF),
        vmem((n_p, 2, prow, width), BF),
        vmem((n_ch, LANES), F32),
        vmem((n_y, n_ch, LANES), F32),
        vmem((n_y, orow, dim), F32),
        vmem((4, steps, orow, dim // 2), BF),
        vmem((4, steps, orow, dim // 2), BF),
        vmem((rows_out, dim), BF),
        dma((7,)),
        dma((n_p,)),
        dma((n_p,)),
        dma((n_p,)),
        dma((n_p,)),
        dma((n_z,)),
        dma((n_z,)),
        dma((n_z,)),
        dma((n_z,)),
        dma((n_p,)),
        dma((n_p,)),
        dma((n_y,)),
        dma((n_y,)),
        dma((4, steps)),
        dma((4, steps)),
        dma((4, steps)),
        dma((4, steps)),
        dma,
    ]
    return pl.pallas_call(
        functools.partial(layer_kernel, sizes),
        out_shape=jax.ShapeDtypeStruct((rows_out, dim), BF),
        in_specs=[smem_spec, smem_spec, vmem_spec, vmem_spec] + [any_spec] * 7,
        out_specs=any_spec,
        scratch_shapes=scratch,
        compiler_params=pltpu.CompilerParams(
            collective_id=0, has_side_effects=True, vmem_limit_bytes=40 << 20
        ),
        name="layer",
    )(
        decay_codes,
        skip_gain,
        clip_start.reshape(n_ch, CH),
        norm_gain.reshape(1, width),
        inner_acts,
        gate_input,
        forward_keys,
        forward_queries,
        backward_keys,
        backward_queries,
        out_weight,
    )


def solution(mesh):
    torus = Mesh(
        mesh.devices.reshape(8, 4, 2, mesh.shape["chan"]), ("seq_0", "seq_1", "seq_2", "chan")
    )
    return jax.shard_map(
        body,
        mesh=torus,
        in_specs=(
            P(SEQ, "chan"),
            P(SEQ, "chan"),
            P(SEQ, None),
            P(SEQ, None),
            P(SEQ, None),
            P(SEQ, None),
            P(None, SEQ, "chan"),
            P(SEQ),
            P("chan"),
            P("chan"),
            P("chan", None),
        ),
        out_specs=P(SEQ, None),
        check_vma=False,
    )
```

```python
import functools

import jax
import jax.numpy as jnp
from jax import lax
from jax.experimental import pallas as pl
from jax.experimental.pallas import tpu as pltpu
from jax.sharding import Mesh
from jax.sharding import PartitionSpec as P

SPAN = 256
POOL = 4
CH = 128
HEAD = 64
LANES = 128
CUTS = 4
SEQ = ("seq_0", "seq_1", "seq_2")
MESH = pl.DeviceIdType.MESH
F32 = jnp.float32
BF = jnp.bfloat16


def log_keep(rate):
    acc = jnp.full_like(rate, 1.0 / 12)
    for n in range(11, 0, -1):
        acc = acc * rate + 1.0 / n
    return -rate * acc


def dot_t(a, b):
    return lax.dot_general(a, b, (((0,), (0,)), ((), ())), preferred_element_type=F32)


def dot_nt(a, b):
    return lax.dot_general(a, b, (((1,), (1,)), ((), ())), preferred_element_type=F32)


def dot(a, b):
    return jnp.dot(a, b, preferred_element_type=F32)


def chains(n_y, cuts):
    far, near = n_y // 2, n_y // 2 - 1
    out = []
    for c in range(cuts):
        up = far if c % 2 == 0 else near
        out.append((1, c, up))
        out.append((-1, c, far + near - up))
    return [c for c in out if c[2] > 0]


def layer_kernel(
    sizes,
    codes_ref,
    skip_ref,
    clip_ref,
    gain_ref,
    acts_hbm,
    gate_hbm,
    fk_hbm,
    fq_hbm,
    bk_hbm,
    bq_hbm,
    w_hbm,
    out_hbm,
    x_ref,
    z_ref,
    fk_ref,
    fq_ref,
    bk_ref,
    bq_ref,
    w_ref,
    y_scr,
    silu_scr,
    st_scr,
    carry_scr,
    cw_scr,
    sbuf,
    recv1,
    pbuf,
    recvp,
    a_scr,
    q_scr,
    zbuf,
    recvz,
    zpbuf,
    recvzp,
    ebuf,
    recv3,
    qbuf,
    recvq,
    part,
    rs_send,
    rs_recv,
    obuf,
    in_sem,
    p1s,
    p1r,
    pps,
    ppr,
    zs,
    zr,
    zps,
    zpr,
    p3s,
    p3r,
    sqs,
    sqr,
    rss,
    rsr,
    ags,
    agr,
    out_sem,
):
    n_z, n_x, n_c, n_y = sizes
    n_p = n_x * n_c
    tokens, width = x_ref.shape
    n_ch = tokens // CH
    n_sp = tokens // SPAN
    heads = width // HEAD
    tiles = width // LANES
    states = fk_ref.shape[1]
    prow = states // n_p
    total_tokens = n_z * n_x * n_c * tokens
    dim = w_ref.shape[1]
    cut_w = dim // CUTS
    links = list(enumerate(chains(n_y, CUTS)))
    rows_out = tokens // POOL
    orow = rows_out // n_y

    iz = lax.axis_index("seq_0")
    ix = lax.axis_index("seq_1")
    ic = lax.axis_index("seq_2")
    iy = lax.axis_index("chan")
    me = ix * n_c + ic

    def plane_peer(k, sign=1):
        px = lax.rem(ix + sign * (k // n_c) + n_x, n_x)
        pc = lax.rem(ic + sign * (k % n_c) + n_c, n_c)
        return px, pc, px * n_c + pc

    def z_peer(k, sign=1):
        return lax.rem(iz + sign * k + n_z, n_z)

    def y_peer(k, sign=1):
        return lax.rem(iy + sign * k + 2 * n_y, n_y)

    barrier = pltpu.get_barrier_semaphore()
    for k in range(1, n_p):
        px, pc, _ = plane_peer(k)
        pl.semaphore_signal(
            barrier, inc=1, device_id={"seq_1": px, "seq_2": pc}, device_id_type=MESH
        )
    for k in range(1, n_z):
        pl.semaphore_signal(barrier, inc=1, device_id={"seq_0": z_peer(k)}, device_id_type=MESH)
    for k in range(1, n_y):
        pl.semaphore_signal(barrier, inc=1, device_id={"chan": y_peer(k)}, device_id_type=MESH)

    loads = [
        pltpu.make_async_copy(src, dst, in_sem.at[n])
        for n, (src, dst) in enumerate(
            (
                (acts_hbm, x_ref),
                (fk_hbm, fk_ref),
                (bk_hbm, bk_ref),
                (fq_hbm, fq_ref),
                (bq_hbm, bq_ref),
                (gate_hbm, z_ref),
                (w_hbm, w_ref),
            )
        )
    ]
    for load in loads:
        load.start()
    waited = set()

    def need(n):
        waited.add(n)
        loads[n].wait()

    sent = []

    low = lax.broadcasted_iota(jnp.int32, (1, LANES), 1) < HEAD
    logs, scal = [], []
    for d in range(2):
        logs.append([])
        scal.append([])
        for s in range(n_sp):
            rates = [
                jnp.full((1, LANES), codes_ref[d, s, h].astype(F32)) * (1.0 / (32.0 * total_tokens))
                for h in range(heads)
            ]
            logs[d].append([log_keep(r) for r in rates])
            scal[d].append([jnp.sqrt(r * (2.0 - r)) for r in rates])

    def as_row(items):
        return jnp.concatenate(
            [jnp.where(low, items[2 * t], items[2 * t + 1]) for t in range(tiles)], axis=1
        )

    log_row = [[as_row(logs[d][s]) for s in range(n_sp)] for d in range(2)]
    scal_row = [[as_row(scal[d][s]) for s in range(n_sp)] for d in range(2)]

    rows = lax.broadcasted_iota(jnp.int32, (CH, CH), 0)
    cols = lax.broadcasted_iota(jnp.int32, (CH, CH), 1)
    lower = rows >= cols
    upper = rows <= cols
    starts = clip_ref[...].astype(F32).astype(BF)
    seg_row = dot(starts, upper.astype(F32).astype(BF))
    seg_col = dot_nt(lower.astype(F32).astype(BF), starts)
    seg_c = [seg_col[:, a : a + 1] for a in range(n_ch)]
    fin = [seg_row[a : a + 1, CH - 1 : CH] for a in range(n_ch)]
    first_m = [(seg_c[a] == 0.0).astype(F32) for a in range(n_ch)]
    last_m = [(seg_c[a] == fin[a]).astype(F32) for a in range(n_ch)]
    clear = [(fin[a] == 0.0).astype(F32) for a in range(n_ch)]
    passing = [
        [jnp.exp(float(CH) * log_row[d][a * CH // SPAN]) * clear[a] for a in range(n_ch)]
        for d in range(2)
    ]

    step_f = lax.broadcasted_iota(jnp.int32, (CH, width), 0).astype(F32)
    grow = (
        [jnp.exp(log_row[0][s] * (CH - 1.0 - step_f)) * scal_row[0][s] for s in range(n_sp)],
        [jnp.exp(log_row[1][s] * step_f) * scal_row[1][s] for s in range(n_sp)],
    )
    for n in range(3):
        need(n)

    def chunk(a):
        return pl.ds(a * CH, CH)

    total_pass = []
    for d in range(2):
        keys_ref = (fk_ref, bk_ref)[d]
        mask = (last_m, first_m)[d]
        order = range(n_ch) if d == 0 else range(n_ch - 1, -1, -1)
        state, through = None, None
        for a in order:
            if state is None:
                st_scr[d, a] = jnp.zeros((states, width), F32)
                carry_scr[d, a] = jnp.ones((8, width), F32)
            else:
                st_scr[d, a] = state
                carry_scr[d, a] = jnp.broadcast_to(through, (8, width))
            scaled = (x_ref[chunk(a), :].astype(F32) * (grow[d][a * CH // SPAN] * mask[a])).astype(BF)
            local = dot_t(keys_ref[chunk(a), :], scaled)
            state = local if state is None else passing[d][a] * state + local
            through = passing[d][a] if through is None else passing[d][a] * through
        for j in range(n_p):
            sbuf[j, d] = state[j * prow : (j + 1) * prow, :].astype(BF)
        for t in range(tiles):
            pbuf[d * tiles + t : d * tiles + t + 1, :] = through[:, t * LANES : (t + 1) * LANES]

    pl.semaphore_wait(barrier, (n_p - 1) + (n_z - 1) + (n_y - 1))

    def p1_copies(k):
        px, pc, pj = plane_peer(k)
        where = {"seq_1": px, "seq_2": pc}
        return (
            pltpu.make_async_remote_copy(
                pbuf, recvp.at[me], pps.at[k], ppr.at[k], device_id=where, device_id_type=MESH
            ),
            pltpu.make_async_remote_copy(
                sbuf.at[pj], recv1.at[me], p1s.at[k], p1r.at[k], device_id=where, device_id_type=MESH
            ),
        )

    def p1_arrivals(k):
        px, pc, pj = plane_peer(k, -1)
        where = {"seq_1": px, "seq_2": pc}
        return (
            pltpu.make_async_remote_copy(
                pbuf, recvp.at[pj], pps.at[k], ppr.at[k], device_id=where, device_id_type=MESH
            ),
            pltpu.make_async_remote_copy(
                sbuf.at[pj], recv1.at[pj], p1s.at[k], p1r.at[k], device_id=where, device_id_type=MESH
            ),
        )

    far_first = sorted(range(1, n_p), key=lambda k: -min(k // n_c, n_x - k // n_c))
    for k in far_first:
        for copy in p1_copies(k):
            copy.start()
            sent.append(copy)
    recv1[me] = sbuf[me]
    recvp[me] = pbuf[...]

    need(3)
    need(4)
    apart = jnp.abs(rows - cols).astype(F32)
    left_m = jnp.where(low, 1.0, 0.0).astype(BF)
    right_m = jnp.where(low, 0.0, 1.0).astype(BF)
    for s in range(n_sp):
        decay = [
            jnp.exp(apart * jnp.where(lower, logs[0][s][h], logs[1][s][h])) for h in range(heads)
        ]
        for a in range(s * SPAN // CH, (s + 1) * SPAN // CH):
            same = seg_c[a] == seg_row[a : a + 1, :]
            ahead = jnp.where(
                same & lower, dot_nt(fq_ref[chunk(a), :], fk_ref[chunk(a), :]), 0.0
            )
            behind = jnp.where(
                same & upper, dot_nt(bq_ref[chunk(a), :], bk_ref[chunk(a), :]), 0.0
            )
            for t in range(tiles):
                pair = jnp.concatenate(
                    [
                        (
                            decay[h] * (scal[0][s][h] * ahead + scal[1][s][h] * behind)
                        ).astype(BF)
                        for h in (2 * t, 2 * t + 1)
                    ],
                    axis=1,
                )
                lanes = pl.ds(t * LANES, LANES)
                xt = x_ref[chunk(a), lanes]
                both = jnp.concatenate([xt * left_m, xt * right_m], axis=0)
                skip = jnp.where(low, skip_ref[2 * t], skip_ref[2 * t + 1])
                y_scr[chunk(a), lanes] = dot(pair, both) + skip * xt.astype(F32)

    for k in range(1, n_p):
        for copy in p1_arrivals(k):
            copy.wait_recv()

    def pass_row(ref, d):
        return jnp.concatenate(
            [ref[d * tiles + t : d * tiles + t + 1, :] for t in range(tiles)], axis=1
        )

    for d in range(2):
        order = range(n_p) if d == 0 else range(n_p - 1, -1, -1)
        state = jnp.zeros((prow, width), F32)
        through = jnp.ones((1, width), F32)
        for q in order:
            a_scr[d, q] = state
            q_scr[d, q] = jnp.broadcast_to(through, (8, width))
            factor = pass_row(recvp.at[q], d)
            state = factor * state + recv1[q, d].astype(F32)
            through = factor * through
        zbuf[d] = state.astype(BF)
        for t in range(tiles):
            zpbuf[d * tiles + t : d * tiles + t + 1, :] = through[:, t * LANES : (t + 1) * LANES]

    def z_copies(k):
        pz = z_peer(k)
        where = {"seq_0": pz}
        d = jnp.where(pz > iz, 0, 1)
        return (
            pltpu.make_async_remote_copy(
                zpbuf, recvzp.at[iz], zps.at[k], zpr.at[k], device_id=where, device_id_type=MESH
            ),
            pltpu.make_async_remote_copy(
                zbuf.at[d], recvz.at[iz], zs.at[k], zr.at[k], device_id=where, device_id_type=MESH
            ),
        )

    def z_arrivals(k):
        pz = z_peer(k, -1)
        where = {"seq_0": pz}
        return (
            pltpu.make_async_remote_copy(
                zpbuf, recvzp.at[pz], zps.at[k], zpr.at[k], device_id=where, device_id_type=MESH
            ),
            pltpu.make_async_remote_copy(
                zbuf.at[0], recvz.at[pz], zs.at[k], zr.at[k], device_id=where, device_id_type=MESH
            ),
        )

    for k in sorted(range(1, n_z), key=lambda k: -min(k, n_z - k)):
        for copy in z_copies(k):
            copy.start()
            sent.append(copy)
    recvz[iz] = jnp.zeros((prow, width), BF)
    recvzp[iz] = zpbuf[...]

    need(5)
    for a in range(n_ch):
        v = z_ref[chunk(a), :].astype(F32)
        silu_scr[chunk(a), :] = v / (1.0 + jnp.exp(-v))
    for s in range(n_sp):
        cw_scr[0, s] = jnp.exp(log_row[0][s] * (step_f + 1.0))
        cw_scr[1, s] = jnp.exp(log_row[1][s] * (float(CH) - step_f))

    for k in range(1, n_z):
        for copy in z_arrivals(k):
            copy.wait_recv()

    for d in range(2):
        state = jnp.zeros((prow, width), F32)
        for q in range(n_z) if d == 0 else range(n_z - 1, -1, -1):
            new = pass_row(recvzp.at[q], d) * state + recvz[q].astype(F32)
            state = jnp.where(q < iz if d == 0 else q > iz, new, state)
        for q in range(n_p):
            ebuf[q, d] = (a_scr[d, q] + q_scr[d, q][0:1, :] * state).astype(BF)

    def p3_copy(k, sign=1):
        px, pc, pj = plane_peer(k, sign)
        return pltpu.make_async_remote_copy(
            ebuf.at[pj],
            recv3.at[me if sign == 1 else pj],
            p3s.at[k],
            p3r.at[k],
            device_id={"seq_1": px, "seq_2": pc},
            device_id_type=MESH,
        )

    for k in far_first:
        copy = p3_copy(k)
        copy.start()
        sent.append(copy)
    recv3[me] = ebuf[me]
    for k in range(1, n_p):
        p3_copy(k, -1).wait_recv()

    for a in range(n_ch):
        s = a * CH // SPAN
        for d in range(2):
            entering = jnp.concatenate([recv3[q, d] for q in range(n_p)], axis=0).astype(F32)
            state = st_scr[d, a] + carry_scr[d, a][0:1, :] * entering
            mask = (first_m, last_m)[d]
            queries = (fq_ref, bq_ref)[d][chunk(a), :]
            y_scr[chunk(a), :] += (cw_scr[d, s] * mask[a]) * dot(queries, state.astype(BF))
        gated = y_scr[chunk(a), :] * silu_scr[chunk(a), :]
        y_scr[chunk(a), :] = gated
        squares = gated * gated
        lanes_sum = squares[:, :LANES]
        for t in range(1, tiles):
            lanes_sum = lanes_sum + squares[:, t * LANES : (t + 1) * LANES]
        qbuf[a : a + 1, :] = jnp.sum(lanes_sum.T, axis=0, keepdims=True)

    def q_copy(k, sign=1):
        py = y_peer(k, sign)
        return pltpu.make_async_remote_copy(
            qbuf,
            recvq.at[iy if sign == 1 else py],
            sqs.at[k],
            sqr.at[k],
            device_id={"chan": py},
            device_id_type=MESH,
        )

    for k in sorted(range(1, n_y), key=lambda k: -min(k, n_y - k)):
        copy = q_copy(k)
        copy.start()
        sent.append(copy)
    recvq[iy] = qbuf[...]
    for k in range(1, n_y):
        q_copy(k, -1).wait_recv()
    squares = recvq[0]
    for k in range(1, n_y):
        squares = squares + recvq[k]
    inv = lax.rsqrt(squares / float(n_y * width) + 1e-05)

    pool = jnp.where(
        lax.broadcasted_iota(jnp.int32, (CH // POOL, CH), 0)
        == lax.broadcasted_iota(jnp.int32, (CH // POOL, CH), 1) // POOL,
        1.0 / POOL,
        0.0,
    ).astype(BF)
    gain = gain_ref[...]
    pooled = []
    for a in range(n_ch):
        inv_col = jnp.broadcast_to(inv[a : a + 1, :], (CH, LANES)).T
        inv_full = jnp.concatenate([inv_col] * tiles, axis=1)
        hidden = (y_scr[chunk(a), :] * inv_full * gain).astype(BF)
        pooled.append(dot(pool, hidden))
    pooled = jnp.concatenate(pooled, axis=0)
    high = pooled.astype(BF)
    rest = (pooled - high.astype(F32)).astype(BF)
    need(6)
    for c in range(2):
        cut = pl.ds(c * (dim // 2), dim // 2)
        w = w_ref[:, cut]
        result = dot(high, w) + dot(rest, w)
        for p in range(n_y):
            part[p, :, cut] = result[p * orow : (p + 1) * orow, :]

    def rs_copy(n, sign, s):
        return pltpu.make_async_remote_copy(
            rs_send.at[n, s],
            rs_recv.at[n, s],
            rss.at[n, s],
            rsr.at[n, s],
            device_id={"chan": y_peer(sign)},
            device_id_type=MESH,
        )

    for s in range(n_y // 2):
        for n, (sign, h, length) in links:
            if s >= length:
                continue
            cut = pl.ds(h * cut_w, cut_w)
            value = part[y_peer(sign * (length - s)), :, cut]
            if s > 0:
                rs_copy(n, sign, s - 1).wait_recv()
                value = value + rs_recv[n, s - 1].astype(F32)
            rs_send[n, s] = value.astype(BF)
            copy = rs_copy(n, sign, s)
            copy.start()
            sent.append(copy)

    def out_rows(p):
        return pl.ds(pl.multiple_of(p * orow, orow), orow)

    def ag_copy(n, sign, h, s, own):
        p = y_peer(-sign * s) if own else y_peer(-sign * (s + 1))
        view = obuf.at[out_rows(p), pl.ds(h * cut_w, cut_w)]
        return pltpu.make_async_remote_copy(
            view,
            view,
            ags.at[n, s],
            agr.at[n, s],
            device_id={"chan": y_peer(sign)},
            device_id_type=MESH,
        )

    def pass_on(n, sign, h, s):
        copy = ag_copy(n, sign, h, s, True)
        copy.start()
        sent.append(copy)

    for h in range(CUTS):
        cut = pl.ds(h * cut_w, cut_w)
        value = part[iy, :, cut]
        for n, (sign, hh, length) in links:
            if hh == h:
                rs_copy(n, sign, length - 1).wait_recv()
                value = value + rs_recv[n, length - 1].astype(F32)
        obuf[out_rows(iy), cut] = value.astype(BF)
        for n, (sign, hh, length) in links:
            if hh == h:
                pass_on(n, sign, h, 0)
    for s in range(1, n_y // 2):
        for n, (sign, h, length) in links:
            if s < length:
                ag_copy(n, sign, h, s - 1, False).wait_recv()
                pass_on(n, sign, h, s)
    for n, (sign, h, length) in links:
        ag_copy(n, sign, h, length - 1, False).wait_recv()
    done = pltpu.make_async_copy(obuf, out_hbm, out_sem)
    done.start()
    for copy in sent:
        copy.wait_send()
    done.wait()


def body(
    inner_acts,
    gate_input,
    forward_keys,
    forward_queries,
    backward_keys,
    backward_queries,
    decay_codes,
    clip_start,
    skip_gain,
    norm_gain,
    out_weight,
):
    sizes = tuple(lax.axis_size(a) for a in SEQ) + (lax.axis_size("chan"),)
    n_z, n_x, n_c, n_y = sizes
    n_p = n_x * n_c
    tokens, width = inner_acts.shape
    states = forward_keys.shape[1]
    dim = out_weight.shape[1]
    n_ch, n_sp = tokens // CH, tokens // SPAN
    prow = states // n_p
    rows_out = tokens // POOL
    orow = rows_out // n_y
    steps = n_y // 2
    vmem = pltpu.VMEM
    dma = pltpu.SemaphoreType.DMA
    any_spec = pl.BlockSpec(memory_space=pl.ANY)
    smem_spec = pl.BlockSpec(memory_space=pltpu.SMEM)
    vmem_spec = pl.BlockSpec(memory_space=pltpu.VMEM)
    scratch = [
        vmem((tokens, width), BF),
        vmem((tokens, width), BF),
        vmem((tokens, states), BF),
        vmem((tokens, states), BF),
        vmem((tokens, states), BF),
        vmem((tokens, states), BF),
        vmem(out_weight.shape, BF),
        vmem((tokens, width), F32),
        vmem((tokens, width), F32),
        vmem((2, n_ch, states, width), F32),
        vmem((2, n_ch, 8, width), F32),
        vmem((2, n_sp, CH, width), F32),
        vmem((n_p, 2, prow, width), BF),
        vmem((n_p, 2, prow, width), BF),
        vmem((8, LANES), F32),
        vmem((n_p, 8, LANES), F32),
        vmem((2, n_p, prow, width), F32),
        vmem((2, n_p, 8, width), F32),
        vmem((2, prow, width), BF),
        vmem((n_z, prow, width), BF),
        vmem((8, LANES), F32),
        vmem((n_z, 8, LANES), F32),
        vmem((n_p, 2, prow, width), BF),
        vmem((n_p, 2, prow, width), BF),
        vmem((n_ch, LANES), F32),
        vmem((n_y, n_ch, LANES), F32),
        vmem((n_y, orow, dim), F32),
        vmem((2 * CUTS, steps, orow, dim // CUTS), BF),
        vmem((2 * CUTS, steps, orow, dim // CUTS), BF),
        vmem((rows_out, dim), BF),
        dma((7,)),
        dma((n_p,)),
        dma((n_p,)),
        dma((n_p,)),
        dma((n_p,)),
        dma((n_z,)),
        dma((n_z,)),
        dma((n_z,)),
        dma((n_z,)),
        dma((n_p,)),
        dma((n_p,)),
        dma((n_y,)),
        dma((n_y,)),
        dma((2 * CUTS, steps)),
        dma((2 * CUTS, steps)),
        dma((2 * CUTS, steps)),
        dma((2 * CUTS, steps)),
        dma,
    ]
    return pl.pallas_call(
        functools.partial(layer_kernel, sizes),
        out_shape=jax.ShapeDtypeStruct((rows_out, dim), BF),
        in_specs=[smem_spec, smem_spec, vmem_spec, vmem_spec] + [any_spec] * 7,
        out_specs=any_spec,
        scratch_shapes=scratch,
        compiler_params=pltpu.CompilerParams(
            collective_id=0, has_side_effects=True, vmem_limit_bytes=67043328
        ),
        name="layer",
    )(
        decay_codes,
        skip_gain,
        clip_start.reshape(n_ch, CH),
        norm_gain.reshape(1, width),
        inner_acts,
        gate_input,
        forward_keys,
        forward_queries,
        backward_keys,
        backward_queries,
        out_weight,
    )


def solution(mesh):
    torus = Mesh(
        mesh.devices.reshape(8, 4, 2, mesh.shape["chan"]), ("seq_0", "seq_1", "seq_2", "chan")
    )
    return jax.shard_map(
        body,
        mesh=torus,
        in_specs=(
            P(SEQ, "chan"),
            P(SEQ, "chan"),
            P(SEQ, None),
            P(SEQ, None),
            P(SEQ, None),
            P(SEQ, None),
            P(None, SEQ, "chan"),
            P(SEQ),
            P("chan"),
            P("chan"),
            P("chan", None),
        ),
        out_specs=P(SEQ, None),
        check_vma=False,
    )
```

```python
import functools

import jax
import jax.numpy as jnp
from jax import lax
from jax.experimental import pallas as pl
from jax.experimental.pallas import tpu as pltpu
from jax.sharding import Mesh
from jax.sharding import PartitionSpec as P

SPAN = 256
POOL = 4
CH = 128
HEAD = 64
LANES = 128
CUTS = 4
SEQ = ("seq_0", "seq_1", "seq_2")
MESH = pl.DeviceIdType.MESH
F32 = jnp.float32
BF = jnp.bfloat16


def log_keep(rate):
    acc = jnp.full_like(rate, 1.0 / 12)
    for n in range(11, 0, -1):
        acc = acc * rate + 1.0 / n
    return -rate * acc


def dot_t(a, b):
    return lax.dot_general(a, b, (((0,), (0,)), ((), ())), preferred_element_type=F32)


def dot_nt(a, b):
    return lax.dot_general(a, b, (((1,), (1,)), ((), ())), preferred_element_type=F32)


def dot(a, b):
    return jnp.dot(a, b, preferred_element_type=F32)


def layer_kernel(
    sizes,
    codes_ref,
    skip_ref,
    clip_ref,
    gain_ref,
    acts_hbm,
    gate_hbm,
    fk_hbm,
    fq_hbm,
    bk_hbm,
    bq_hbm,
    w_hbm,
    out_hbm,
    x_ref,
    z_ref,
    fk_ref,
    fq_ref,
    bk_ref,
    bq_ref,
    w_ref,
    y_scr,
    silu_scr,
    st_scr,
    carry_scr,
    cw_scr,
    sbuf,
    recv1,
    pbuf,
    recvp,
    a_scr,
    q_scr,
    zbuf,
    recvz,
    zpbuf,
    recvzp,
    ebuf,
    recv3,
    qbuf,
    recvq,
    part,
    rs_send,
    rs_recv,
    obuf,
    in_sem,
    p1s,
    p1r,
    pps,
    ppr,
    zs,
    zr,
    zps,
    zpr,
    p3s,
    p3r,
    sqs,
    sqr,
    rss,
    rsr,
    ags,
    agr,
    out_sem,
):
    n_z, n_x, n_c, n_y = sizes
    n_p = n_x * n_c
    tokens, width = x_ref.shape
    n_ch = tokens // CH
    n_sp = tokens // SPAN
    heads = width // HEAD
    tiles = width // LANES
    states = fk_ref.shape[1]
    prow = states // n_p
    total_tokens = n_z * n_x * n_c * tokens
    dim = w_ref.shape[1]
    cut_w = dim // CUTS
    ways = [
        (2 * h + i, sign, h, (sign == 1) == (h % 2 == 0))
        for h in range(CUTS)
        for i, sign in enumerate((1, -1))
    ]
    rows_out = tokens // POOL
    orow = rows_out // n_y

    iz = lax.axis_index("seq_0")
    ix = lax.axis_index("seq_1")
    ic = lax.axis_index("seq_2")
    iy = lax.axis_index("chan")
    me = ix * n_c + ic

    def plane_peer(k, sign=1):
        px = lax.rem(ix + sign * (k // n_c) + n_x, n_x)
        pc = lax.rem(ic + sign * (k % n_c) + n_c, n_c)
        return px, pc, px * n_c + pc

    def z_peer(k, sign=1):
        return lax.rem(iz + sign * k + n_z, n_z)

    def y_peer(k, sign=1):
        return lax.rem(iy + sign * k + 2 * n_y, n_y)

    loads = [
        pltpu.make_async_copy(src, dst, in_sem.at[n])
        for n, (src, dst) in enumerate(
            (
                (acts_hbm, x_ref),
                (fk_hbm, fk_ref),
                (bk_hbm, bk_ref),
                (fq_hbm, fq_ref),
                (bq_hbm, bq_ref),
                (gate_hbm, z_ref),
                (w_hbm, w_ref),
            )
        )
    ]
    for load in loads:
        load.start()
    waited = set()

    def need(n):
        waited.add(n)
        loads[n].wait()

    sent = []

    barrier = pltpu.get_barrier_semaphore()
    for k in range(1, n_p):
        px, pc, _ = plane_peer(k)
        pl.semaphore_signal(
            barrier, inc=1, device_id={"seq_1": px, "seq_2": pc}, device_id_type=MESH
        )
    for k in range(1, n_z):
        pl.semaphore_signal(barrier, inc=1, device_id={"seq_0": z_peer(k)}, device_id_type=MESH)
    for k in range(1, n_y):
        pl.semaphore_signal(barrier, inc=1, device_id={"chan": y_peer(k)}, device_id_type=MESH)

    low = lax.broadcasted_iota(jnp.int32, (1, LANES), 1) < HEAD
    logs, scal = [], []
    for d in range(2):
        logs.append([])
        scal.append([])
        for s in range(n_sp):
            rates = [
                jnp.full((1, LANES), codes_ref[d, s, h].astype(F32)) * (1.0 / (32.0 * total_tokens))
                for h in range(heads)
            ]
            logs[d].append([log_keep(r) for r in rates])
            scal[d].append([jnp.sqrt(r * (2.0 - r)) for r in rates])

    def as_row(items):
        return jnp.concatenate(
            [jnp.where(low, items[2 * t], items[2 * t + 1]) for t in range(tiles)], axis=1
        )

    log_row = [[as_row(logs[d][s]) for s in range(n_sp)] for d in range(2)]
    scal_row = [[as_row(scal[d][s]) for s in range(n_sp)] for d in range(2)]

    rows = lax.broadcasted_iota(jnp.int32, (CH, CH), 0)
    cols = lax.broadcasted_iota(jnp.int32, (CH, CH), 1)
    lower = rows >= cols
    upper = rows <= cols
    starts = clip_ref[...].astype(F32).astype(BF)
    seg_row = dot(starts, upper.astype(F32).astype(BF))
    seg_col = dot_nt(lower.astype(F32).astype(BF), starts)
    seg_c = [seg_col[:, a : a + 1] for a in range(n_ch)]
    fin = [seg_row[a : a + 1, CH - 1 : CH] for a in range(n_ch)]
    first_m = [(seg_c[a] == 0.0).astype(F32) for a in range(n_ch)]
    last_m = [(seg_c[a] == fin[a]).astype(F32) for a in range(n_ch)]
    clear = [(fin[a] == 0.0).astype(F32) for a in range(n_ch)]
    passing = [
        [jnp.exp(float(CH) * log_row[d][a * CH // SPAN]) * clear[a] for a in range(n_ch)]
        for d in range(2)
    ]

    step_f = lax.broadcasted_iota(jnp.int32, (CH, width), 0).astype(F32)
    grow = (
        [jnp.exp(log_row[0][s] * (CH - 1.0 - step_f)) * scal_row[0][s] for s in range(n_sp)],
        [jnp.exp(log_row[1][s] * step_f) * scal_row[1][s] for s in range(n_sp)],
    )
    for n in range(3):
        need(n)

    def chunk(a):
        return pl.ds(a * CH, CH)

    for d in range(2):
        keys_ref = (fk_ref, bk_ref)[d]
        mask = (last_m, first_m)[d]
        order = range(n_ch) if d == 0 else range(n_ch - 1, -1, -1)
        state, through = None, None
        for a in order:
            if state is None:
                st_scr[d, a] = jnp.zeros((states, width), F32)
                carry_scr[d, a] = jnp.ones((8, width), F32)
            else:
                st_scr[d, a] = state
                carry_scr[d, a] = jnp.broadcast_to(through, (8, width))
            scaled = (x_ref[chunk(a), :].astype(F32) * (grow[d][a * CH // SPAN] * mask[a])).astype(BF)
            local = dot_t(keys_ref[chunk(a), :], scaled)
            state = local if state is None else passing[d][a] * state + local
            through = passing[d][a] if through is None else passing[d][a] * through
        for j in range(n_p):
            sbuf[j, d] = state[j * prow : (j + 1) * prow, :].astype(BF)
        for t in range(tiles):
            pbuf[d * tiles + t : d * tiles + t + 1, :] = through[:, t * LANES : (t + 1) * LANES]

    pl.semaphore_wait(barrier, (n_p - 1) + (n_z - 1) + (n_y - 1))

    def pp_copy(k, sign=1):
        px, pc, pj = plane_peer(k, sign)
        return pltpu.make_async_remote_copy(
            pbuf,
            recvp.at[me if sign == 1 else pj],
            pps.at[k],
            ppr.at[k],
            device_id={"seq_1": px, "seq_2": pc},
            device_id_type=MESH,
        )

    def p1_copy(k, sign=1):
        px, pc, pj = plane_peer(k, sign)
        return pltpu.make_async_remote_copy(
            sbuf.at[pj],
            recv1.at[me if sign == 1 else pj],
            p1s.at[k],
            p1r.at[k],
            device_id={"seq_1": px, "seq_2": pc},
            device_id_type=MESH,
        )

    def go(copy):
        copy.start()
        sent.append(copy)

    far_first = sorted(range(1, n_p), key=lambda k: -min(k // n_c, n_x - k // n_c))
    for k in far_first:
        go(pp_copy(k))
    for k in far_first:
        go(p1_copy(k))
    recv1[me] = sbuf[me]
    recvp[me] = pbuf[...]

    need(3)
    need(4)
    apart = jnp.abs(rows - cols).astype(F32)
    left_m = jnp.where(low, 1.0, 0.0).astype(BF)
    right_m = jnp.where(low, 0.0, 1.0).astype(BF)
    for s in range(n_sp):
        decay = [
            jnp.exp(apart * jnp.where(lower, logs[0][s][h], logs[1][s][h])) for h in range(heads)
        ]
        for a in range(s * SPAN // CH, (s + 1) * SPAN // CH):
            same = seg_c[a] == seg_row[a : a + 1, :]
            ahead = jnp.where(
                same & lower, dot_nt(fq_ref[chunk(a), :], fk_ref[chunk(a), :]), 0.0
            )
            behind = jnp.where(
                same & upper, dot_nt(bq_ref[chunk(a), :], bk_ref[chunk(a), :]), 0.0
            )
            for t in range(tiles):
                pair = jnp.concatenate(
                    [
                        (
                            decay[h] * (scal[0][s][h] * ahead + scal[1][s][h] * behind)
                        ).astype(BF)
                        for h in (2 * t, 2 * t + 1)
                    ],
                    axis=1,
                )
                lanes = pl.ds(t * LANES, LANES)
                xt = x_ref[chunk(a), lanes]
                both = jnp.concatenate([xt * left_m, xt * right_m], axis=0)
                skip = jnp.where(low, skip_ref[2 * t], skip_ref[2 * t + 1])
                y_scr[chunk(a), lanes] = dot(pair, both) + skip * xt.astype(F32)

    def pass_row(ref, d):
        return jnp.concatenate(
            [ref[d * tiles + t : d * tiles + t + 1, :] for t in range(tiles)], axis=1
        )

    def z_way(k, sign=1):
        pz = z_peer(k, sign)
        return pz, iz if sign == 1 else pz

    def zp_copy(k, sign=1):
        pz, slot = z_way(k, sign)
        return pltpu.make_async_remote_copy(
            zpbuf,
            recvzp.at[slot],
            zps.at[k],
            zpr.at[k],
            device_id={"seq_0": pz},
            device_id_type=MESH,
        )

    z_far_first = sorted(range(1, n_z), key=lambda k: -min(k, n_z - k))
    for k in range(1, n_p):
        pp_copy(k, -1).wait_recv()
    for d in range(2):
        through = jnp.ones((1, width), F32)
        for q in range(n_p) if d == 0 else range(n_p - 1, -1, -1):
            q_scr[d, q] = jnp.broadcast_to(through, (8, width))
            through = pass_row(recvp.at[q], d) * through
        for t in range(tiles):
            zpbuf[d * tiles + t : d * tiles + t + 1, :] = through[:, t * LANES : (t + 1) * LANES]
    for k in z_far_first:
        go(zp_copy(k))
    recvzp[iz] = zpbuf[...]

    need(5)
    for a in range(n_ch):
        v = z_ref[chunk(a), :].astype(F32)
        silu_scr[chunk(a), :] = v / (1.0 + jnp.exp(-v))
    for s in range(n_sp):
        cw_scr[0, s] = jnp.exp(log_row[0][s] * (step_f + 1.0))
        cw_scr[1, s] = jnp.exp(log_row[1][s] * (float(CH) - step_f))

    for k in range(1, n_p):
        p1_copy(k, -1).wait_recv()

    for d in range(2):
        order = range(n_p) if d == 0 else range(n_p - 1, -1, -1)
        state = jnp.zeros((prow, width), F32)
        for q in order:
            a_scr[d, q] = state
            state = pass_row(recvp.at[q], d) * state + recv1[q, d].astype(F32)
        zbuf[d] = state.astype(BF)

    def z_copy(k, sign=1):
        pz, slot = z_way(k, sign)
        return pltpu.make_async_remote_copy(
            zbuf.at[jnp.where(pz > iz, 0, 1)],
            recvz.at[slot],
            zs.at[k],
            zr.at[k],
            device_id={"seq_0": pz},
            device_id_type=MESH,
        )

    for k in z_far_first:
        go(z_copy(k))
    recvz[iz] = jnp.zeros((prow, width), BF)

    for k in range(1, n_z):
        zp_copy(k, -1).wait_recv()
        z_copy(k, -1).wait_recv()

    for d in range(2):
        state = jnp.zeros((prow, width), F32)
        for q in range(n_z) if d == 0 else range(n_z - 1, -1, -1):
            new = pass_row(recvzp.at[q], d) * state + recvz[q].astype(F32)
            state = jnp.where(q < iz if d == 0 else q > iz, new, state)
        for q in range(n_p):
            ebuf[q, d] = (a_scr[d, q] + q_scr[d, q][0:1, :] * state).astype(BF)

    def p3_copy(k, sign=1):
        px, pc, pj = plane_peer(k, sign)
        return pltpu.make_async_remote_copy(
            ebuf.at[pj],
            recv3.at[me if sign == 1 else pj],
            p3s.at[k],
            p3r.at[k],
            device_id={"seq_1": px, "seq_2": pc},
            device_id_type=MESH,
        )

    for k in far_first:
        go(p3_copy(k))
    recv3[me] = ebuf[me]
    for k in range(1, n_p):
        p3_copy(k, -1).wait_recv()

    for a in range(n_ch):
        s = a * CH // SPAN
        for d in range(2):
            entering = jnp.concatenate([recv3[q, d] for q in range(n_p)], axis=0).astype(F32)
            state = st_scr[d, a] + carry_scr[d, a][0:1, :] * entering
            mask = (first_m, last_m)[d]
            queries = (fq_ref, bq_ref)[d][chunk(a), :]
            y_scr[chunk(a), :] += (cw_scr[d, s] * mask[a]) * dot(queries, state.astype(BF))
        gated = y_scr[chunk(a), :] * silu_scr[chunk(a), :]
        y_scr[chunk(a), :] = gated
        squares = gated * gated
        lanes_sum = squares[:, :LANES]
        for t in range(1, tiles):
            lanes_sum = lanes_sum + squares[:, t * LANES : (t + 1) * LANES]
        qbuf[a : a + 1, :] = jnp.sum(lanes_sum.T, axis=0, keepdims=True)

    def q_copy(k, sign=1):
        py = y_peer(k, sign)
        return pltpu.make_async_remote_copy(
            qbuf,
            recvq.at[iy if sign == 1 else py],
            sqs.at[k],
            sqr.at[k],
            device_id={"chan": py},
            device_id_type=MESH,
        )

    for k in sorted(range(1, n_y), key=lambda k: -min(k, n_y - k)):
        go(q_copy(k))
    recvq[iy] = qbuf[...]
    for k in range(1, n_y):
        q_copy(k, -1).wait_recv()
    squares = recvq[0]
    for k in range(1, n_y):
        squares = squares + recvq[k]
    inv = lax.rsqrt(squares / float(n_y * width) + 1e-05)

    pool = jnp.where(
        lax.broadcasted_iota(jnp.int32, (CH // POOL, CH), 0)
        == lax.broadcasted_iota(jnp.int32, (CH // POOL, CH), 1) // POOL,
        1.0 / POOL,
        0.0,
    ).astype(BF)
    gain = gain_ref[...]
    pooled = []
    for a in range(n_ch):
        inv_col = jnp.broadcast_to(inv[a : a + 1, :], (CH, LANES)).T
        inv_full = jnp.concatenate([inv_col] * tiles, axis=1)
        hidden = (y_scr[chunk(a), :] * inv_full * gain).astype(BF)
        pooled.append(dot(pool, hidden))
    pooled = jnp.concatenate(pooled, axis=0)
    pooled = pooled.astype(BF)
    need(6)
    for c in range(2):
        cut = pl.ds(c * (dim // 2), dim // 2)
        w = w_ref[:, cut]
        result = dot(pooled, w)
        for p in range(n_y):
            part[p, :, cut] = result[p * orow : (p + 1) * orow, :]

    def lanes_of(h):
        return pl.ds(h * cut_w, cut_w)

    def rs_copy(n, slot, sign, hops):
        return pltpu.make_async_remote_copy(
            rs_send.at[n, slot],
            rs_recv.at[n, slot],
            rss.at[n, slot],
            rsr.at[n, slot],
            device_id={"chan": y_peer(sign * hops)},
            device_id_type=MESH,
        )

    def send_part(n, slot, sign, h, away, hops):
        rs_send[n, slot] = part[y_peer(sign * away), :, lanes_of(h)].astype(BF)
        go(rs_copy(n, slot, sign, hops))

    for n, sign, h, far in ways:
        if far:
            send_part(n, 0, sign, h, 4, 2)
    for n, sign, h, far in ways:
        send_part(n, 1, sign, h, 3, 1)
    for n, sign, h, far in ways:
        send_part(n, 2, sign, h, 1, 1)
    for n, sign, h, far in ways:
        value = part[y_peer(2 * sign), :, lanes_of(h)]
        rs_copy(n, 1, sign, 1).wait_recv()
        value = value + rs_recv[n, 1].astype(F32)
        if far:
            rs_copy(n, 0, sign, 2).wait_recv()
            value = value + rs_recv[n, 0].astype(F32)
        rs_send[n, 3] = value.astype(BF)
        go(rs_copy(n, 3, sign, 2))

    def ag_copy(n, slot, sign, h, hops, rows_from):
        p = pl.multiple_of(y_peer(rows_from) * orow, orow)
        view = obuf.at[pl.ds(p, orow), lanes_of(h)]
        return pltpu.make_async_remote_copy(
            view,
            view,
            ags.at[n, slot],
            agr.at[n, slot],
            device_id={"chan": y_peer(sign * hops)},
            device_id_type=MESH,
        )

    for h in range(CUTS):
        value = part[iy, :, lanes_of(h)]
        for n, sign, hh, far in ways:
            if hh == h:
                rs_copy(n, 2, sign, 1).wait_recv()
                value = value + rs_recv[n, 2].astype(F32)
                rs_copy(n, 3, sign, 2).wait_recv()
                value = value + rs_recv[n, 3].astype(F32)
        obuf[pl.ds(pl.multiple_of(iy * orow, orow), orow), lanes_of(h)] = value.astype(BF)
        for n, sign, hh, far in ways:
            if hh == h:
                go(ag_copy(n, 0, sign, h, 2, 0))
                go(ag_copy(n, 1, sign, h, 1, 0))
    for n, sign, h, far in ways:
        ag_copy(n, 0, sign, h, 2, -2 * sign).wait_recv()
        if far:
            go(ag_copy(n, 3, sign, h, 2, -2 * sign))
        go(ag_copy(n, 2, sign, h, 1, -2 * sign))
    for n, sign, h, far in ways:
        ag_copy(n, 1, sign, h, 1, -sign).wait_recv()
        ag_copy(n, 2, sign, h, 1, -3 * sign).wait_recv()
        if far:
            ag_copy(n, 3, sign, h, 2, -4 * sign).wait_recv()
    done = pltpu.make_async_copy(obuf, out_hbm, out_sem)
    done.start()
    for copy in sent:
        copy.wait_send()
    done.wait()


def body(
    inner_acts,
    gate_input,
    forward_keys,
    forward_queries,
    backward_keys,
    backward_queries,
    decay_codes,
    clip_start,
    skip_gain,
    norm_gain,
    out_weight,
):
    sizes = tuple(lax.axis_size(a) for a in SEQ) + (lax.axis_size("chan"),)
    n_z, n_x, n_c, n_y = sizes
    n_p = n_x * n_c
    tokens, width = inner_acts.shape
    states = forward_keys.shape[1]
    dim = out_weight.shape[1]
    n_ch, n_sp = tokens // CH, tokens // SPAN
    prow = states // n_p
    rows_out = tokens // POOL
    orow = rows_out // n_y
    steps = 4
    vmem = pltpu.VMEM
    dma = pltpu.SemaphoreType.DMA
    any_spec = pl.BlockSpec(memory_space=pl.ANY)
    smem_spec = pl.BlockSpec(memory_space=pltpu.SMEM)
    vmem_spec = pl.BlockSpec(memory_space=pltpu.VMEM)
    scratch = [
        vmem((tokens, width), BF),
        vmem((tokens, width), BF),
        vmem((tokens, states), BF),
        vmem((tokens, states), BF),
        vmem((tokens, states), BF),
        vmem((tokens, states), BF),
        vmem(out_weight.shape, BF),
        vmem((tokens, width), F32),
        vmem((tokens, width), F32),
        vmem((2, n_ch, states, width), F32),
        vmem((2, n_ch, 8, width), F32),
        vmem((2, n_sp, CH, width), F32),
        vmem((n_p, 2, prow, width), BF),
        vmem((n_p, 2, prow, width), BF),
        vmem((8, LANES), F32),
        vmem((n_p, 8, LANES), F32),
        vmem((2, n_p, prow, width), F32),
        vmem((2, n_p, 8, width), F32),
        vmem((2, prow, width), BF),
        vmem((n_z, prow, width), BF),
        vmem((8, LANES), F32),
        vmem((n_z, 8, LANES), F32),
        vmem((n_p, 2, prow, width), BF),
        vmem((n_p, 2, prow, width), BF),
        vmem((n_ch, LANES), F32),
        vmem((n_y, n_ch, LANES), F32),
        vmem((n_y, orow, dim), F32),
        vmem((2 * CUTS, steps, orow, dim // CUTS), BF),
        vmem((2 * CUTS, steps, orow, dim // CUTS), BF),
        vmem((rows_out, dim), BF),
        dma((7,)),
        dma((n_p,)),
        dma((n_p,)),
        dma((n_p,)),
        dma((n_p,)),
        dma((n_z,)),
        dma((n_z,)),
        dma((n_z,)),
        dma((n_z,)),
        dma((n_p,)),
        dma((n_p,)),
        dma((n_y,)),
        dma((n_y,)),
        dma((2 * CUTS, steps)),
        dma((2 * CUTS, steps)),
        dma((2 * CUTS, steps)),
        dma((2 * CUTS, steps)),
        dma,
    ]
    return pl.pallas_call(
        functools.partial(layer_kernel, sizes),
        out_shape=jax.ShapeDtypeStruct((rows_out, dim), BF),
        in_specs=[smem_spec, smem_spec, vmem_spec, vmem_spec] + [any_spec] * 7,
        out_specs=any_spec,
        scratch_shapes=scratch,
        compiler_params=pltpu.CompilerParams(
            collective_id=0, has_side_effects=True, vmem_limit_bytes=67043328
        ),
        name="layer",
    )(
        decay_codes,
        skip_gain,
        clip_start.reshape(n_ch, CH),
        norm_gain.reshape(1, width),
        inner_acts,
        gate_input,
        forward_keys,
        forward_queries,
        backward_keys,
        backward_queries,
        out_weight,
    )


def solution(mesh):
    torus = Mesh(
        mesh.devices.reshape(8, 4, 2, mesh.shape["chan"]), ("seq_0", "seq_1", "seq_2", "chan")
    )
    return jax.shard_map(
        body,
        mesh=torus,
        in_specs=(
            P(SEQ, "chan"),
            P(SEQ, "chan"),
            P(SEQ, None),
            P(SEQ, None),
            P(SEQ, None),
            P(SEQ, None),
            P(None, SEQ, "chan"),
            P(SEQ),
            P("chan"),
            P("chan"),
            P("chan", None),
        ),
        out_specs=P(SEQ, None),
        check_vma=False,
    )
```

```python
import functools

import jax
import jax.numpy as jnp
from jax import lax
from jax.experimental import pallas as pl
from jax.experimental.pallas import tpu as pltpu
from jax.sharding import Mesh
from jax.sharding import PartitionSpec as P

SPAN = 256
POOL = 4
CH = 128
HEAD = 64
LANES = 128
CUTS = 4
SEQ = ("seq_0", "seq_1", "seq_2")
MESH = pl.DeviceIdType.MESH
F32 = jnp.float32
BF = jnp.bfloat16


def log_keep(rate):
    acc = jnp.full_like(rate, 1.0 / 12)
    for n in range(11, 0, -1):
        acc = acc * rate + 1.0 / n
    return -rate * acc


def dot_t(a, b):
    return lax.dot_general(a, b, (((0,), (0,)), ((), ())), preferred_element_type=F32)


def dot_nt(a, b):
    return lax.dot_general(a, b, (((1,), (1,)), ((), ())), preferred_element_type=F32)


def dot(a, b):
    return jnp.dot(a, b, preferred_element_type=F32)


def layer_kernel(
    sizes,
    codes_hbm,
    skip_hbm,
    clip_hbm,
    gain_hbm,
    acts_hbm,
    gate_hbm,
    fk_hbm,
    fq_hbm,
    bk_hbm,
    bq_hbm,
    w_hbm,
    out_ref,
    codes_ref,
    skip_ref,
    clip_ref,
    gain_ref,
    x_ref,
    z_ref,
    fk_ref,
    fq_ref,
    bk_ref,
    bq_ref,
    w_ref,
    y_scr,
    silu_scr,
    st_scr,
    carry_scr,
    cw_scr,
    sbuf,
    recv1,
    pbuf,
    recvp,
    a_scr,
    q_scr,
    zbuf,
    recvz,
    zpbuf,
    recvzp,
    ebuf,
    recv3,
    qbuf,
    recvq,
    part,
    rs_send,
    rs_recv,
    obuf,
    in_sem,
    p1s,
    p1r,
    pps,
    ppr,
    zs,
    zr,
    zps,
    zpr,
    p3s,
    p3r,
    sqs,
    sqr,
    rss,
    rsr,
    ags,
    agr,
    out_sem,
):
    n_z, n_x, n_c, n_y = sizes
    n_p = n_x * n_c
    tokens, width = x_ref.shape
    n_ch = tokens // CH
    n_sp = tokens // SPAN
    heads = width // HEAD
    tiles = width // LANES
    states = fk_ref.shape[1]
    prow = states // n_p
    total_tokens = n_z * n_x * n_c * tokens
    dim = w_ref.shape[1]
    cut_w = dim // CUTS
    ways = [
        (2 * h + i, sign, h, (sign == 1) == (h % 2 == 0))
        for h in range(CUTS)
        for i, sign in enumerate((1, -1))
    ]
    rows_out = tokens // POOL
    orow = rows_out // n_y

    iz = lax.axis_index("seq_0")
    ix = lax.axis_index("seq_1")
    ic = lax.axis_index("seq_2")
    iy = lax.axis_index("chan")
    me = ix * n_c + ic

    def plane_peer(k, sign=1):
        px = lax.rem(ix + sign * (k // n_c) + n_x, n_x)
        pc = lax.rem(ic + sign * (k % n_c) + n_c, n_c)
        return px, pc, px * n_c + pc

    def z_peer(k, sign=1):
        return lax.rem(iz + sign * k + n_z, n_z)

    def y_peer(k, sign=1):
        return lax.rem(iy + sign * k + 2 * n_y, n_y)

    loads = [
        pltpu.make_async_copy(src, dst, in_sem.at[n])
        for n, (src, dst) in enumerate(
            (
                (codes_hbm, codes_ref),
                (clip_hbm, clip_ref),
                (acts_hbm, x_ref),
                (fk_hbm, fk_ref),
                (bk_hbm, bk_ref),
                (fq_hbm, fq_ref),
                (bq_hbm, bq_ref),
                (skip_hbm, skip_ref),
                (gate_hbm, z_ref),
                (gain_hbm, gain_ref),
                (w_hbm, w_ref),
            )
        )
    ]
    for load in loads[:5]:
        load.start()

    def need(*which):
        for n in which:
            loads[n].wait()

    sent = []

    barrier = pltpu.get_barrier_semaphore()
    for k in range(1, n_p):
        px, pc, _ = plane_peer(k)
        pl.semaphore_signal(
            barrier, inc=1, device_id={"seq_1": px, "seq_2": pc}, device_id_type=MESH
        )
    for k in range(1, n_z):
        pl.semaphore_signal(barrier, inc=1, device_id={"seq_0": z_peer(k)}, device_id_type=MESH)
    for k in range(1, n_y):
        pl.semaphore_signal(barrier, inc=1, device_id={"chan": y_peer(k)}, device_id_type=MESH)

    need(0, 1)
    low = lax.broadcasted_iota(jnp.int32, (1, LANES), 1) < HEAD
    logs, scal = [], []
    for d in range(2):
        logs.append([])
        scal.append([])
        for s in range(n_sp):
            rates = [
                jnp.full((1, LANES), codes_ref[d, s, h].astype(F32)) * (1.0 / (32.0 * total_tokens))
                for h in range(heads)
            ]
            logs[d].append([log_keep(r) for r in rates])
            scal[d].append([jnp.sqrt(r * (2.0 - r)) for r in rates])

    def as_row(items):
        return jnp.concatenate(
            [jnp.where(low, items[2 * t], items[2 * t + 1]) for t in range(tiles)], axis=1
        )

    log_row = [[as_row(logs[d][s]) for s in range(n_sp)] for d in range(2)]
    scal_row = [[as_row(scal[d][s]) for s in range(n_sp)] for d in range(2)]

    rows = lax.broadcasted_iota(jnp.int32, (CH, CH), 0)
    cols = lax.broadcasted_iota(jnp.int32, (CH, CH), 1)
    lower = rows >= cols
    upper = rows <= cols
    starts = clip_ref[...].astype(F32).astype(BF)
    seg_row = dot(starts, upper.astype(F32).astype(BF))
    seg_col = dot_nt(lower.astype(F32).astype(BF), starts)
    seg_c = [seg_col[:, a : a + 1] for a in range(n_ch)]
    fin = [seg_row[a : a + 1, CH - 1 : CH] for a in range(n_ch)]
    first_m = [(seg_c[a] == 0.0).astype(F32) for a in range(n_ch)]
    last_m = [(seg_c[a] == fin[a]).astype(F32) for a in range(n_ch)]
    clear = [(fin[a] == 0.0).astype(F32) for a in range(n_ch)]
    passing = [
        [jnp.exp(float(CH) * log_row[d][a * CH // SPAN]) * clear[a] for a in range(n_ch)]
        for d in range(2)
    ]

    step_f = lax.broadcasted_iota(jnp.int32, (CH, width), 0).astype(F32)
    grow = (
        [jnp.exp(log_row[0][s] * (CH - 1.0 - step_f)) * scal_row[0][s] for s in range(n_sp)],
        [jnp.exp(log_row[1][s] * step_f) * scal_row[1][s] for s in range(n_sp)],
    )
    need(2, 3, 4)
    for load in loads[5:9]:
        load.start()

    def chunk(a):
        return pl.ds(a * CH, CH)

    for d in range(2):
        keys_ref = (fk_ref, bk_ref)[d]
        mask = (last_m, first_m)[d]
        order = range(n_ch) if d == 0 else range(n_ch - 1, -1, -1)
        state, through = None, None
        for a in order:
            if state is None:
                st_scr[d, a] = jnp.zeros((states, width), F32)
                carry_scr[d, a] = jnp.ones((8, width), F32)
            else:
                st_scr[d, a] = state
                carry_scr[d, a] = jnp.broadcast_to(through, (8, width))
            scaled = (x_ref[chunk(a), :].astype(F32) * (grow[d][a * CH // SPAN] * mask[a])).astype(BF)
            local = dot_t(keys_ref[chunk(a), :], scaled)
            state = local if state is None else passing[d][a] * state + local
            through = passing[d][a] if through is None else passing[d][a] * through
        for j in range(n_p):
            sbuf[j, d] = state[j * prow : (j + 1) * prow, :].astype(BF)
        for t in range(tiles):
            pbuf[d * tiles + t : d * tiles + t + 1, :] = through[:, t * LANES : (t + 1) * LANES]

    pl.semaphore_wait(barrier, (n_p - 1) + (n_z - 1) + (n_y - 1))

    def pp_copy(k, sign=1):
        px, pc, pj = plane_peer(k, sign)
        return pltpu.make_async_remote_copy(
            pbuf,
            recvp.at[me if sign == 1 else pj],
            pps.at[k],
            ppr.at[k],
            device_id={"seq_1": px, "seq_2": pc},
            device_id_type=MESH,
        )

    def p1_copy(k, sign=1):
        px, pc, pj = plane_peer(k, sign)
        return pltpu.make_async_remote_copy(
            sbuf.at[pj],
            recv1.at[me if sign == 1 else pj],
            p1s.at[k],
            p1r.at[k],
            device_id={"seq_1": px, "seq_2": pc},
            device_id_type=MESH,
        )

    def go(copy):
        copy.start()
        sent.append(copy)

    far_first = sorted(range(1, n_p), key=lambda k: -min(k // n_c, n_x - k // n_c))
    for k in far_first:
        go(pp_copy(k))
    for k in far_first:
        go(p1_copy(k))
    recv1[me] = sbuf[me]
    recvp[me] = pbuf[...]

    need(5, 6, 7)
    for load in loads[9:]:
        load.start()
    apart = jnp.abs(rows - cols).astype(F32)
    left_m = jnp.where(low, 1.0, 0.0).astype(BF)
    right_m = jnp.where(low, 0.0, 1.0).astype(BF)
    for s in range(n_sp):
        decay = [
            jnp.exp(apart * jnp.where(lower, logs[0][s][h], logs[1][s][h])) for h in range(heads)
        ]
        for a in range(s * SPAN // CH, (s + 1) * SPAN // CH):
            same = seg_c[a] == seg_row[a : a + 1, :]
            ahead = jnp.where(
                same & lower, dot_nt(fq_ref[chunk(a), :], fk_ref[chunk(a), :]), 0.0
            )
            behind = jnp.where(
                same & upper, dot_nt(bq_ref[chunk(a), :], bk_ref[chunk(a), :]), 0.0
            )
            for t in range(tiles):
                pair = jnp.concatenate(
                    [
                        (
                            decay[h] * (scal[0][s][h] * ahead + scal[1][s][h] * behind)
                        ).astype(BF)
                        for h in (2 * t, 2 * t + 1)
                    ],
                    axis=1,
                )
                lanes = pl.ds(t * LANES, LANES)
                xt = x_ref[chunk(a), lanes]
                both = jnp.concatenate([xt * left_m, xt * right_m], axis=0)
                skip = jnp.where(low, skip_ref[2 * t], skip_ref[2 * t + 1])
                y_scr[chunk(a), lanes] = dot(pair, both) + skip * xt.astype(F32)

    def pass_row(ref, d):
        return jnp.concatenate(
            [ref[d * tiles + t : d * tiles + t + 1, :] for t in range(tiles)], axis=1
        )

    def z_way(k, sign=1):
        pz = z_peer(k, sign)
        return pz, iz if sign == 1 else pz

    def zp_copy(k, sign=1):
        pz, slot = z_way(k, sign)
        return pltpu.make_async_remote_copy(
            zpbuf,
            recvzp.at[slot],
            zps.at[k],
            zpr.at[k],
            device_id={"seq_0": pz},
            device_id_type=MESH,
        )

    z_far_first = sorted(range(1, n_z), key=lambda k: -min(k, n_z - k))
    for k in range(1, n_p):
        pp_copy(k, -1).wait_recv()
    for d in range(2):
        through = jnp.ones((1, width), F32)
        for q in range(n_p) if d == 0 else range(n_p - 1, -1, -1):
            q_scr[d, q] = jnp.broadcast_to(through, (8, width))
            through = pass_row(recvp.at[q], d) * through
        for t in range(tiles):
            zpbuf[d * tiles + t : d * tiles + t + 1, :] = through[:, t * LANES : (t + 1) * LANES]
    for k in z_far_first:
        go(zp_copy(k))
    recvzp[iz] = zpbuf[...]

    need(8)
    for a in range(n_ch):
        v = z_ref[chunk(a), :].astype(F32)
        silu_scr[chunk(a), :] = v / (1.0 + jnp.exp(-v))
    for s in range(n_sp):
        cw_scr[0, s] = jnp.exp(log_row[0][s] * (step_f + 1.0))
        cw_scr[1, s] = jnp.exp(log_row[1][s] * (float(CH) - step_f))

    for k in range(1, n_p):
        p1_copy(k, -1).wait_recv()

    for d in range(2):
        order = range(n_p) if d == 0 else range(n_p - 1, -1, -1)
        state = jnp.zeros((prow, width), F32)
        for q in order:
            a_scr[d, q] = state
            state = pass_row(recvp.at[q], d) * state + recv1[q, d].astype(F32)
        zbuf[d] = state.astype(BF)

    def z_copy(k, sign=1):
        pz, slot = z_way(k, sign)
        return pltpu.make_async_remote_copy(
            zbuf.at[jnp.where(pz > iz, 0, 1)],
            recvz.at[slot],
            zs.at[k],
            zr.at[k],
            device_id={"seq_0": pz},
            device_id_type=MESH,
        )

    for k in z_far_first:
        go(z_copy(k))
    recvz[iz] = jnp.zeros((prow, width), BF)

    for k in range(1, n_z):
        zp_copy(k, -1).wait_recv()
        z_copy(k, -1).wait_recv()

    for d in range(2):
        state = jnp.zeros((prow, width), F32)
        for q in range(n_z) if d == 0 else range(n_z - 1, -1, -1):
            new = pass_row(recvzp.at[q], d) * state + recvz[q].astype(F32)
            state = jnp.where(q < iz if d == 0 else q > iz, new, state)
        for q in range(n_p):
            ebuf[q, d] = (a_scr[d, q] + q_scr[d, q][0:1, :] * state).astype(BF)

    def p3_copy(k, sign=1):
        px, pc, pj = plane_peer(k, sign)
        return pltpu.make_async_remote_copy(
            ebuf.at[pj],
            recv3.at[me if sign == 1 else pj],
            p3s.at[k],
            p3r.at[k],
            device_id={"seq_1": px, "seq_2": pc},
            device_id_type=MESH,
        )

    for k in far_first:
        go(p3_copy(k))
    recv3[me] = ebuf[me]
    for k in range(1, n_p):
        p3_copy(k, -1).wait_recv()

    for a in range(n_ch):
        s = a * CH // SPAN
        for d in range(2):
            entering = jnp.concatenate([recv3[q, d] for q in range(n_p)], axis=0).astype(F32)
            state = st_scr[d, a] + carry_scr[d, a][0:1, :] * entering
            mask = (first_m, last_m)[d]
            queries = (fq_ref, bq_ref)[d][chunk(a), :]
            y_scr[chunk(a), :] += (cw_scr[d, s] * mask[a]) * dot(queries, state.astype(BF))
        gated = y_scr[chunk(a), :] * silu_scr[chunk(a), :]
        y_scr[chunk(a), :] = gated
        squares = gated * gated
        lanes_sum = squares[:, :LANES]
        for t in range(1, tiles):
            lanes_sum = lanes_sum + squares[:, t * LANES : (t + 1) * LANES]
        qbuf[a : a + 1, :] = jnp.sum(lanes_sum.T, axis=0, keepdims=True)

    def q_copy(k, sign=1):
        py = y_peer(k, sign)
        return pltpu.make_async_remote_copy(
            qbuf,
            recvq.at[iy if sign == 1 else py],
            sqs.at[k],
            sqr.at[k],
            device_id={"chan": py},
            device_id_type=MESH,
        )

    for k in sorted(range(1, n_y), key=lambda k: -min(k, n_y - k)):
        go(q_copy(k))
    recvq[iy] = qbuf[...]
    for k in range(1, n_y):
        q_copy(k, -1).wait_recv()
    squares = recvq[0]
    for k in range(1, n_y):
        squares = squares + recvq[k]
    inv = lax.rsqrt(squares / float(n_y * width) + 1e-05)

    pool = jnp.where(
        lax.broadcasted_iota(jnp.int32, (CH // POOL, CH), 0)
        == lax.broadcasted_iota(jnp.int32, (CH // POOL, CH), 1) // POOL,
        1.0 / POOL,
        0.0,
    ).astype(BF)
    need(9)
    gain = gain_ref[...]
    pooled = []
    for a in range(n_ch):
        inv_col = jnp.broadcast_to(inv[a : a + 1, :], (CH, LANES)).T
        inv_full = jnp.concatenate([inv_col] * tiles, axis=1)
        hidden = (y_scr[chunk(a), :] * inv_full * gain).astype(BF)
        pooled.append(dot(pool, hidden))
    pooled = jnp.concatenate(pooled, axis=0)
    pooled = pooled.astype(BF)
    need(10)
    for c in range(2):
        cut = pl.ds(c * (dim // 2), dim // 2)
        w = w_ref[:, cut]
        result = dot(pooled, w)
        for p in range(n_y):
            part[p, :, cut] = result[p * orow : (p + 1) * orow, :]

    def lanes_of(h):
        return pl.ds(h * cut_w, cut_w)

    def rs_copy(n, slot, sign, hops):
        return pltpu.make_async_remote_copy(
            rs_send.at[n, slot],
            rs_recv.at[n, slot],
            rss.at[n, slot],
            rsr.at[n, slot],
            device_id={"chan": y_peer(sign * hops)},
            device_id_type=MESH,
        )

    def send_part(n, slot, sign, h, away, hops):
        rs_send[n, slot] = part[y_peer(sign * away), :, lanes_of(h)].astype(BF)
        go(rs_copy(n, slot, sign, hops))

    for n, sign, h, far in ways:
        if far:
            send_part(n, 0, sign, h, 4, 2)
    for n, sign, h, far in ways:
        send_part(n, 1, sign, h, 3, 1)
    for n, sign, h, far in ways:
        send_part(n, 2, sign, h, 1, 1)
    for n, sign, h, far in ways:
        value = part[y_peer(2 * sign), :, lanes_of(h)]
        rs_copy(n, 1, sign, 1).wait_recv()
        value = value + rs_recv[n, 1].astype(F32)
        if far:
            rs_copy(n, 0, sign, 2).wait_recv()
            value = value + rs_recv[n, 0].astype(F32)
        rs_send[n, 3] = value.astype(BF)
        go(rs_copy(n, 3, sign, 2))

    def ag_copy(n, slot, sign, h, hops, rows_from):
        p = pl.multiple_of(y_peer(rows_from) * orow, orow)
        view = out_ref.at[pl.ds(p, orow), lanes_of(h)]
        return pltpu.make_async_remote_copy(
            obuf.at[:, lanes_of(h)] if rows_from == 0 else view,
            view,
            ags.at[n, slot],
            agr.at[n, slot],
            device_id={"chan": y_peer(sign * hops)},
            device_id_type=MESH,
        )

    for h in range(CUTS):
        value = part[iy, :, lanes_of(h)]
        for n, sign, hh, far in ways:
            if hh == h:
                rs_copy(n, 2, sign, 1).wait_recv()
                value = value + rs_recv[n, 2].astype(F32)
                rs_copy(n, 3, sign, 2).wait_recv()
                value = value + rs_recv[n, 3].astype(F32)
        obuf[:, lanes_of(h)] = value.astype(BF)
        for n, sign, hh, far in ways:
            if hh == h:
                go(ag_copy(n, 0, sign, h, 2, 0))
                go(ag_copy(n, 1, sign, h, 1, 0))
    done = pltpu.make_async_copy(
        obuf, out_ref.at[pl.ds(pl.multiple_of(iy * orow, orow), orow), :], out_sem
    )
    done.start()
    for n, sign, h, far in ways:
        ag_copy(n, 0, sign, h, 2, -2 * sign).wait_recv()
        if far:
            go(ag_copy(n, 3, sign, h, 2, -2 * sign))
        go(ag_copy(n, 2, sign, h, 1, -2 * sign))
    for n, sign, h, far in ways:
        ag_copy(n, 1, sign, h, 1, -sign).wait_recv()
        ag_copy(n, 2, sign, h, 1, -3 * sign).wait_recv()
        if far:
            ag_copy(n, 3, sign, h, 2, -4 * sign).wait_recv()
    done.wait()
    for copy in sent:
        copy.wait_send()


def body(
    inner_acts,
    gate_input,
    forward_keys,
    forward_queries,
    backward_keys,
    backward_queries,
    decay_codes,
    clip_start,
    skip_gain,
    norm_gain,
    out_weight,
):
    sizes = tuple(lax.axis_size(a) for a in SEQ) + (lax.axis_size("chan"),)
    n_z, n_x, n_c, n_y = sizes
    n_p = n_x * n_c
    tokens, width = inner_acts.shape
    states = forward_keys.shape[1]
    dim = out_weight.shape[1]
    n_ch, n_sp = tokens // CH, tokens // SPAN
    prow = states // n_p
    rows_out = tokens // POOL
    orow = rows_out // n_y
    steps = 4
    vmem = pltpu.VMEM
    dma = pltpu.SemaphoreType.DMA
    scratch = [
        pltpu.SMEM(decay_codes.shape, jnp.int32),
        pltpu.SMEM(skip_gain.shape, F32),
        vmem((n_ch, CH), jnp.int32),
        vmem((1, width), F32),
        vmem((tokens, width), BF),
        vmem((tokens, width), BF),
        vmem((tokens, states), BF),
        vmem((tokens, states), BF),
        vmem((tokens, states), BF),
        vmem((tokens, states), BF),
        vmem(out_weight.shape, BF),
        vmem((tokens, width), F32),
        vmem((tokens, width), F32),
        vmem((2, n_ch, states, width), F32),
        vmem((2, n_ch, 8, width), F32),
        vmem((2, n_sp, CH, width), F32),
        vmem((n_p, 2, prow, width), BF),
        vmem((n_p, 2, prow, width), BF),
        vmem((8, LANES), F32),
        vmem((n_p, 8, LANES), F32),
        vmem((2, n_p, prow, width), F32),
        vmem((2, n_p, 8, width), F32),
        vmem((2, prow, width), BF),
        vmem((n_z, prow, width), BF),
        vmem((8, LANES), F32),
        vmem((n_z, 8, LANES), F32),
        vmem((n_p, 2, prow, width), BF),
        vmem((n_p, 2, prow, width), BF),
        vmem((n_ch, LANES), F32),
        vmem((n_y, n_ch, LANES), F32),
        vmem((n_y, orow, dim), F32),
        vmem((2 * CUTS, steps, orow, dim // CUTS), BF),
        vmem((2 * CUTS, steps, orow, dim // CUTS), BF),
        vmem((orow, dim), BF),
        dma((11,)),
        dma((n_p,)),
        dma((n_p,)),
        dma((n_p,)),
        dma((n_p,)),
        dma((n_z,)),
        dma((n_z,)),
        dma((n_z,)),
        dma((n_z,)),
        dma((n_p,)),
        dma((n_p,)),
        dma((n_y,)),
        dma((n_y,)),
        dma((2 * CUTS, steps)),
        dma((2 * CUTS, steps)),
        dma((2 * CUTS, steps)),
        dma((2 * CUTS, steps)),
        dma,
    ]
    return pl.pallas_call(
        functools.partial(layer_kernel, sizes),
        out_shape=jax.ShapeDtypeStruct((rows_out, dim), BF),
        in_specs=[pl.BlockSpec(memory_space=pltpu.HBM)] * 11,
        out_specs=pl.BlockSpec(memory_space=pl.ANY),
        scratch_shapes=scratch,
        compiler_params=pltpu.CompilerParams(
            collective_id=0, has_side_effects=True, vmem_limit_bytes=40 << 20
        ),
        name="layer",
    )(*(pltpu.with_memory_space_constraint(v, pltpu.HBM) for v in (
        decay_codes,
        skip_gain,
        clip_start.reshape(n_ch, CH),
        norm_gain.reshape(1, width),
        inner_acts,
        gate_input,
        forward_keys,
        forward_queries,
        backward_keys,
        backward_queries,
        out_weight,
    )))


def solution(mesh):
    torus = Mesh(
        mesh.devices.reshape(8, 4, 2, mesh.shape["chan"]), ("seq_0", "seq_1", "seq_2", "chan")
    )
    return jax.shard_map(
        body,
        mesh=torus,
        in_specs=(
            P(SEQ, "chan"),
            P(SEQ, "chan"),
            P(SEQ, None),
            P(SEQ, None),
            P(SEQ, None),
            P(SEQ, None),
            P(None, SEQ, "chan"),
            P(SEQ),
            P("chan"),
            P("chan"),
            P("chan", None),
        ),
        out_specs=P(SEQ, None),
        check_vma=False,
    )
```

```python
import functools

import jax
import jax.numpy as jnp
from jax import lax
from jax.experimental import pallas as pl
from jax.experimental.pallas import tpu as pltpu
from jax.sharding import Mesh
from jax.sharding import PartitionSpec as P

SPAN = 256
POOL = 4
CH = 128
HEAD = 64
LANES = 128
CUTS = 4
SEQ = ("seq_0", "seq_1", "seq_2")
MESH = pl.DeviceIdType.MESH
F32 = jnp.float32
BF = jnp.bfloat16


def log_keep(rate):
    acc = jnp.full_like(rate, 1.0 / 12)
    for n in range(11, 0, -1):
        acc = acc * rate + 1.0 / n
    return -rate * acc


def dot_t(a, b):
    return lax.dot_general(a, b, (((0,), (0,)), ((), ())), preferred_element_type=F32)


def dot_nt(a, b):
    return lax.dot_general(a, b, (((1,), (1,)), ((), ())), preferred_element_type=F32)


def dot(a, b):
    return jnp.dot(a, b, preferred_element_type=F32)


def layer_kernel(
    sizes,
    codes_hbm,
    skip_hbm,
    clip_hbm,
    gain_hbm,
    acts_hbm,
    gate_hbm,
    fk_hbm,
    fq_hbm,
    bk_hbm,
    bq_hbm,
    w_hbm,
    out_ref,
    codes_ref,
    skip_ref,
    clip_ref,
    gain_ref,
    x_ref,
    z_ref,
    fk_ref,
    fq_ref,
    bk_ref,
    bq_ref,
    w_ref,
    y_scr,
    silu_scr,
    st_scr,
    carry_scr,
    cw_scr,
    sbuf,
    recv1,
    pbuf,
    recvp,
    a_scr,
    q_scr,
    zbuf,
    recvz,
    zpbuf,
    recvzp,
    ebuf,
    recv3,
    qbuf,
    recvq,
    part,
    rs_send,
    rs_recv,
    obuf,
    in_sem,
    p1s,
    p1r,
    pps,
    ppr,
    zs,
    zr,
    zps,
    zpr,
    p3s,
    p3r,
    sqs,
    sqr,
    rss,
    rsr,
    ags,
    agr,
    out_sem,
):
    n_z, n_x, n_c, n_y = sizes
    n_p = n_x * n_c
    tokens, width = x_ref.shape
    n_ch = tokens // CH
    n_sp = tokens // SPAN
    heads = width // HEAD
    tiles = width // LANES
    states = fk_ref.shape[1]
    prow = states // n_p
    total_tokens = n_z * n_x * n_c * tokens
    dim = w_ref.shape[1]
    cut_w = dim // CUTS
    ways = [
        (2 * h + i, sign, h, (sign == 1) == (h % 2 == 0))
        for h in range(CUTS)
        for i, sign in enumerate((1, -1))
    ]
    rows_out = tokens // POOL
    orow = rows_out // n_y

    iz = lax.axis_index("seq_0")
    ix = lax.axis_index("seq_1")
    ic = lax.axis_index("seq_2")
    iy = lax.axis_index("chan")
    me = ix * n_c + ic

    def plane_peer(k, sign=1):
        px = lax.rem(ix + sign * (k // n_c) + n_x, n_x)
        pc = lax.rem(ic + sign * (k % n_c) + n_c, n_c)
        return px, pc, px * n_c + pc

    def z_peer(k, sign=1):
        return lax.rem(iz + sign * k + n_z, n_z)

    def y_peer(k, sign=1):
        return lax.rem(iy + sign * k + 2 * n_y, n_y)

    loads = [
        pltpu.make_async_copy(src, dst, in_sem.at[n])
        for n, (src, dst) in enumerate(
            (
                (codes_hbm, codes_ref),
                (clip_hbm, clip_ref),
                (acts_hbm, x_ref),
                (fk_hbm, fk_ref),
                (bk_hbm, bk_ref),
                (fq_hbm, fq_ref),
                (bq_hbm, bq_ref),
                (skip_hbm, skip_ref),
                (gate_hbm, z_ref),
                (gain_hbm, gain_ref),
                (w_hbm, w_ref),
            )
        )
    ]
    for load in loads[:5]:
        load.start()

    def need(*which):
        for n in which:
            loads[n].wait()

    sent = []

    barrier = pltpu.get_barrier_semaphore()
    for k in range(1, n_p):
        px, pc, _ = plane_peer(k)
        pl.semaphore_signal(
            barrier, inc=1, device_id={"seq_1": px, "seq_2": pc}, device_id_type=MESH
        )
    for k in range(1, n_z):
        pl.semaphore_signal(barrier, inc=1, device_id={"seq_0": z_peer(k)}, device_id_type=MESH)
    for k in range(1, n_y):
        pl.semaphore_signal(barrier, inc=1, device_id={"chan": y_peer(k)}, device_id_type=MESH)

    need(0, 1)
    low = lax.broadcasted_iota(jnp.int32, (1, LANES), 1) < HEAD
    logs, scal = [], []
    for d in range(2):
        logs.append([])
        scal.append([])
        for s in range(n_sp):
            rates = [
                jnp.full((1, LANES), codes_ref[d, s, h].astype(F32)) * (1.0 / (32.0 * total_tokens))
                for h in range(heads)
            ]
            logs[d].append([log_keep(r) for r in rates])
            scal[d].append([jnp.sqrt(r * (2.0 - r)) for r in rates])

    def as_row(items):
        return jnp.concatenate(
            [jnp.where(low, items[2 * t], items[2 * t + 1]) for t in range(tiles)], axis=1
        )

    log_row = [[as_row(logs[d][s]) for s in range(n_sp)] for d in range(2)]
    scal_row = [[as_row(scal[d][s]) for s in range(n_sp)] for d in range(2)]

    rows = lax.broadcasted_iota(jnp.int32, (CH, CH), 0)
    cols = lax.broadcasted_iota(jnp.int32, (CH, CH), 1)
    lower = rows >= cols
    upper = rows <= cols
    starts = clip_ref[...].astype(F32).astype(BF)
    seg_row = dot(starts, upper.astype(F32).astype(BF))
    seg_col = dot_nt(lower.astype(F32).astype(BF), starts)
    seg_c = [seg_col[:, a : a + 1] for a in range(n_ch)]
    fin = [seg_row[a : a + 1, CH - 1 : CH] for a in range(n_ch)]
    first_m = [(seg_c[a] == 0.0).astype(F32) for a in range(n_ch)]
    last_m = [(seg_c[a] == fin[a]).astype(F32) for a in range(n_ch)]
    clear = [(fin[a] == 0.0).astype(F32) for a in range(n_ch)]
    passing = [
        [jnp.exp(float(CH) * log_row[d][a * CH // SPAN]) * clear[a] for a in range(n_ch)]
        for d in range(2)
    ]

    step_f = lax.broadcasted_iota(jnp.int32, (CH, width), 0).astype(F32)
    grow = (
        [jnp.exp(log_row[0][s] * (CH - 1.0 - step_f)) * scal_row[0][s] for s in range(n_sp)],
        [jnp.exp(log_row[1][s] * step_f) * scal_row[1][s] for s in range(n_sp)],
    )
    need(2, 3, 4)
    for load in loads[5:9]:
        load.start()

    def chunk(a):
        return pl.ds(a * CH, CH)

    through = [[None] * n_ch, [None] * n_ch]
    for d in range(2):
        left = jnp.ones((1, width), F32)
        for a in range(n_ch) if d == 0 else range(n_ch - 1, -1, -1):
            through[d][a] = left
            left = passing[d][a] * left
        for t in range(tiles):
            pbuf[d * tiles + t : d * tiles + t + 1, :] = left[:, t * LANES : (t + 1) * LANES]

    def own_states(d):
        keys_ref = (fk_ref, bk_ref)[d]
        mask = (last_m, first_m)[d]
        state = None
        for a in range(n_ch) if d == 0 else range(n_ch - 1, -1, -1):
            if state is not None:
                st_scr[d, a] = state
            scaled = (x_ref[chunk(a), :].astype(F32) * (grow[d][a * CH // SPAN] * mask[a])).astype(BF)
            local = dot_t(keys_ref[chunk(a), :], scaled)
            state = local if state is None else passing[d][a] * state + local
        for j in range(n_p):
            sbuf[j, d] = state[j * prow : (j + 1) * prow, :].astype(BF)

    own_states(0)
    pl.semaphore_wait(barrier, (n_p - 1) + (n_z - 1) + (n_y - 1))

    def pp_copy(k, sign=1):
        px, pc, pj = plane_peer(k, sign)
        return pltpu.make_async_remote_copy(
            pbuf,
            recvp.at[me if sign == 1 else pj],
            pps.at[k],
            ppr.at[k],
            device_id={"seq_1": px, "seq_2": pc},
            device_id_type=MESH,
        )

    def p1_copy(d, k, sign=1):
        px, pc, pj = plane_peer(k, sign)
        return pltpu.make_async_remote_copy(
            sbuf.at[pj, d],
            recv1.at[me if sign == 1 else pj, d],
            p1s.at[d, k],
            p1r.at[d, k],
            device_id={"seq_1": px, "seq_2": pc},
            device_id_type=MESH,
        )

    def go(copy):
        copy.start()
        sent.append(copy)

    far_first = sorted(range(1, n_p), key=lambda k: -min(k // n_c, n_x - k // n_c))
    for k in far_first:
        go(pp_copy(k))
    for k in far_first:
        go(p1_copy(0, k))
    own_states(1)
    for k in far_first:
        go(p1_copy(1, k))
    recv1[me] = sbuf[me]
    recvp[me] = pbuf[...]

    need(5, 6, 7)
    for load in loads[9:]:
        load.start()
    apart = jnp.abs(rows - cols).astype(F32)
    left_m = jnp.where(low, 1.0, 0.0).astype(BF)
    right_m = jnp.where(low, 0.0, 1.0).astype(BF)
    for s in range(n_sp):
        decay = [
            jnp.exp(apart * jnp.where(lower, logs[0][s][h], logs[1][s][h])) for h in range(heads)
        ]
        for a in range(s * SPAN // CH, (s + 1) * SPAN // CH):
            same = seg_c[a] == seg_row[a : a + 1, :]
            ahead = jnp.where(
                same & lower, dot_nt(fq_ref[chunk(a), :], fk_ref[chunk(a), :]), 0.0
            )
            behind = jnp.where(
                same & upper, dot_nt(bq_ref[chunk(a), :], bk_ref[chunk(a), :]), 0.0
            )
            for t in range(tiles):
                pair = jnp.concatenate(
                    [
                        (
                            decay[h] * (scal[0][s][h] * ahead + scal[1][s][h] * behind)
                        ).astype(BF)
                        for h in (2 * t, 2 * t + 1)
                    ],
                    axis=1,
                )
                lanes = pl.ds(t * LANES, LANES)
                xt = x_ref[chunk(a), lanes]
                both = jnp.concatenate([xt * left_m, xt * right_m], axis=0)
                skip = jnp.where(low, skip_ref[2 * t], skip_ref[2 * t + 1])
                y_scr[chunk(a), lanes] = dot(pair, both) + skip * xt.astype(F32)

    def pass_row(ref, d):
        return jnp.concatenate(
            [ref[d * tiles + t : d * tiles + t + 1, :] for t in range(tiles)], axis=1
        )

    def z_way(k, sign=1):
        pz = z_peer(k, sign)
        return pz, iz if sign == 1 else pz

    def zp_copy(k, sign=1):
        pz, slot = z_way(k, sign)
        return pltpu.make_async_remote_copy(
            zpbuf,
            recvzp.at[slot],
            zps.at[k],
            zpr.at[k],
            device_id={"seq_0": pz},
            device_id_type=MESH,
        )

    z_far_first = sorted(range(1, n_z), key=lambda k: -min(k, n_z - k))
    for k in range(1, n_p):
        pp_copy(k, -1).wait_recv()
    for d in range(2):
        left = jnp.ones((1, width), F32)
        for q in range(n_p) if d == 0 else range(n_p - 1, -1, -1):
            q_scr[d, q] = jnp.broadcast_to(left, (8, width))
            left = pass_row(recvp.at[q], d) * left
        for t in range(tiles):
            zpbuf[d * tiles + t : d * tiles + t + 1, :] = left[:, t * LANES : (t + 1) * LANES]
    for k in z_far_first:
        go(zp_copy(k))
    recvzp[iz] = zpbuf[...]

    need(8)
    for a in range(n_ch):
        v = z_ref[chunk(a), :].astype(F32)
        silu_scr[chunk(a), :] = v / (1.0 + jnp.exp(-v))
    for s in range(n_sp):
        cw_scr[0, s] = jnp.exp(log_row[0][s] * (step_f + 1.0))
        cw_scr[1, s] = jnp.exp(log_row[1][s] * (float(CH) - step_f))

    for d in range(2):
        for k in range(1, n_p):
            p1_copy(d, k, -1).wait_recv()

    for d in range(2):
        order = range(n_p) if d == 0 else range(n_p - 1, -1, -1)
        state = jnp.zeros((prow, width), F32)
        for q in order:
            a_scr[d, q] = state
            state = pass_row(recvp.at[q], d) * state + recv1[q, d].astype(F32)
        zbuf[d] = state.astype(BF)

    def z_copy(k, sign=1):
        pz, slot = z_way(k, sign)
        return pltpu.make_async_remote_copy(
            zbuf.at[jnp.where(pz > iz, 0, 1)],
            recvz.at[slot],
            zs.at[k],
            zr.at[k],
            device_id={"seq_0": pz},
            device_id_type=MESH,
        )

    for k in z_far_first:
        go(z_copy(k))
    recvz[iz] = jnp.zeros((prow, width), BF)

    for a in range(n_ch):
        silu = silu_scr[chunk(a), :]
        local = y_scr[chunk(a), :]
        for d in range(2):
            first = a == (0 if d == 0 else n_ch - 1)
            reach = cw_scr[d, a * CH // SPAN] * (first_m, last_m)[d][a]
            if first:
                carry_scr[d, a] = reach * silu
            else:
                queries = (fq_ref, bq_ref)[d][chunk(a), :]
                local = local + reach * dot(queries, st_scr[d, a].astype(BF))
                carry_scr[d, a] = reach * silu * through[d][a]
        y_scr[chunk(a), :] = local * silu

    for k in range(1, n_z):
        zp_copy(k, -1).wait_recv()
        z_copy(k, -1).wait_recv()

    for d in range(2):
        state = jnp.zeros((prow, width), F32)
        for q in range(n_z) if d == 0 else range(n_z - 1, -1, -1):
            new = pass_row(recvzp.at[q], d) * state + recvz[q].astype(F32)
            state = jnp.where(q < iz if d == 0 else q > iz, new, state)
        for q in range(n_p):
            ebuf[q, d] = (a_scr[d, q] + q_scr[d, q][0:1, :] * state).astype(BF)

    def p3_copy(k, sign=1):
        px, pc, pj = plane_peer(k, sign)
        return pltpu.make_async_remote_copy(
            ebuf.at[pj],
            recv3.at[me if sign == 1 else pj],
            p3s.at[k],
            p3r.at[k],
            device_id={"seq_1": px, "seq_2": pc},
            device_id_type=MESH,
        )

    for k in far_first:
        go(p3_copy(k))
    recv3[me] = ebuf[me]
    for k in range(1, n_p):
        p3_copy(k, -1).wait_recv()

    for a in range(n_ch):
        gated = y_scr[chunk(a), :]
        for d in range(2):
            entering = jnp.concatenate([recv3[q, d] for q in range(n_p)], axis=0)
            gated = gated + carry_scr[d, a] * dot((fq_ref, bq_ref)[d][chunk(a), :], entering)
        y_scr[chunk(a), :] = gated
        squares = gated * gated
        lanes_sum = squares[:, :LANES]
        for t in range(1, tiles):
            lanes_sum = lanes_sum + squares[:, t * LANES : (t + 1) * LANES]
        qbuf[a : a + 1, :] = jnp.sum(lanes_sum.T, axis=0, keepdims=True)

    def q_copy(k, sign=1):
        py = y_peer(k, sign)
        return pltpu.make_async_remote_copy(
            qbuf,
            recvq.at[iy if sign == 1 else py],
            sqs.at[k],
            sqr.at[k],
            device_id={"chan": py},
            device_id_type=MESH,
        )

    for k in sorted(range(1, n_y), key=lambda k: -min(k, n_y - k)):
        go(q_copy(k))
    recvq[iy] = qbuf[...]
    need(9)
    gain = gain_ref[...]
    for a in range(n_ch):
        y_scr[chunk(a), :] = y_scr[chunk(a), :] * gain
    for k in range(1, n_y):
        q_copy(k, -1).wait_recv()
    squares = recvq[0]
    for k in range(1, n_y):
        squares = squares + recvq[k]
    inv = lax.rsqrt(squares / float(n_y * width) + 1e-05)

    pool = jnp.where(
        lax.broadcasted_iota(jnp.int32, (CH // POOL, CH), 0)
        == lax.broadcasted_iota(jnp.int32, (CH // POOL, CH), 1) // POOL,
        1.0 / POOL,
        0.0,
    ).astype(BF)
    pooled = []
    for a in range(n_ch):
        inv_col = jnp.broadcast_to(inv[a : a + 1, :], (CH, LANES)).T
        inv_full = jnp.concatenate([inv_col] * tiles, axis=1)
        hidden = (y_scr[chunk(a), :] * inv_full).astype(BF)
        pooled.append(dot(pool, hidden))
    pooled = jnp.concatenate(pooled, axis=0)
    pooled = pooled.astype(BF)
    def lanes_of(h):
        return pl.ds(h * cut_w, cut_w)

    def rs_copy(n, slot, sign, hops):
        return pltpu.make_async_remote_copy(
            rs_send.at[n, slot],
            rs_recv.at[n, slot],
            rss.at[n, slot],
            rsr.at[n, slot],
            device_id={"chan": y_peer(sign * hops)},
            device_id_type=MESH,
        )

    def send_part(n, slot, sign, h, away, hops):
        rs_send[n, slot] = part[y_peer(sign * away), :, lanes_of(h)].astype(BF)
        go(rs_copy(n, slot, sign, hops))

    need(10)
    for c in range(2):
        cut = pl.ds(c * (dim // 2), dim // 2)
        result = dot(pooled, w_ref[:, cut])
        for p in range(n_y):
            part[p, :, cut] = result[p * orow : (p + 1) * orow, :]
        mine = [way for way in ways if way[2] * 2 // CUTS == c]
        for n, sign, h, far in mine:
            if far:
                send_part(n, 0, sign, h, 4, 2)
        for n, sign, h, far in mine:
            send_part(n, 1, sign, h, 3, 1)
    for n, sign, h, far in ways:
        send_part(n, 2, sign, h, 1, 1)
    for n, sign, h, far in ways:
        value = part[y_peer(2 * sign), :, lanes_of(h)]
        rs_copy(n, 1, sign, 1).wait_recv()
        value = value + rs_recv[n, 1].astype(F32)
        if far:
            rs_copy(n, 0, sign, 2).wait_recv()
            value = value + rs_recv[n, 0].astype(F32)
        rs_send[n, 3] = value.astype(BF)
        go(rs_copy(n, 3, sign, 2))

    def ag_copy(n, slot, sign, h, hops, rows_from):
        p = pl.multiple_of(y_peer(rows_from) * orow, orow)
        view = out_ref.at[pl.ds(p, orow), lanes_of(h)]
        return pltpu.make_async_remote_copy(
            obuf.at[:, lanes_of(h)] if rows_from == 0 else view,
            view,
            ags.at[n, slot],
            agr.at[n, slot],
            device_id={"chan": y_peer(sign * hops)},
            device_id_type=MESH,
        )

    for h in range(CUTS):
        value = part[iy, :, lanes_of(h)]
        for n, sign, hh, far in ways:
            if hh == h:
                rs_copy(n, 2, sign, 1).wait_recv()
                value = value + rs_recv[n, 2].astype(F32)
                rs_copy(n, 3, sign, 2).wait_recv()
                value = value + rs_recv[n, 3].astype(F32)
        obuf[:, lanes_of(h)] = value.astype(BF)
        for n, sign, hh, far in ways:
            if hh == h:
                go(ag_copy(n, 0, sign, h, 2, 0))
                go(ag_copy(n, 1, sign, h, 1, 0))
    done = pltpu.make_async_copy(
        obuf, out_ref.at[pl.ds(pl.multiple_of(iy * orow, orow), orow), :], out_sem
    )
    done.start()
    for n, sign, h, far in ways:
        ag_copy(n, 0, sign, h, 2, -2 * sign).wait_recv()
        if far:
            go(ag_copy(n, 3, sign, h, 2, -2 * sign))
        go(ag_copy(n, 2, sign, h, 1, -2 * sign))
    for n, sign, h, far in ways:
        ag_copy(n, 1, sign, h, 1, -sign).wait_recv()
        ag_copy(n, 2, sign, h, 1, -3 * sign).wait_recv()
        if far:
            ag_copy(n, 3, sign, h, 2, -4 * sign).wait_recv()
    done.wait()
    for copy in sent:
        copy.wait_send()


def body(
    inner_acts,
    gate_input,
    forward_keys,
    forward_queries,
    backward_keys,
    backward_queries,
    decay_codes,
    clip_start,
    skip_gain,
    norm_gain,
    out_weight,
):
    sizes = tuple(lax.axis_size(a) for a in SEQ) + (lax.axis_size("chan"),)
    n_z, n_x, n_c, n_y = sizes
    n_p = n_x * n_c
    tokens, width = inner_acts.shape
    states = forward_keys.shape[1]
    dim = out_weight.shape[1]
    n_ch, n_sp = tokens // CH, tokens // SPAN
    prow = states // n_p
    rows_out = tokens // POOL
    orow = rows_out // n_y
    steps = 4
    vmem = pltpu.VMEM
    dma = pltpu.SemaphoreType.DMA
    scratch = [
        pltpu.SMEM(decay_codes.shape, jnp.int32),
        pltpu.SMEM(skip_gain.shape, F32),
        vmem((n_ch, CH), jnp.int32),
        vmem((1, width), F32),
        vmem((tokens, width), BF),
        vmem((tokens, width), BF),
        vmem((tokens, states), BF),
        vmem((tokens, states), BF),
        vmem((tokens, states), BF),
        vmem((tokens, states), BF),
        vmem(out_weight.shape, BF),
        vmem((tokens, width), F32),
        vmem((tokens, width), F32),
        vmem((2, n_ch, states, width), F32),
        vmem((2, n_ch, CH, width), F32),
        vmem((2, n_sp, CH, width), F32),
        vmem((n_p, 2, prow, width), BF),
        vmem((n_p, 2, prow, width), BF),
        vmem((8, LANES), F32),
        vmem((n_p, 8, LANES), F32),
        vmem((2, n_p, prow, width), F32),
        vmem((2, n_p, 8, width), F32),
        vmem((2, prow, width), BF),
        vmem((n_z, prow, width), BF),
        vmem((8, LANES), F32),
        vmem((n_z, 8, LANES), F32),
        vmem((n_p, 2, prow, width), BF),
        vmem((n_p, 2, prow, width), BF),
        vmem((n_ch, LANES), F32),
        vmem((n_y, n_ch, LANES), F32),
        vmem((n_y, orow, dim), F32),
        vmem((2 * CUTS, steps, orow, dim // CUTS), BF),
        vmem((2 * CUTS, steps, orow, dim // CUTS), BF),
        vmem((orow, dim), BF),
        dma((11,)),
        dma((2, n_p)),
        dma((2, n_p)),
        dma((n_p,)),
        dma((n_p,)),
        dma((n_z,)),
        dma((n_z,)),
        dma((n_z,)),
        dma((n_z,)),
        dma((n_p,)),
        dma((n_p,)),
        dma((n_y,)),
        dma((n_y,)),
        dma((2 * CUTS, steps)),
        dma((2 * CUTS, steps)),
        dma((2 * CUTS, steps)),
        dma((2 * CUTS, steps)),
        dma,
    ]
    return pl.pallas_call(
        functools.partial(layer_kernel, sizes),
        out_shape=jax.ShapeDtypeStruct((rows_out, dim), BF),
        in_specs=[pl.BlockSpec(memory_space=pltpu.HBM)] * 11,
        out_specs=pl.BlockSpec(memory_space=pl.ANY),
        scratch_shapes=scratch,
        compiler_params=pltpu.CompilerParams(
            collective_id=0, has_side_effects=True, vmem_limit_bytes=40 << 20
        ),
        name="layer",
    )(*(pltpu.with_memory_space_constraint(v, pltpu.HBM) for v in (
        decay_codes,
        skip_gain,
        clip_start.reshape(n_ch, CH),
        norm_gain.reshape(1, width),
        inner_acts,
        gate_input,
        forward_keys,
        forward_queries,
        backward_keys,
        backward_queries,
        out_weight,
    )))


def solution(mesh):
    torus = Mesh(
        mesh.devices.reshape(8, 4, 2, mesh.shape["chan"]), ("seq_0", "seq_1", "seq_2", "chan")
    )
    return jax.shard_map(
        body,
        mesh=torus,
        in_specs=(
            P(SEQ, "chan"),
            P(SEQ, "chan"),
            P(SEQ, None),
            P(SEQ, None),
            P(SEQ, None),
            P(SEQ, None),
            P(None, SEQ, "chan"),
            P(SEQ),
            P("chan"),
            P("chan"),
            P("chan", None),
        ),
        out_specs=P(SEQ, None),
        check_vma=False,
    )
```

```python
import functools

import jax
import jax.numpy as jnp
from jax import lax
from jax.experimental import pallas as pl
from jax.experimental.pallas import tpu as pltpu
from jax.sharding import Mesh
from jax.sharding import PartitionSpec as P

SPAN = 256
POOL = 4
CH = 128
HEAD = 64
LANES = 128
CUTS = 4
SEQ = ("seq_0", "seq_1", "seq_2")
MESH = pl.DeviceIdType.MESH
F32 = jnp.float32
BF = jnp.bfloat16


def log_keep(rate):
    acc = jnp.full_like(rate, 1.0 / 12)
    for n in range(11, 0, -1):
        acc = acc * rate + 1.0 / n
    return -rate * acc


def dot_t(a, b):
    return lax.dot_general(a, b, (((0,), (0,)), ((), ())), preferred_element_type=F32)


def dot_nt(a, b):
    return lax.dot_general(a, b, (((1,), (1,)), ((), ())), preferred_element_type=F32)


def dot(a, b):
    return jnp.dot(a, b, preferred_element_type=F32)


def layer_kernel(
    sizes,
    codes_hbm,
    skip_hbm,
    clip_hbm,
    gain_hbm,
    acts_hbm,
    gate_hbm,
    fk_hbm,
    fq_hbm,
    bk_hbm,
    bq_hbm,
    w_hbm,
    out_ref,
    codes_ref,
    skip_ref,
    clip_ref,
    gain_ref,
    x_ref,
    z_ref,
    fk_ref,
    fq_ref,
    bk_ref,
    bq_ref,
    w_ref,
    y_scr,
    silu_scr,
    st_scr,
    carry_scr,
    cw_scr,
    sbuf,
    recv1,
    pbuf,
    recvp,
    a_scr,
    q_scr,
    zbuf,
    recvz,
    zpbuf,
    recvzp,
    ebuf,
    recv3,
    qbuf,
    recvq,
    part,
    rs_send,
    rs_recv,
    obuf,
    in_sem,
    p1s,
    p1r,
    pps,
    ppr,
    zs,
    zr,
    zps,
    zpr,
    p3s,
    p3r,
    sqs,
    sqr,
    rss,
    rsr,
    ags,
    agr,
    out_sem,
):
    n_z, n_x, n_c, n_y = sizes
    n_p = n_x * n_c
    tokens, width = x_ref.shape
    n_ch = tokens // CH
    n_sp = tokens // SPAN
    heads = width // HEAD
    tiles = width // LANES
    states = fk_ref.shape[1]
    prow = states // n_p
    total_tokens = n_z * n_x * n_c * tokens
    dim = w_ref.shape[1]
    cut_w = dim // CUTS
    ways = [
        (2 * h + i, sign, h, (sign == 1) == (h % 2 == 0))
        for h in range(CUTS)
        for i, sign in enumerate((1, -1))
    ]
    rows_out = tokens // POOL
    orow = rows_out // n_y

    iz = lax.axis_index("seq_0")
    ix = lax.axis_index("seq_1")
    ic = lax.axis_index("seq_2")
    iy = lax.axis_index("chan")
    me = ix * n_c + ic

    def plane_peer(k, sign=1):
        px = lax.rem(ix + sign * (k // n_c) + n_x, n_x)
        pc = lax.rem(ic + sign * (k % n_c) + n_c, n_c)
        return px, pc, px * n_c + pc

    def z_peer(k, sign=1):
        return lax.rem(iz + sign * k + n_z, n_z)

    def y_peer(k, sign=1):
        return lax.rem(iy + sign * k + 2 * n_y, n_y)

    loads = [
        pltpu.make_async_copy(src, dst, in_sem.at[n])
        for n, (src, dst) in enumerate(
            (
                (codes_hbm, codes_ref),
                (clip_hbm, clip_ref),
                (acts_hbm, x_ref),
                (fk_hbm, fk_ref),
                (bk_hbm, bk_ref),
                (fq_hbm, fq_ref),
                (bq_hbm, bq_ref),
                (skip_hbm, skip_ref),
                (gate_hbm, z_ref),
                (gain_hbm, gain_ref),
                (w_hbm, w_ref),
            )
        )
    ]
    for load in loads[:5]:
        load.start()

    def need(*which):
        for n in which:
            loads[n].wait()

    sent = []

    for d in range(2):
        for q in range(n_z):
            recvz[d, q] = jnp.zeros((prow, width), BF)

    barrier = pltpu.get_barrier_semaphore()
    for k in range(1, n_p):
        px, pc, _ = plane_peer(k)
        pl.semaphore_signal(
            barrier, inc=1, device_id={"seq_1": px, "seq_2": pc}, device_id_type=MESH
        )
    for k in range(1, n_z):
        pl.semaphore_signal(barrier, inc=1, device_id={"seq_0": z_peer(k)}, device_id_type=MESH)
    for k in range(1, n_y):
        pl.semaphore_signal(barrier, inc=1, device_id={"chan": y_peer(k)}, device_id_type=MESH)

    need(0, 1)
    low = lax.broadcasted_iota(jnp.int32, (1, LANES), 1) < HEAD
    logs, scal = [], []
    for d in range(2):
        logs.append([])
        scal.append([])
        for s in range(n_sp):
            rates = [
                jnp.full((1, LANES), codes_ref[d, s, h].astype(F32)) * (1.0 / (32.0 * total_tokens))
                for h in range(heads)
            ]
            logs[d].append([log_keep(r) for r in rates])
            scal[d].append([jnp.sqrt(r * (2.0 - r)) for r in rates])

    def as_row(items):
        return jnp.concatenate(
            [jnp.where(low, items[2 * t], items[2 * t + 1]) for t in range(tiles)], axis=1
        )

    log_row = [[as_row(logs[d][s]) for s in range(n_sp)] for d in range(2)]
    scal_row = [[as_row(scal[d][s]) for s in range(n_sp)] for d in range(2)]

    rows = lax.broadcasted_iota(jnp.int32, (CH, CH), 0)
    cols = lax.broadcasted_iota(jnp.int32, (CH, CH), 1)
    lower = rows >= cols
    upper = rows <= cols
    starts = clip_ref[...].astype(F32).astype(BF)
    seg_row = dot(starts, upper.astype(F32).astype(BF))
    seg_col = dot_nt(lower.astype(F32).astype(BF), starts)
    seg_c = [seg_col[:, a : a + 1] for a in range(n_ch)]
    fin = [seg_row[a : a + 1, CH - 1 : CH] for a in range(n_ch)]
    first_m = [(seg_c[a] == 0.0).astype(F32) for a in range(n_ch)]
    last_m = [(seg_c[a] == fin[a]).astype(F32) for a in range(n_ch)]
    clear = [(fin[a] == 0.0).astype(F32) for a in range(n_ch)]
    passing = [
        [jnp.exp(float(CH) * log_row[d][a * CH // SPAN]) * clear[a] for a in range(n_ch)]
        for d in range(2)
    ]

    step_f = lax.broadcasted_iota(jnp.int32, (CH, width), 0).astype(F32)
    grow = (
        [jnp.exp(log_row[0][s] * (CH - 1.0 - step_f)) * scal_row[0][s] for s in range(n_sp)],
        [jnp.exp(log_row[1][s] * step_f) * scal_row[1][s] for s in range(n_sp)],
    )
    need(2, 3, 4)
    for load in loads[5:9]:
        load.start()

    def chunk(a):
        return pl.ds(a * CH, CH)

    through = [[None] * n_ch, [None] * n_ch]
    for d in range(2):
        left = jnp.ones((1, width), F32)
        for a in range(n_ch) if d == 0 else range(n_ch - 1, -1, -1):
            through[d][a] = left
            left = passing[d][a] * left
        for t in range(tiles):
            pbuf[d * tiles + t : d * tiles + t + 1, :] = left[:, t * LANES : (t + 1) * LANES]

    def own_states(d):
        keys_ref = (fk_ref, bk_ref)[d]
        mask = (last_m, first_m)[d]
        state = None
        for a in range(n_ch) if d == 0 else range(n_ch - 1, -1, -1):
            if state is not None:
                st_scr[d, a] = state
            scaled = (x_ref[chunk(a), :].astype(F32) * (grow[d][a * CH // SPAN] * mask[a])).astype(BF)
            local = dot_t(keys_ref[chunk(a), :], scaled)
            state = local if state is None else passing[d][a] * state + local
        for j in range(n_p):
            sbuf[j, d] = state[j * prow : (j + 1) * prow, :].astype(BF)

    own_states(1)
    pl.semaphore_wait(barrier, (n_p - 1) + (n_z - 1) + (n_y - 1))

    def pp_copy(k, sign=1):
        px, pc, pj = plane_peer(k, sign)
        return pltpu.make_async_remote_copy(
            pbuf,
            recvp.at[me if sign == 1 else pj],
            pps.at[k],
            ppr.at[k],
            device_id={"seq_1": px, "seq_2": pc},
            device_id_type=MESH,
        )

    def p1_copy(d, k, sign=1):
        px, pc, pj = plane_peer(k, sign)
        return pltpu.make_async_remote_copy(
            sbuf.at[pj, d],
            recv1.at[me if sign == 1 else pj, d],
            p1s.at[d, k],
            p1r.at[d, k],
            device_id={"seq_1": px, "seq_2": pc},
            device_id_type=MESH,
        )

    def go(copy):
        copy.start()
        sent.append(copy)

    far_first = sorted(range(1, n_p), key=lambda k: -min(k // n_c, n_x - k // n_c))
    for k in far_first:
        go(pp_copy(k))
    for k in far_first:
        go(p1_copy(1, k))
    own_states(0)
    for k in far_first:
        go(p1_copy(0, k))
    recv1[me] = sbuf[me]
    recvp[me] = pbuf[...]

    need(5, 6, 7)
    for load in loads[9:]:
        load.start()
    apart = jnp.abs(rows - cols).astype(F32)
    left_m = jnp.where(low, 1.0, 0.0).astype(BF)
    right_m = jnp.where(low, 0.0, 1.0).astype(BF)
    for s in range(n_sp):
        decay = [
            jnp.exp(apart * jnp.where(lower, logs[0][s][h], logs[1][s][h])) for h in range(heads)
        ]
        for a in range(s * SPAN // CH, (s + 1) * SPAN // CH):
            same = seg_c[a] == seg_row[a : a + 1, :]
            ahead = jnp.where(
                same & lower, dot_nt(fq_ref[chunk(a), :], fk_ref[chunk(a), :]), 0.0
            )
            behind = jnp.where(
                same & upper, dot_nt(bq_ref[chunk(a), :], bk_ref[chunk(a), :]), 0.0
            )
            for t in range(tiles):
                pair = jnp.concatenate(
                    [
                        (
                            decay[h] * (scal[0][s][h] * ahead + scal[1][s][h] * behind)
                        ).astype(BF)
                        for h in (2 * t, 2 * t + 1)
                    ],
                    axis=1,
                )
                lanes = pl.ds(t * LANES, LANES)
                xt = x_ref[chunk(a), lanes]
                both = jnp.concatenate([xt * left_m, xt * right_m], axis=0)
                skip = jnp.where(low, skip_ref[2 * t], skip_ref[2 * t + 1])
                y_scr[chunk(a), lanes] = dot(pair, both) + skip * xt.astype(F32)

    def pass_row(ref, d):
        return jnp.concatenate(
            [ref[d * tiles + t : d * tiles + t + 1, :] for t in range(tiles)], axis=1
        )

    def z_way(k, sign=1):
        pz = z_peer(k, sign)
        return pz, iz if sign == 1 else pz

    def zp_copy(k, sign=1):
        pz, slot = z_way(k, sign)
        return pltpu.make_async_remote_copy(
            zpbuf,
            recvzp.at[slot],
            zps.at[k],
            zpr.at[k],
            device_id={"seq_0": pz},
            device_id_type=MESH,
        )

    z_far_first = sorted(range(1, n_z), key=lambda k: -min(k, n_z - k))
    for k in range(1, n_p):
        pp_copy(k, -1).wait_recv()
    for d in range(2):
        left = jnp.ones((1, width), F32)
        for q in range(n_p) if d == 0 else range(n_p - 1, -1, -1):
            q_scr[d, q] = jnp.broadcast_to(left, (8, width))
            left = pass_row(recvp.at[q], d) * left
        for t in range(tiles):
            zpbuf[d * tiles + t : d * tiles + t + 1, :] = left[:, t * LANES : (t + 1) * LANES]
    for k in z_far_first:
        go(zp_copy(k))
    recvzp[iz] = zpbuf[...]

    need(8)
    for a in range(n_ch):
        v = z_ref[chunk(a), :].astype(F32)
        silu_scr[chunk(a), :] = v / (1.0 + jnp.exp(-v))
    for s in range(n_sp):
        cw_scr[0, s] = jnp.exp(log_row[0][s] * (step_f + 1.0))
        cw_scr[1, s] = jnp.exp(log_row[1][s] * (float(CH) - step_f))

    def z_copy(d, k, sign=1):
        pz, slot = z_way(k, sign)
        return pltpu.make_async_remote_copy(
            zbuf.at[d],
            recvz.at[d, slot],
            zs.at[k],
            zr.at[k],
            device_id={"seq_0": pz},
            device_id_type=MESH,
        )

    def above(q):
        return q > iz

    def below(q):
        return q < iz

    def send_total(d, k):
        @pl.when((above, below)[d](z_peer(k)))
        def _():
            z_copy(d, k).start()

    def total_arrived(d, k):
        @pl.when((below, above)[d](z_peer(k, -1)))
        def _():
            z_copy(d, k, -1).wait_recv()

    for d in (1, 0):
        for k in range(1, n_p):
            p1_copy(d, k, -1).wait_recv()
        state = jnp.zeros((prow, width), F32)
        for q in range(n_p) if d == 0 else range(n_p - 1, -1, -1):
            a_scr[d, q] = state
            state = pass_row(recvp.at[q], d) * state + recv1[q, d].astype(F32)
        zbuf[d] = state.astype(BF)
        for k in z_far_first:
            send_total(d, k)

    for a in range(n_ch):
        silu = silu_scr[chunk(a), :]
        local = y_scr[chunk(a), :]
        for d in range(2):
            first = a == (0 if d == 0 else n_ch - 1)
            reach = cw_scr[d, a * CH // SPAN] * (first_m, last_m)[d][a]
            if first:
                carry_scr[d, a] = reach * silu
            else:
                queries = (fq_ref, bq_ref)[d][chunk(a), :]
                local = local + reach * dot(queries, st_scr[d, a].astype(BF))
                carry_scr[d, a] = reach * silu * through[d][a]
        y_scr[chunk(a), :] = local * silu

    def p3_copy(d, k, sign=1):
        px, pc, pj = plane_peer(k, sign)
        return pltpu.make_async_remote_copy(
            ebuf.at[pj, d],
            recv3.at[me if sign == 1 else pj, d],
            p3s.at[d, k],
            p3r.at[d, k],
            device_id={"seq_1": px, "seq_2": pc},
            device_id_type=MESH,
        )

    for k in range(1, n_z):
        zp_copy(k, -1).wait_recv()
    for d in (1, 0):
        for k in range(1, n_z):
            total_arrived(d, k)
        state = jnp.zeros((prow, width), F32)
        for q in range(n_z) if d == 0 else range(n_z - 1, -1, -1):
            new = pass_row(recvzp.at[q], d) * state + recvz[d, q].astype(F32)
            state = jnp.where((below, above)[d](q), new, state)
        for q in range(n_p):
            ebuf[q, d] = (a_scr[d, q] + q_scr[d, q][0:1, :] * state).astype(BF)
        for k in far_first:
            go(p3_copy(d, k))
        recv3[me, d] = ebuf[me, d]

    def entering_part(d, a):
        entering = jnp.concatenate([recv3[q, d] for q in range(n_p)], axis=0)
        return carry_scr[d, a] * dot((fq_ref, bq_ref)[d][chunk(a), :], entering)

    for k in range(1, n_p):
        p3_copy(1, k, -1).wait_recv()
    for a in range(n_ch):
        y_scr[chunk(a), :] += entering_part(1, a)
    for k in range(1, n_p):
        p3_copy(0, k, -1).wait_recv()
    for a in range(n_ch):
        gated = y_scr[chunk(a), :] + entering_part(0, a)
        y_scr[chunk(a), :] = gated
        squares = gated * gated
        lanes_sum = squares[:, :LANES]
        for t in range(1, tiles):
            lanes_sum = lanes_sum + squares[:, t * LANES : (t + 1) * LANES]
        qbuf[a : a + 1, :] = jnp.sum(lanes_sum.T, axis=0, keepdims=True)

    def q_copy(k, sign=1):
        py = y_peer(k, sign)
        return pltpu.make_async_remote_copy(
            qbuf,
            recvq.at[iy if sign == 1 else py],
            sqs.at[k],
            sqr.at[k],
            device_id={"chan": py},
            device_id_type=MESH,
        )

    for k in sorted(range(1, n_y), key=lambda k: -min(k, n_y - k)):
        go(q_copy(k))
    recvq[iy] = qbuf[...]
    need(9)
    gain = gain_ref[...]
    for a in range(n_ch):
        y_scr[chunk(a), :] = y_scr[chunk(a), :] * gain
    for k in range(1, n_y):
        q_copy(k, -1).wait_recv()
    squares = recvq[0]
    for k in range(1, n_y):
        squares = squares + recvq[k]
    inv = lax.rsqrt(squares / float(n_y * width) + 1e-05)

    pool = jnp.where(
        lax.broadcasted_iota(jnp.int32, (CH // POOL, CH), 0)
        == lax.broadcasted_iota(jnp.int32, (CH // POOL, CH), 1) // POOL,
        1.0 / POOL,
        0.0,
    ).astype(BF)
    pooled = []
    for a in range(n_ch):
        inv_col = jnp.broadcast_to(inv[a : a + 1, :], (CH, LANES)).T
        inv_full = jnp.concatenate([inv_col] * tiles, axis=1)
        hidden = (y_scr[chunk(a), :] * inv_full).astype(BF)
        pooled.append(dot(pool, hidden))
    pooled = jnp.concatenate(pooled, axis=0)
    pooled = pooled.astype(BF)
    def lanes_of(h):
        return pl.ds(h * cut_w, cut_w)

    def rs_copy(n, slot, sign, hops):
        return pltpu.make_async_remote_copy(
            rs_send.at[n, slot],
            rs_recv.at[n, slot],
            rss.at[n, slot],
            rsr.at[n, slot],
            device_id={"chan": y_peer(sign * hops)},
            device_id_type=MESH,
        )

    def send_part(n, slot, sign, h, away, hops):
        rs_send[n, slot] = part[y_peer(sign * away), :, lanes_of(h)].astype(BF)
        go(rs_copy(n, slot, sign, hops))

    need(10)
    for c in range(2):
        cut = pl.ds(c * (dim // 2), dim // 2)
        result = dot(pooled, w_ref[:, cut])
        for p in range(n_y):
            part[p, :, cut] = result[p * orow : (p + 1) * orow, :]
        mine = [way for way in ways if way[2] * 2 // CUTS == c]
        for n, sign, h, far in mine:
            if far:
                send_part(n, 0, sign, h, 4, 2)
        for n, sign, h, far in mine:
            send_part(n, 1, sign, h, 3, 1)
    for n, sign, h, far in ways:
        send_part(n, 2, sign, h, 1, 1)
    for n, sign, h, far in ways:
        value = part[y_peer(2 * sign), :, lanes_of(h)]
        rs_copy(n, 1, sign, 1).wait_recv()
        value = value + rs_recv[n, 1].astype(F32)
        if far:
            rs_copy(n, 0, sign, 2).wait_recv()
            value = value + rs_recv[n, 0].astype(F32)
        rs_send[n, 3] = value.astype(BF)
        go(rs_copy(n, 3, sign, 2))

    def ag_copy(n, slot, sign, h, hops, rows_from):
        p = pl.multiple_of(y_peer(rows_from) * orow, orow)
        view = out_ref.at[pl.ds(p, orow), lanes_of(h)]
        return pltpu.make_async_remote_copy(
            obuf.at[:, lanes_of(h)] if rows_from == 0 else view,
            view,
            ags.at[n, slot],
            agr.at[n, slot],
            device_id={"chan": y_peer(sign * hops)},
            device_id_type=MESH,
        )

    for h in range(CUTS):
        value = part[iy, :, lanes_of(h)]
        for n, sign, hh, far in ways:
            if hh == h:
                rs_copy(n, 2, sign, 1).wait_recv()
                value = value + rs_recv[n, 2].astype(F32)
                rs_copy(n, 3, sign, 2).wait_recv()
                value = value + rs_recv[n, 3].astype(F32)
        obuf[:, lanes_of(h)] = value.astype(BF)
        for n, sign, hh, far in ways:
            if hh == h:
                go(ag_copy(n, 0, sign, h, 2, 0))
                go(ag_copy(n, 1, sign, h, 1, 0))
    done = pltpu.make_async_copy(
        obuf, out_ref.at[pl.ds(pl.multiple_of(iy * orow, orow), orow), :], out_sem
    )
    done.start()
    for n, sign, h, far in ways:
        ag_copy(n, 0, sign, h, 2, -2 * sign).wait_recv()
        if far:
            go(ag_copy(n, 3, sign, h, 2, -2 * sign))
        go(ag_copy(n, 2, sign, h, 1, -2 * sign))
    for n, sign, h, far in ways:
        ag_copy(n, 1, sign, h, 1, -sign).wait_recv()
        ag_copy(n, 2, sign, h, 1, -3 * sign).wait_recv()
        if far:
            ag_copy(n, 3, sign, h, 2, -4 * sign).wait_recv()
    done.wait()
    for k in range(1, n_z):
        z_copy(0, k).wait_send()
    for copy in sent:
        copy.wait_send()


def body(
    inner_acts,
    gate_input,
    forward_keys,
    forward_queries,
    backward_keys,
    backward_queries,
    decay_codes,
    clip_start,
    skip_gain,
    norm_gain,
    out_weight,
):
    sizes = tuple(lax.axis_size(a) for a in SEQ) + (lax.axis_size("chan"),)
    n_z, n_x, n_c, n_y = sizes
    n_p = n_x * n_c
    tokens, width = inner_acts.shape
    states = forward_keys.shape[1]
    dim = out_weight.shape[1]
    n_ch, n_sp = tokens // CH, tokens // SPAN
    prow = states // n_p
    rows_out = tokens // POOL
    orow = rows_out // n_y
    steps = 4
    vmem = pltpu.VMEM
    dma = pltpu.SemaphoreType.DMA
    scratch = [
        pltpu.SMEM(decay_codes.shape, jnp.int32),
        pltpu.SMEM(skip_gain.shape, F32),
        vmem((n_ch, CH), jnp.int32),
        vmem((1, width), F32),
        vmem((tokens, width), BF),
        vmem((tokens, width), BF),
        vmem((tokens, states), BF),
        vmem((tokens, states), BF),
        vmem((tokens, states), BF),
        vmem((tokens, states), BF),
        vmem(out_weight.shape, BF),
        vmem((tokens, width), F32),
        vmem((tokens, width), F32),
        vmem((2, n_ch, states, width), F32),
        vmem((2, n_ch, CH, width), F32),
        vmem((2, n_sp, CH, width), F32),
        vmem((n_p, 2, prow, width), BF),
        vmem((n_p, 2, prow, width), BF),
        vmem((8, LANES), F32),
        vmem((n_p, 8, LANES), F32),
        vmem((2, n_p, prow, width), F32),
        vmem((2, n_p, 8, width), F32),
        vmem((2, prow, width), BF),
        vmem((2, n_z, prow, width), BF),
        vmem((8, LANES), F32),
        vmem((n_z, 8, LANES), F32),
        vmem((n_p, 2, prow, width), BF),
        vmem((n_p, 2, prow, width), BF),
        vmem((n_ch, LANES), F32),
        vmem((n_y, n_ch, LANES), F32),
        vmem((n_y, orow, dim), F32),
        vmem((2 * CUTS, steps, orow, dim // CUTS), BF),
        vmem((2 * CUTS, steps, orow, dim // CUTS), BF),
        vmem((orow, dim), BF),
        dma((11,)),
        dma((2, n_p)),
        dma((2, n_p)),
        dma((n_p,)),
        dma((n_p,)),
        dma((n_z,)),
        dma((n_z,)),
        dma((n_z,)),
        dma((n_z,)),
        dma((2, n_p)),
        dma((2, n_p)),
        dma((n_y,)),
        dma((n_y,)),
        dma((2 * CUTS, steps)),
        dma((2 * CUTS, steps)),
        dma((2 * CUTS, steps)),
        dma((2 * CUTS, steps)),
        dma,
    ]
    return pl.pallas_call(
        functools.partial(layer_kernel, sizes),
        out_shape=jax.ShapeDtypeStruct((rows_out, dim), BF),
        in_specs=[pl.BlockSpec(memory_space=pltpu.HBM)] * 11,
        out_specs=pl.BlockSpec(memory_space=pl.ANY),
        scratch_shapes=scratch,
        compiler_params=pltpu.CompilerParams(
            collective_id=0, has_side_effects=True, vmem_limit_bytes=40 << 20
        ),
        name="layer",
    )(*(pltpu.with_memory_space_constraint(v, pltpu.HBM) for v in (
        decay_codes,
        skip_gain,
        clip_start.reshape(n_ch, CH),
        norm_gain.reshape(1, width),
        inner_acts,
        gate_input,
        forward_keys,
        forward_queries,
        backward_keys,
        backward_queries,
        out_weight,
    )))


def solution(mesh):
    torus = Mesh(
        mesh.devices.reshape(8, 4, 2, mesh.shape["chan"]), ("seq_0", "seq_1", "seq_2", "chan")
    )
    return jax.shard_map(
        body,
        mesh=torus,
        in_specs=(
            P(SEQ, "chan"),
            P(SEQ, "chan"),
            P(SEQ, None),
            P(SEQ, None),
            P(SEQ, None),
            P(SEQ, None),
            P(None, SEQ, "chan"),
            P(SEQ),
            P("chan"),
            P("chan"),
            P("chan", None),
        ),
        out_specs=P(SEQ, None),
        check_vma=False,
    )
```

```python
import functools

import jax
import jax.numpy as jnp
from jax import lax
from jax.experimental import pallas as pl
from jax.experimental.pallas import tpu as pltpu
from jax.sharding import Mesh
from jax.sharding import PartitionSpec as P

SPAN = 256
POOL = 4
CH = 128
HEAD = 64
LANES = 128
CUTS = 2
SEQ = ("seq_0", "seq_1", "seq_2")
MESH = pl.DeviceIdType.MESH
F32 = jnp.float32
BF = jnp.bfloat16


def log_keep(rate):
    acc = jnp.full_like(rate, 1.0 / 12)
    for n in range(11, 0, -1):
        acc = acc * rate + 1.0 / n
    return -rate * acc


def dot_t(a, b):
    return lax.dot_general(a, b, (((0,), (0,)), ((), ())), preferred_element_type=F32)


def dot_nt(a, b):
    return lax.dot_general(a, b, (((1,), (1,)), ((), ())), preferred_element_type=F32)


def dot(a, b):
    return jnp.dot(a, b, preferred_element_type=F32)


def layer_kernel(
    sizes,
    codes_hbm,
    skip_hbm,
    clip_hbm,
    gain_hbm,
    acts_hbm,
    gate_hbm,
    fk_hbm,
    fq_hbm,
    bk_hbm,
    bq_hbm,
    w_hbm,
    out_ref,
    codes_ref,
    skip_ref,
    clip_ref,
    gain_ref,
    x_ref,
    z_ref,
    fk_ref,
    fq_ref,
    bk_ref,
    bq_ref,
    w_ref,
    y_scr,
    silu_scr,
    st_scr,
    carry_scr,
    cw_scr,
    sbuf,
    recv1,
    pbuf,
    recvp,
    a_scr,
    q_scr,
    zbuf,
    recvz,
    zpbuf,
    recvzp,
    ebuf,
    recv3,
    qbuf,
    recvq,
    part,
    rs_send,
    rs_recv,
    obuf,
    in_sem,
    p1s,
    p1r,
    pps,
    ppr,
    zs,
    zr,
    zps,
    zpr,
    p3s,
    p3r,
    sqs,
    sqr,
    rss,
    rsr,
    ags,
    agr,
    out_sem,
):
    n_z, n_x, n_c, n_y = sizes
    n_p = n_x * n_c
    tokens, width = x_ref.shape
    n_ch = tokens // CH
    n_sp = tokens // SPAN
    heads = width // HEAD
    tiles = width // LANES
    states = fk_ref.shape[1]
    prow = states // n_p
    total_tokens = n_z * n_x * n_c * tokens
    dim = w_ref.shape[1]
    cut_w = dim // CUTS
    ways = [
        (2 * h + i, sign, h, (sign == 1) == (h % 2 == 0))
        for h in range(CUTS)
        for i, sign in enumerate((1, -1))
    ]
    rows_out = tokens // POOL
    orow = rows_out // n_y

    iz = lax.axis_index("seq_0")
    ix = lax.axis_index("seq_1")
    ic = lax.axis_index("seq_2")
    iy = lax.axis_index("chan")
    me = ix * n_c + ic

    def plane_peer(k, sign=1):
        px = lax.rem(ix + sign * (k // n_c) + n_x, n_x)
        pc = lax.rem(ic + sign * (k % n_c) + n_c, n_c)
        return px, pc, px * n_c + pc

    def z_peer(k, sign=1):
        return lax.rem(iz + sign * k + n_z, n_z)

    def y_peer(k, sign=1):
        return lax.rem(iy + sign * k + 2 * n_y, n_y)

    loads = [
        pltpu.make_async_copy(src, dst, in_sem.at[n])
        for n, (src, dst) in enumerate(
            (
                (codes_hbm, codes_ref),
                (clip_hbm, clip_ref),
                (acts_hbm, x_ref),
                (fk_hbm, fk_ref),
                (bk_hbm, bk_ref),
                (fq_hbm, fq_ref),
                (bq_hbm, bq_ref),
                (skip_hbm, skip_ref),
                (gate_hbm, z_ref),
                (gain_hbm, gain_ref),
                (w_hbm, w_ref),
            )
        )
    ]
    for load in loads[:5]:
        load.start()

    def need(*which):
        for n in which:
            loads[n].wait()

    sent = []

    for d in range(2):
        for q in range(n_z):
            recvz[d, q] = jnp.zeros((prow, width), BF)

    barrier = pltpu.get_barrier_semaphore()
    for k in range(1, n_p):
        px, pc, _ = plane_peer(k)
        pl.semaphore_signal(
            barrier, inc=1, device_id={"seq_1": px, "seq_2": pc}, device_id_type=MESH
        )
    for k in range(1, n_z):
        pl.semaphore_signal(barrier, inc=1, device_id={"seq_0": z_peer(k)}, device_id_type=MESH)
    for k in range(1, n_y):
        pl.semaphore_signal(barrier, inc=1, device_id={"chan": y_peer(k)}, device_id_type=MESH)

    need(0, 1)
    low = lax.broadcasted_iota(jnp.int32, (1, LANES), 1) < HEAD
    logs, scal = [], []
    for d in range(2):
        logs.append([])
        scal.append([])
        for s in range(n_sp):
            rates = [
                jnp.full((1, LANES), codes_ref[d, s, h].astype(F32)) * (1.0 / (32.0 * total_tokens))
                for h in range(heads)
            ]
            logs[d].append([log_keep(r) for r in rates])
            scal[d].append([jnp.sqrt(r * (2.0 - r)) for r in rates])

    def as_row(items):
        return jnp.concatenate(
            [jnp.where(low, items[2 * t], items[2 * t + 1]) for t in range(tiles)], axis=1
        )

    log_row = [[as_row(logs[d][s]) for s in range(n_sp)] for d in range(2)]
    scal_row = [[as_row(scal[d][s]) for s in range(n_sp)] for d in range(2)]

    rows = lax.broadcasted_iota(jnp.int32, (CH, CH), 0)
    cols = lax.broadcasted_iota(jnp.int32, (CH, CH), 1)
    lower = rows >= cols
    upper = rows <= cols
    starts = clip_ref[...].astype(F32).astype(BF)
    seg_row = dot(starts, upper.astype(F32).astype(BF))
    seg_col = dot_nt(lower.astype(F32).astype(BF), starts)
    seg_c = [seg_col[:, a : a + 1] for a in range(n_ch)]
    fin = [seg_row[a : a + 1, CH - 1 : CH] for a in range(n_ch)]
    first_m = [(seg_c[a] == 0.0).astype(F32) for a in range(n_ch)]
    last_m = [(seg_c[a] == fin[a]).astype(F32) for a in range(n_ch)]
    clear = [(fin[a] == 0.0).astype(F32) for a in range(n_ch)]
    passing = [
        [jnp.exp(float(CH) * log_row[d][a * CH // SPAN]) * clear[a] for a in range(n_ch)]
        for d in range(2)
    ]

    step_f = lax.broadcasted_iota(jnp.int32, (CH, width), 0).astype(F32)

    def growth(d):
        steps = CH - 1.0 - step_f if d == 0 else step_f
        return [jnp.exp(log_row[d][s] * steps) * scal_row[d][s] for s in range(n_sp)]

    grow = {1: growth(1)}
    need(2, 3, 4)
    for load in loads[5:9]:
        load.start()

    def chunk(a):
        return pl.ds(a * CH, CH)

    through = [[None] * n_ch, [None] * n_ch]
    for d in range(2):
        left = jnp.ones((1, width), F32)
        for a in range(n_ch) if d == 0 else range(n_ch - 1, -1, -1):
            through[d][a] = left
            left = passing[d][a] * left
        for t in range(tiles):
            pbuf[d * tiles + t : d * tiles + t + 1, :] = left[:, t * LANES : (t + 1) * LANES]

    def own_states(d):
        keys_ref = (fk_ref, bk_ref)[d]
        mask = (last_m, first_m)[d]
        state = None
        for a in range(n_ch) if d == 0 else range(n_ch - 1, -1, -1):
            if state is not None:
                st_scr[d, a] = state
            scaled = (x_ref[chunk(a), :].astype(F32) * (grow[d][a * CH // SPAN] * mask[a])).astype(BF)
            local = dot_t(keys_ref[chunk(a), :], scaled)
            state = local if state is None else passing[d][a] * state + local
        for j in range(n_p):
            sbuf[j, d] = state[j * prow : (j + 1) * prow, :].astype(BF)

    own_states(1)
    pl.semaphore_wait(barrier, (n_p - 1) + (n_z - 1) + (n_y - 1))

    def pp_copy(k, sign=1):
        px, pc, pj = plane_peer(k, sign)
        return pltpu.make_async_remote_copy(
            pbuf,
            recvp.at[me if sign == 1 else pj],
            pps.at[k],
            ppr.at[k],
            device_id={"seq_1": px, "seq_2": pc},
            device_id_type=MESH,
        )

    def p1_copy(d, k, sign=1):
        px, pc, pj = plane_peer(k, sign)
        return pltpu.make_async_remote_copy(
            sbuf.at[pj, d],
            recv1.at[me if sign == 1 else pj, d],
            p1s.at[d, k],
            p1r.at[d, k],
            device_id={"seq_1": px, "seq_2": pc},
            device_id_type=MESH,
        )

    def go(copy):
        copy.start()
        sent.append(copy)

    far_first = sorted(range(1, n_p), key=lambda k: -min(k // n_c, n_x - k // n_c))
    for k in far_first:
        go(pp_copy(k))
    for k in far_first:
        go(p1_copy(1, k))
    grow[0] = growth(0)
    own_states(0)
    for k in far_first:
        go(p1_copy(0, k))
    recv1[me] = sbuf[me]
    recvp[me] = pbuf[...]

    need(5, 6, 7)
    for load in loads[9:]:
        load.start()
    apart = jnp.abs(rows - cols).astype(F32)
    left_m = jnp.where(low, 1.0, 0.0).astype(BF)
    right_m = jnp.where(low, 0.0, 1.0).astype(BF)
    for s in range(n_sp):
        decay = [
            jnp.exp(apart * jnp.where(lower, logs[0][s][h], logs[1][s][h])) for h in range(heads)
        ]
        for a in range(s * SPAN // CH, (s + 1) * SPAN // CH):
            same = seg_c[a] == seg_row[a : a + 1, :]
            ahead = jnp.where(
                same & lower, dot_nt(fq_ref[chunk(a), :], fk_ref[chunk(a), :]), 0.0
            )
            behind = jnp.where(
                same & upper, dot_nt(bq_ref[chunk(a), :], bk_ref[chunk(a), :]), 0.0
            )
            for t in range(tiles):
                pair = jnp.concatenate(
                    [
                        (
                            decay[h] * (scal[0][s][h] * ahead + scal[1][s][h] * behind)
                        ).astype(BF)
                        for h in (2 * t, 2 * t + 1)
                    ],
                    axis=1,
                )
                lanes = pl.ds(t * LANES, LANES)
                xt = x_ref[chunk(a), lanes]
                both = jnp.concatenate([xt * left_m, xt * right_m], axis=0)
                skip = jnp.where(low, skip_ref[2 * t], skip_ref[2 * t + 1])
                y_scr[chunk(a), lanes] = dot(pair, both) + skip * xt.astype(F32)

    def pass_row(ref, d):
        return jnp.concatenate(
            [ref[d * tiles + t : d * tiles + t + 1, :] for t in range(tiles)], axis=1
        )

    def z_way(k, sign=1):
        pz = z_peer(k, sign)
        return pz, iz if sign == 1 else pz

    def zp_copy(k, sign=1):
        pz, slot = z_way(k, sign)
        return pltpu.make_async_remote_copy(
            zpbuf,
            recvzp.at[slot],
            zps.at[k],
            zpr.at[k],
            device_id={"seq_0": pz},
            device_id_type=MESH,
        )

    z_far_first = sorted(range(1, n_z), key=lambda k: -min(k, n_z - k))
    for k in range(1, n_p):
        pp_copy(k, -1).wait_recv()
    for d in range(2):
        left = jnp.ones((1, width), F32)
        for q in range(n_p) if d == 0 else range(n_p - 1, -1, -1):
            q_scr[d, q] = jnp.broadcast_to(left, (8, width))
            left = pass_row(recvp.at[q], d) * left
        for t in range(tiles):
            zpbuf[d * tiles + t : d * tiles + t + 1, :] = left[:, t * LANES : (t + 1) * LANES]
    for k in z_far_first:
        go(zp_copy(k))
    recvzp[iz] = zpbuf[...]

    def z_copy(d, k, sign=1):
        pz, slot = z_way(k, sign)
        return pltpu.make_async_remote_copy(
            zbuf.at[d],
            recvz.at[d, slot],
            zs.at[k],
            zr.at[k],
            device_id={"seq_0": pz},
            device_id_type=MESH,
        )

    def above(q):
        return q > iz

    def below(q):
        return q < iz

    def send_total(d, k):
        @pl.when((above, below)[d](z_peer(k)))
        def _():
            z_copy(d, k).start()

    def total_arrived(d, k):
        @pl.when((below, above)[d](z_peer(k, -1)))
        def _():
            z_copy(d, k, -1).wait_recv()

    for d in (1, 0):
        for k in range(1, n_p):
            p1_copy(d, k, -1).wait_recv()
        state = jnp.zeros((prow, width), F32)
        for q in range(n_p) if d == 0 else range(n_p - 1, -1, -1):
            a_scr[d, q] = state
            state = pass_row(recvp.at[q], d) * state + recv1[q, d].astype(F32)
        zbuf[d] = state.astype(BF)
        for k in z_far_first:
            send_total(d, k)

    need(8)
    for a in range(n_ch):
        v = z_ref[chunk(a), :].astype(F32)
        silu_scr[chunk(a), :] = v / (1.0 + jnp.exp(-v))
    for s in range(n_sp):
        cw_scr[0, s] = jnp.exp(log_row[0][s] * (step_f + 1.0))
        cw_scr[1, s] = jnp.exp(log_row[1][s] * (float(CH) - step_f))

    for a in range(n_ch):
        silu = silu_scr[chunk(a), :]
        local = y_scr[chunk(a), :]
        for d in range(2):
            first = a == (0 if d == 0 else n_ch - 1)
            reach = cw_scr[d, a * CH // SPAN] * (first_m, last_m)[d][a]
            if first:
                carry_scr[d, a] = reach * silu
            else:
                queries = (fq_ref, bq_ref)[d][chunk(a), :]
                local = local + reach * dot(queries, st_scr[d, a].astype(BF))
                carry_scr[d, a] = reach * silu * through[d][a]
        y_scr[chunk(a), :] = local * silu

    def p3_copy(d, k, sign=1):
        px, pc, pj = plane_peer(k, sign)
        return pltpu.make_async_remote_copy(
            ebuf.at[pj, d],
            recv3.at[me if sign == 1 else pj, d],
            p3s.at[d, k],
            p3r.at[d, k],
            device_id={"seq_1": px, "seq_2": pc},
            device_id_type=MESH,
        )

    for k in range(1, n_z):
        zp_copy(k, -1).wait_recv()
    for d in (1, 0):
        for k in range(1, n_z):
            total_arrived(d, k)
        state = jnp.zeros((prow, width), F32)
        for q in range(n_z) if d == 0 else range(n_z - 1, -1, -1):
            new = pass_row(recvzp.at[q], d) * state + recvz[d, q].astype(F32)
            state = jnp.where((below, above)[d](q), new, state)
        for q in range(n_p):
            ebuf[q, d] = (a_scr[d, q] + q_scr[d, q][0:1, :] * state).astype(BF)
        for k in far_first:
            go(p3_copy(d, k))
        recv3[me, d] = ebuf[me, d]

    def entering_part(d, a):
        entering = jnp.concatenate([recv3[q, d] for q in range(n_p)], axis=0)
        return carry_scr[d, a] * dot((fq_ref, bq_ref)[d][chunk(a), :], entering)

    for k in range(1, n_p):
        p3_copy(1, k, -1).wait_recv()
    for a in range(n_ch):
        y_scr[chunk(a), :] += entering_part(1, a)
    for k in range(1, n_p):
        p3_copy(0, k, -1).wait_recv()
    for a in range(n_ch):
        gated = y_scr[chunk(a), :] + entering_part(0, a)
        y_scr[chunk(a), :] = gated
        squares = gated * gated
        lanes_sum = squares[:, :LANES]
        for t in range(1, tiles):
            lanes_sum = lanes_sum + squares[:, t * LANES : (t + 1) * LANES]
        qbuf[a : a + 1, :] = jnp.sum(lanes_sum.T, axis=0, keepdims=True)

    def q_copy(k, sign=1):
        py = y_peer(k, sign)
        return pltpu.make_async_remote_copy(
            qbuf,
            recvq.at[iy if sign == 1 else py],
            sqs.at[k],
            sqr.at[k],
            device_id={"chan": py},
            device_id_type=MESH,
        )

    for k in sorted(range(1, n_y), key=lambda k: -min(k, n_y - k)):
        go(q_copy(k))
    recvq[iy] = qbuf[...]
    need(9)
    gain = gain_ref[...]
    for a in range(n_ch):
        y_scr[chunk(a), :] = y_scr[chunk(a), :] * gain
    for k in range(1, n_y):
        q_copy(k, -1).wait_recv()
    squares = recvq[0]
    for k in range(1, n_y):
        squares = squares + recvq[k]
    inv = lax.rsqrt(squares / float(n_y * width) + 1e-05)

    pool = jnp.where(
        lax.broadcasted_iota(jnp.int32, (CH // POOL, CH), 0)
        == lax.broadcasted_iota(jnp.int32, (CH // POOL, CH), 1) // POOL,
        1.0 / POOL,
        0.0,
    ).astype(BF)
    pooled = []
    for a in range(n_ch):
        inv_col = jnp.broadcast_to(inv[a : a + 1, :], (CH, LANES)).T
        inv_full = jnp.concatenate([inv_col] * tiles, axis=1)
        hidden = (y_scr[chunk(a), :] * inv_full).astype(BF)
        pooled.append(dot(pool, hidden))
    pooled = jnp.concatenate(pooled, axis=0)
    pooled = pooled.astype(BF)
    def lanes_of(h):
        return pl.ds(h * cut_w, cut_w)

    def rs_copy(n, slot, sign, hops):
        return pltpu.make_async_remote_copy(
            rs_send.at[n, slot],
            rs_recv.at[n, slot],
            rss.at[n, slot],
            rsr.at[n, slot],
            device_id={"chan": y_peer(sign * hops)},
            device_id_type=MESH,
        )

    def send_part(n, slot, sign, h, away, hops):
        rs_send[n, slot] = part[y_peer(sign * away), :, lanes_of(h)].astype(BF)
        go(rs_copy(n, slot, sign, hops))

    need(10)
    for c in range(2):
        cut = pl.ds(c * (dim // 2), dim // 2)
        result = dot(pooled, w_ref[:, cut])
        for p in range(n_y):
            part[p, :, cut] = result[p * orow : (p + 1) * orow, :]
        mine = [way for way in ways if way[2] * 2 // CUTS == c]
        for n, sign, h, far in mine:
            if far:
                send_part(n, 0, sign, h, 4, 2)
        for n, sign, h, far in mine:
            send_part(n, 1, sign, h, 3, 1)
    for n, sign, h, far in ways:
        send_part(n, 2, sign, h, 1, 1)
    for n, sign, h, far in ways:
        value = part[y_peer(2 * sign), :, lanes_of(h)]
        rs_copy(n, 1, sign, 1).wait_recv()
        value = value + rs_recv[n, 1].astype(F32)
        if far:
            rs_copy(n, 0, sign, 2).wait_recv()
            value = value + rs_recv[n, 0].astype(F32)
        rs_send[n, 3] = value.astype(BF)
        go(rs_copy(n, 3, sign, 2))

    def ag_copy(n, slot, sign, h, hops, rows_from):
        p = pl.multiple_of(y_peer(rows_from) * orow, orow)
        view = out_ref.at[pl.ds(p, orow), lanes_of(h)]
        return pltpu.make_async_remote_copy(
            obuf.at[:, lanes_of(h)] if rows_from == 0 else view,
            view,
            ags.at[n, slot],
            agr.at[n, slot],
            device_id={"chan": y_peer(sign * hops)},
            device_id_type=MESH,
        )

    for h in range(CUTS):
        value = part[iy, :, lanes_of(h)]
        for n, sign, hh, far in ways:
            if hh == h:
                rs_copy(n, 2, sign, 1).wait_recv()
                value = value + rs_recv[n, 2].astype(F32)
                rs_copy(n, 3, sign, 2).wait_recv()
                value = value + rs_recv[n, 3].astype(F32)
        obuf[:, lanes_of(h)] = value.astype(BF)
        for n, sign, hh, far in ways:
            if hh == h:
                go(ag_copy(n, 0, sign, h, 2, 0))
                go(ag_copy(n, 1, sign, h, 1, 0))
    done = pltpu.make_async_copy(
        obuf, out_ref.at[pl.ds(pl.multiple_of(iy * orow, orow), orow), :], out_sem
    )
    done.start()
    for n, sign, h, far in ways:
        ag_copy(n, 0, sign, h, 2, -2 * sign).wait_recv()
        if far:
            go(ag_copy(n, 3, sign, h, 2, -2 * sign))
        go(ag_copy(n, 2, sign, h, 1, -2 * sign))
    for n, sign, h, far in ways:
        ag_copy(n, 1, sign, h, 1, -sign).wait_recv()
        ag_copy(n, 2, sign, h, 1, -3 * sign).wait_recv()
        if far:
            ag_copy(n, 3, sign, h, 2, -4 * sign).wait_recv()
    done.wait()
    for k in range(1, n_z):
        z_copy(0, k).wait_send()
    for copy in sent:
        copy.wait_send()


def body(
    inner_acts,
    gate_input,
    forward_keys,
    forward_queries,
    backward_keys,
    backward_queries,
    decay_codes,
    clip_start,
    skip_gain,
    norm_gain,
    out_weight,
):
    sizes = tuple(lax.axis_size(a) for a in SEQ) + (lax.axis_size("chan"),)
    n_z, n_x, n_c, n_y = sizes
    n_p = n_x * n_c
    tokens, width = inner_acts.shape
    states = forward_keys.shape[1]
    dim = out_weight.shape[1]
    n_ch, n_sp = tokens // CH, tokens // SPAN
    prow = states // n_p
    rows_out = tokens // POOL
    orow = rows_out // n_y
    steps = 4
    vmem = pltpu.VMEM
    dma = pltpu.SemaphoreType.DMA
    scratch = [
        pltpu.SMEM(decay_codes.shape, jnp.int32),
        pltpu.SMEM(skip_gain.shape, F32),
        vmem((n_ch, CH), jnp.int32),
        vmem((1, width), F32),
        vmem((tokens, width), BF),
        vmem((tokens, width), BF),
        vmem((tokens, states), BF),
        vmem((tokens, states), BF),
        vmem((tokens, states), BF),
        vmem((tokens, states), BF),
        vmem(out_weight.shape, BF),
        vmem((tokens, width), F32),
        vmem((tokens, width), F32),
        vmem((2, n_ch, states, width), F32),
        vmem((2, n_ch, CH, width), F32),
        vmem((2, n_sp, CH, width), F32),
        vmem((n_p, 2, prow, width), BF),
        vmem((n_p, 2, prow, width), BF),
        vmem((8, LANES), F32),
        vmem((n_p, 8, LANES), F32),
        vmem((2, n_p, prow, width), F32),
        vmem((2, n_p, 8, width), F32),
        vmem((2, prow, width), BF),
        vmem((2, n_z, prow, width), BF),
        vmem((8, LANES), F32),
        vmem((n_z, 8, LANES), F32),
        vmem((n_p, 2, prow, width), BF),
        vmem((n_p, 2, prow, width), BF),
        vmem((n_ch, LANES), F32),
        vmem((n_y, n_ch, LANES), F32),
        vmem((n_y, orow, dim), F32),
        vmem((2 * CUTS, steps, orow, dim // CUTS), BF),
        vmem((2 * CUTS, steps, orow, dim // CUTS), BF),
        vmem((orow, dim), BF),
        dma((11,)),
        dma((2, n_p)),
        dma((2, n_p)),
        dma((n_p,)),
        dma((n_p,)),
        dma((n_z,)),
        dma((n_z,)),
        dma((n_z,)),
        dma((n_z,)),
        dma((2, n_p)),
        dma((2, n_p)),
        dma((n_y,)),
        dma((n_y,)),
        dma((2 * CUTS, steps)),
        dma((2 * CUTS, steps)),
        dma((2 * CUTS, steps)),
        dma((2 * CUTS, steps)),
        dma,
    ]
    return pl.pallas_call(
        functools.partial(layer_kernel, sizes),
        out_shape=jax.ShapeDtypeStruct((rows_out, dim), BF),
        in_specs=[pl.BlockSpec(memory_space=pltpu.HBM)] * 11,
        out_specs=pl.BlockSpec(memory_space=pl.ANY),
        scratch_shapes=scratch,
        compiler_params=pltpu.CompilerParams(
            collective_id=0, has_side_effects=True, vmem_limit_bytes=40 << 20
        ),
        name="layer",
    )(*(pltpu.with_memory_space_constraint(v, pltpu.HBM) for v in (
        decay_codes,
        skip_gain,
        clip_start.reshape(n_ch, CH),
        norm_gain.reshape(1, width),
        inner_acts,
        gate_input,
        forward_keys,
        forward_queries,
        backward_keys,
        backward_queries,
        out_weight,
    )))


def solution(mesh):
    torus = Mesh(
        mesh.devices.reshape(8, 4, 2, mesh.shape["chan"]), ("seq_0", "seq_1", "seq_2", "chan")
    )
    return jax.shard_map(
        body,
        mesh=torus,
        in_specs=(
            P(SEQ, "chan"),
            P(SEQ, "chan"),
            P(SEQ, None),
            P(SEQ, None),
            P(SEQ, None),
            P(SEQ, None),
            P(None, SEQ, "chan"),
            P(SEQ),
            P("chan"),
            P("chan"),
            P("chan", None),
        ),
        out_specs=P(SEQ, None),
        check_vma=False,
    )
```

```python
import functools

import jax
import jax.numpy as jnp
from jax import lax
from jax.experimental import pallas as pl
from jax.experimental.pallas import tpu as pltpu
from jax.sharding import Mesh
from jax.sharding import PartitionSpec as P

SPAN = 256
POOL = 4
CH = 128
HEAD = 64
LANES = 128
CUTS = 2
SEQ = ("seq_0", "seq_1", "seq_2")
MESH = pl.DeviceIdType.MESH
F32 = jnp.float32
BF = jnp.bfloat16


def log_keep(rate):
    acc = jnp.full_like(rate, 1.0 / 12)
    for n in range(11, 0, -1):
        acc = acc * rate + 1.0 / n
    return -rate * acc


def dot_t(a, b):
    return lax.dot_general(a, b, (((0,), (0,)), ((), ())), preferred_element_type=F32)


def dot_nt(a, b):
    return lax.dot_general(a, b, (((1,), (1,)), ((), ())), preferred_element_type=F32)


def dot(a, b):
    return jnp.dot(a, b, preferred_element_type=F32)


def layer_kernel(
    sizes,
    codes_hbm,
    skip_hbm,
    clip_hbm,
    gain_hbm,
    acts_hbm,
    gate_hbm,
    fk_hbm,
    fq_hbm,
    bk_hbm,
    bq_hbm,
    w_hbm,
    out_ref,
    codes_ref,
    skip_ref,
    clip_ref,
    gain_ref,
    x_ref,
    z_ref,
    fk_ref,
    fq_ref,
    bk_ref,
    bq_ref,
    w_ref,
    y_scr,
    silu_scr,
    st_scr,
    carry_scr,
    cw_scr,
    sbuf,
    recv1,
    pbuf,
    recvp,
    a_scr,
    q_scr,
    zbuf,
    recvz,
    zpbuf,
    recvzp,
    ebuf,
    recv3,
    qbuf,
    recvq,
    part,
    rs_send,
    rs_recv,
    obuf,
    in_sem,
    p1s,
    p1r,
    pps,
    ppr,
    zs,
    zr,
    zps,
    zpr,
    p3s,
    p3r,
    sqs,
    sqr,
    rss,
    rsr,
    ags,
    agr,
    out_sem,
):
    n_z, n_x, n_c, n_y = sizes
    n_p = n_x * n_c
    tokens, width = x_ref.shape
    n_ch = tokens // CH
    n_sp = tokens // SPAN
    heads = width // HEAD
    tiles = width // LANES
    states = fk_ref.shape[1]
    prow = states // n_p
    total_tokens = n_z * n_x * n_c * tokens
    dim = w_ref.shape[1]
    cut_w = dim // CUTS
    ways = [
        (2 * h + i, sign, h, (sign == 1) == (h % 2 == 0))
        for h in range(CUTS)
        for i, sign in enumerate((1, -1))
    ]
    rows_out = tokens // POOL
    orow = rows_out // n_y

    iz = lax.axis_index("seq_0")
    ix = lax.axis_index("seq_1")
    ic = lax.axis_index("seq_2")
    iy = lax.axis_index("chan")
    me = ix * n_c + ic

    def plane_peer(k, sign=1):
        px = lax.rem(ix + sign * (k // n_c) + n_x, n_x)
        pc = lax.rem(ic + sign * (k % n_c) + n_c, n_c)
        return px, pc, px * n_c + pc

    def z_peer(k, sign=1):
        return lax.rem(iz + sign * k + n_z, n_z)

    def y_peer(k, sign=1):
        return lax.rem(iy + sign * k + 2 * n_y, n_y)

    loads = [
        pltpu.make_async_copy(src, dst, in_sem.at[n])
        for n, (src, dst) in enumerate(
            (
                (codes_hbm, codes_ref),
                (clip_hbm, clip_ref),
                (acts_hbm, x_ref),
                (fk_hbm, fk_ref),
                (bk_hbm, bk_ref),
                (fq_hbm, fq_ref),
                (bq_hbm, bq_ref),
                (skip_hbm, skip_ref),
                (gate_hbm, z_ref),
                (gain_hbm, gain_ref),
                (w_hbm, w_ref),
            )
        )
    ]
    for load in loads[:5]:
        load.start()

    def need(*which):
        for n in which:
            loads[n].wait()

    sent = []

    for d in range(2):
        for q in range(n_z):
            recvz[d, q] = jnp.zeros((prow, width), BF)

    barrier = pltpu.get_barrier_semaphore()
    for k in range(1, n_p):
        px, pc, _ = plane_peer(k)
        pl.semaphore_signal(
            barrier, inc=1, device_id={"seq_1": px, "seq_2": pc}, device_id_type=MESH
        )
    for k in range(1, n_z):
        pl.semaphore_signal(barrier, inc=1, device_id={"seq_0": z_peer(k)}, device_id_type=MESH)
    for k in range(1, n_y):
        pl.semaphore_signal(barrier, inc=1, device_id={"chan": y_peer(k)}, device_id_type=MESH)

    need(0, 1)
    low = lax.broadcasted_iota(jnp.int32, (1, LANES), 1) < HEAD
    logs, scal = [], []
    for d in range(2):
        logs.append([])
        scal.append([])
        for s in range(n_sp):
            rates = [
                jnp.full((1, LANES), codes_ref[d, s, h].astype(F32)) * (1.0 / (32.0 * total_tokens))
                for h in range(heads)
            ]
            logs[d].append([log_keep(r) for r in rates])
            scal[d].append([jnp.sqrt(r * (2.0 - r)) for r in rates])

    def as_row(items):
        return jnp.concatenate(
            [jnp.where(low, items[2 * t], items[2 * t + 1]) for t in range(tiles)], axis=1
        )

    log_row = [[as_row(logs[d][s]) for s in range(n_sp)] for d in range(2)]
    scal_row = [[as_row(scal[d][s]) for s in range(n_sp)] for d in range(2)]

    rows = lax.broadcasted_iota(jnp.int32, (CH, CH), 0)
    cols = lax.broadcasted_iota(jnp.int32, (CH, CH), 1)
    lower = rows >= cols
    upper = rows <= cols
    starts = clip_ref[...].astype(F32).astype(BF)
    seg_row = dot(starts, upper.astype(F32).astype(BF))
    seg_col = dot_nt(lower.astype(F32).astype(BF), starts)
    seg_c = [seg_col[:, a : a + 1] for a in range(n_ch)]
    fin = [seg_row[a : a + 1, CH - 1 : CH] for a in range(n_ch)]
    first_m = [(seg_c[a] == 0.0).astype(F32) for a in range(n_ch)]
    last_m = [(seg_c[a] == fin[a]).astype(F32) for a in range(n_ch)]
    clear = [(fin[a] == 0.0).astype(F32) for a in range(n_ch)]
    passing = [
        [jnp.exp(float(CH) * log_row[d][a * CH // SPAN]) * clear[a] for a in range(n_ch)]
        for d in range(2)
    ]

    step_f = lax.broadcasted_iota(jnp.int32, (CH, width), 0).astype(F32)

    def growth(d):
        steps = CH - 1.0 - step_f if d == 0 else step_f
        return [jnp.exp(log_row[d][s] * steps) * scal_row[d][s] for s in range(n_sp)]

    grow = {1: growth(1)}
    need(2, 3, 4)
    for load in loads[5:9]:
        load.start()

    def chunk(a):
        return pl.ds(a * CH, CH)

    through = [[None] * n_ch, [None] * n_ch]
    for d in range(2):
        left = jnp.ones((1, width), F32)
        for a in range(n_ch) if d == 0 else range(n_ch - 1, -1, -1):
            through[d][a] = left
            left = passing[d][a] * left
        for t in range(tiles):
            pbuf[d * tiles + t : d * tiles + t + 1, :] = left[:, t * LANES : (t + 1) * LANES]

    def own_states(d):
        keys_ref = (fk_ref, bk_ref)[d]
        mask = (last_m, first_m)[d]
        state = None
        for a in range(n_ch) if d == 0 else range(n_ch - 1, -1, -1):
            if state is not None:
                st_scr[d, a] = state
            scaled = (x_ref[chunk(a), :].astype(F32) * (grow[d][a * CH // SPAN] * mask[a])).astype(BF)
            local = dot_t(keys_ref[chunk(a), :], scaled)
            state = local if state is None else passing[d][a] * state + local
        for j in range(n_p):
            sbuf[j, d] = state[j * prow : (j + 1) * prow, :].astype(BF)

    own_states(1)
    pl.semaphore_wait(barrier, (n_p - 1) + (n_z - 1) + (n_y - 1))

    def pp_copy(k, sign=1):
        px, pc, pj = plane_peer(k, sign)
        return pltpu.make_async_remote_copy(
            pbuf,
            recvp.at[me if sign == 1 else pj],
            pps.at[k],
            ppr.at[k],
            device_id={"seq_1": px, "seq_2": pc},
            device_id_type=MESH,
        )

    def p1_copy(d, k, sign=1):
        px, pc, pj = plane_peer(k, sign)
        return pltpu.make_async_remote_copy(
            sbuf.at[pj, d],
            recv1.at[me if sign == 1 else pj, d],
            p1s.at[d, k],
            p1r.at[d, k],
            device_id={"seq_1": px, "seq_2": pc},
            device_id_type=MESH,
        )

    def go(copy):
        copy.start()
        sent.append(copy)

    far_first = sorted(range(1, n_p), key=lambda k: -min(k // n_c, n_x - k // n_c))
    for k in far_first:
        go(pp_copy(k))
    for k in far_first:
        go(p1_copy(1, k))
    grow[0] = growth(0)
    own_states(0)
    for k in far_first:
        go(p1_copy(0, k))
    recv1[me] = sbuf[me]
    recvp[me] = pbuf[...]

    need(5, 6, 7)
    for load in loads[9:]:
        load.start()
    apart = jnp.abs(rows - cols).astype(F32)
    left_m = jnp.where(low, 1.0, 0.0).astype(BF)
    right_m = jnp.where(low, 0.0, 1.0).astype(BF)
    for s in range(n_sp):
        decay = [
            jnp.exp(apart * jnp.where(lower, logs[0][s][h], logs[1][s][h])) for h in range(heads)
        ]
        for a in range(s * SPAN // CH, (s + 1) * SPAN // CH):
            same = seg_c[a] == seg_row[a : a + 1, :]
            ahead = jnp.where(
                same & lower, dot_nt(fq_ref[chunk(a), :], fk_ref[chunk(a), :]), 0.0
            )
            behind = jnp.where(
                same & upper, dot_nt(bq_ref[chunk(a), :], bk_ref[chunk(a), :]), 0.0
            )
            for t in range(tiles):
                pair = jnp.concatenate(
                    [
                        (
                            decay[h] * (scal[0][s][h] * ahead + scal[1][s][h] * behind)
                        ).astype(BF)
                        for h in (2 * t, 2 * t + 1)
                    ],
                    axis=1,
                )
                lanes = pl.ds(t * LANES, LANES)
                xt = x_ref[chunk(a), lanes]
                both = jnp.concatenate([xt * left_m, xt * right_m], axis=0)
                skip = jnp.where(low, skip_ref[2 * t], skip_ref[2 * t + 1])
                y_scr[chunk(a), lanes] = dot(pair, both) + skip * xt.astype(F32)

    def pass_row(ref, d):
        return jnp.concatenate(
            [ref[d * tiles + t : d * tiles + t + 1, :] for t in range(tiles)], axis=1
        )

    def z_way(k, sign=1):
        pz = z_peer(k, sign)
        return pz, iz if sign == 1 else pz

    def zp_copy(k, sign=1):
        pz, slot = z_way(k, sign)
        return pltpu.make_async_remote_copy(
            zpbuf,
            recvzp.at[slot],
            zps.at[k],
            zpr.at[k],
            device_id={"seq_0": pz},
            device_id_type=MESH,
        )

    z_far_first = sorted(range(1, n_z), key=lambda k: -min(k, n_z - k))
    for k in range(1, n_p):
        pp_copy(k, -1).wait_recv()
    for d in range(2):
        left = jnp.ones((1, width), F32)
        for q in range(n_p) if d == 0 else range(n_p - 1, -1, -1):
            q_scr[d, q] = jnp.broadcast_to(left, (8, width))
            left = pass_row(recvp.at[q], d) * left
        for t in range(tiles):
            zpbuf[d * tiles + t : d * tiles + t + 1, :] = left[:, t * LANES : (t + 1) * LANES]
    for k in z_far_first:
        go(zp_copy(k))
    recvzp[iz] = zpbuf[...]

    def z_copy(d, k, sign=1):
        pz, slot = z_way(k, sign)
        return pltpu.make_async_remote_copy(
            zbuf.at[d],
            recvz.at[d, slot],
            zs.at[k],
            zr.at[k],
            device_id={"seq_0": pz},
            device_id_type=MESH,
        )

    def above(q):
        return q > iz

    def below(q):
        return q < iz

    def send_total(d, k):
        @pl.when((above, below)[d](z_peer(k)))
        def _():
            z_copy(d, k).start()

    def total_arrived(d, k):
        @pl.when((below, above)[d](z_peer(k, -1)))
        def _():
            z_copy(d, k, -1).wait_recv()

    for d in (1, 0):
        for k in range(1, n_p):
            p1_copy(d, k, -1).wait_recv()
        state = jnp.zeros((prow, width), F32)
        for q in range(n_p) if d == 0 else range(n_p - 1, -1, -1):
            a_scr[d, q] = state
            state = pass_row(recvp.at[q], d) * state + recv1[q, d].astype(F32)
        zbuf[d] = state.astype(BF)
        for k in z_far_first:
            send_total(d, k)

    need(8)
    for a in range(n_ch):
        v = z_ref[chunk(a), :].astype(F32)
        silu_scr[chunk(a), :] = v / (1.0 + jnp.exp(-v))
    for s in range(n_sp):
        cw_scr[0, s] = jnp.exp(log_row[0][s] * (step_f + 1.0))
        cw_scr[1, s] = jnp.exp(log_row[1][s] * (float(CH) - step_f))

    for a in range(n_ch):
        silu = silu_scr[chunk(a), :]
        local = y_scr[chunk(a), :]
        for d in range(2):
            first = a == (0 if d == 0 else n_ch - 1)
            reach = cw_scr[d, a * CH // SPAN] * (first_m, last_m)[d][a]
            if first:
                carry_scr[d, a] = reach * silu
            else:
                queries = (fq_ref, bq_ref)[d][chunk(a), :]
                local = local + reach * dot(queries, st_scr[d, a].astype(BF))
                carry_scr[d, a] = reach * silu * through[d][a]
        y_scr[chunk(a), :] = local * silu

    def p3_copy(d, k, sign=1):
        px, pc, pj = plane_peer(k, sign)
        return pltpu.make_async_remote_copy(
            ebuf.at[pj, d],
            recv3.at[me if sign == 1 else pj, d],
            p3s.at[d, k],
            p3r.at[d, k],
            device_id={"seq_1": px, "seq_2": pc},
            device_id_type=MESH,
        )

    for k in range(1, n_z):
        zp_copy(k, -1).wait_recv()
    for d in (1, 0):
        for k in range(1, n_z):
            total_arrived(d, k)
        state = jnp.zeros((prow, width), F32)
        for q in range(n_z) if d == 0 else range(n_z - 1, -1, -1):
            new = pass_row(recvzp.at[q], d) * state + recvz[d, q].astype(F32)
            state = jnp.where((below, above)[d](q), new, state)
        for q in range(n_p):
            ebuf[q, d] = (a_scr[d, q] + q_scr[d, q][0:1, :] * state).astype(BF)
        for k in far_first:
            go(p3_copy(d, k))
        recv3[me, d] = ebuf[me, d]

    def entering_part(d, a):
        entering = jnp.concatenate([recv3[q, d] for q in range(n_p)], axis=0)
        return carry_scr[d, a] * dot((fq_ref, bq_ref)[d][chunk(a), :], entering)

    for k in range(1, n_p):
        p3_copy(1, k, -1).wait_recv()
    for a in range(n_ch):
        y_scr[chunk(a), :] += entering_part(1, a)
    for k in range(1, n_p):
        p3_copy(0, k, -1).wait_recv()
    for a in range(n_ch):
        gated = y_scr[chunk(a), :] + entering_part(0, a)
        y_scr[chunk(a), :] = gated
        squares = gated * gated
        lanes_sum = squares[:, :LANES]
        for t in range(1, tiles):
            lanes_sum = lanes_sum + squares[:, t * LANES : (t + 1) * LANES]
        qbuf[a : a + 1, :] = jnp.sum(lanes_sum.T, axis=0, keepdims=True)

    def q_copy(k, sign=1):
        py = y_peer(k, sign)
        return pltpu.make_async_remote_copy(
            qbuf,
            recvq.at[iy if sign == 1 else py],
            sqs.at[k],
            sqr.at[k],
            device_id={"chan": py},
            device_id_type=MESH,
        )

    for k in sorted(range(1, n_y), key=lambda k: -min(k, n_y - k)):
        go(q_copy(k))
    recvq[iy] = qbuf[...]
    need(9)
    gain = gain_ref[...]
    for a in range(n_ch):
        y_scr[chunk(a), :] = y_scr[chunk(a), :] * gain
    for k in range(1, n_y):
        q_copy(k, -1).wait_recv()
    squares = recvq[0]
    for k in range(1, n_y):
        squares = squares + recvq[k]
    inv = lax.rsqrt(squares / float(n_y * width) + 1e-05)

    pool = jnp.where(
        lax.broadcasted_iota(jnp.int32, (CH // POOL, CH), 0)
        == lax.broadcasted_iota(jnp.int32, (CH // POOL, CH), 1) // POOL,
        1.0 / POOL,
        0.0,
    ).astype(BF)
    pooled = []
    for a in range(n_ch):
        inv_col = jnp.broadcast_to(inv[a : a + 1, :], (CH, LANES)).T
        inv_full = jnp.concatenate([inv_col] * tiles, axis=1)
        hidden = (y_scr[chunk(a), :] * inv_full).astype(BF)
        pooled.append(dot(pool, hidden))
    pooled = jnp.concatenate(pooled, axis=0)
    pooled = pooled.astype(BF)
    def lanes_of(h):
        return pl.ds(h * cut_w, cut_w)

    def rs_copy(n, slot, sign, hops):
        return pltpu.make_async_remote_copy(
            rs_send.at[n, slot],
            rs_recv.at[n, slot],
            rss.at[n, slot],
            rsr.at[n, slot],
            device_id={"chan": y_peer(sign * hops)},
            device_id_type=MESH,
        )

    def send_part(n, slot, sign, h, away, hops):
        rs_send[n, slot] = part[y_peer(sign * away), :, lanes_of(h)].astype(BF)
        go(rs_copy(n, slot, sign, hops))

    need(10)
    for c in range(2):
        cut = pl.ds(c * (dim // 2), dim // 2)
        result = dot(pooled, w_ref[:, cut])
        for p in range(n_y):
            part[p, :, cut] = result[p * orow : (p + 1) * orow, :]
        mine = [way for way in ways if way[2] * 2 // CUTS == c]
        for n, sign, h, far in mine:
            if far:
                send_part(n, 0, sign, h, 4, 2)
        for n, sign, h, far in mine:
            send_part(n, 1, sign, h, 3, 1)
    for n, sign, h, far in ways:
        send_part(n, 2, sign, h, 1, 1)
    for n, sign, h, far in ways:
        value = part[y_peer(2 * sign), :, lanes_of(h)]
        rs_copy(n, 1, sign, 1).wait_recv()
        value = value + rs_recv[n, 1].astype(F32)
        if far:
            rs_copy(n, 0, sign, 2).wait_recv()
            value = value + rs_recv[n, 0].astype(F32)
        rs_send[n, 3] = value.astype(BF)
        go(rs_copy(n, 3, sign, 2))

    def ag_copy(n, slot, sign, h, hops, rows_from):
        p = pl.multiple_of(y_peer(rows_from) * orow, orow)
        view = out_ref.at[pl.ds(p, orow), lanes_of(h)]
        return pltpu.make_async_remote_copy(
            obuf.at[:, lanes_of(h)] if rows_from == 0 else view,
            view,
            ags.at[n, slot],
            agr.at[n, slot],
            device_id={"chan": y_peer(sign * hops)},
            device_id_type=MESH,
        )

    for h in range(CUTS):
        value = part[iy, :, lanes_of(h)]
        for n, sign, hh, far in ways:
            if hh == h:
                rs_copy(n, 2, sign, 1).wait_recv()
                value = value + rs_recv[n, 2].astype(F32)
                rs_copy(n, 3, sign, 2).wait_recv()
                value = value + rs_recv[n, 3].astype(F32)
        obuf[:, lanes_of(h)] = value.astype(BF)
        for n, sign, hh, far in ways:
            if hh == h:
                go(ag_copy(n, 0, sign, h, 2, 0))
    for n, sign, h, far in ways:
        go(ag_copy(n, 1, sign, h, 1, 0))
    done = pltpu.make_async_copy(
        obuf, out_ref.at[pl.ds(pl.multiple_of(iy * orow, orow), orow), :], out_sem
    )
    done.start()
    for n, sign, h, far in ways:
        ag_copy(n, 0, sign, h, 2, -2 * sign).wait_recv()
        if far:
            go(ag_copy(n, 3, sign, h, 2, -2 * sign))
        go(ag_copy(n, 2, sign, h, 1, -2 * sign))
    for n, sign, h, far in ways:
        ag_copy(n, 1, sign, h, 1, -sign).wait_recv()
        ag_copy(n, 2, sign, h, 1, -3 * sign).wait_recv()
        if far:
            ag_copy(n, 3, sign, h, 2, -4 * sign).wait_recv()
    done.wait()
    for k in range(1, n_z):
        z_copy(0, k).wait_send()
    for copy in sent:
        copy.wait_send()


def body(
    inner_acts,
    gate_input,
    forward_keys,
    forward_queries,
    backward_keys,
    backward_queries,
    decay_codes,
    clip_start,
    skip_gain,
    norm_gain,
    out_weight,
):
    sizes = tuple(lax.axis_size(a) for a in SEQ) + (lax.axis_size("chan"),)
    n_z, n_x, n_c, n_y = sizes
    n_p = n_x * n_c
    tokens, width = inner_acts.shape
    states = forward_keys.shape[1]
    dim = out_weight.shape[1]
    n_ch, n_sp = tokens // CH, tokens // SPAN
    prow = states // n_p
    rows_out = tokens // POOL
    orow = rows_out // n_y
    steps = 4
    vmem = pltpu.VMEM
    dma = pltpu.SemaphoreType.DMA
    scratch = [
        pltpu.SMEM(decay_codes.shape, jnp.int32),
        pltpu.SMEM(skip_gain.shape, F32),
        vmem((n_ch, CH), jnp.int32),
        vmem((1, width), F32),
        vmem((tokens, width), BF),
        vmem((tokens, width), BF),
        vmem((tokens, states), BF),
        vmem((tokens, states), BF),
        vmem((tokens, states), BF),
        vmem((tokens, states), BF),
        vmem(out_weight.shape, BF),
        vmem((tokens, width), F32),
        vmem((tokens, width), F32),
        vmem((2, n_ch, states, width), F32),
        vmem((2, n_ch, CH, width), F32),
        vmem((2, n_sp, CH, width), F32),
        vmem((n_p, 2, prow, width), BF),
        vmem((n_p, 2, prow, width), BF),
        vmem((8, LANES), F32),
        vmem((n_p, 8, LANES), F32),
        vmem((2, n_p, prow, width), F32),
        vmem((2, n_p, 8, width), F32),
        vmem((2, prow, width), BF),
        vmem((2, n_z, prow, width), BF),
        vmem((8, LANES), F32),
        vmem((n_z, 8, LANES), F32),
        vmem((n_p, 2, prow, width), BF),
        vmem((n_p, 2, prow, width), BF),
        vmem((n_ch, LANES), F32),
        vmem((n_y, n_ch, LANES), F32),
        vmem((n_y, orow, dim), F32),
        vmem((2 * CUTS, steps, orow, dim // CUTS), BF),
        vmem((2 * CUTS, steps, orow, dim // CUTS), BF),
        vmem((orow, dim), BF),
        dma((11,)),
        dma((2, n_p)),
        dma((2, n_p)),
        dma((n_p,)),
        dma((n_p,)),
        dma((n_z,)),
        dma((n_z,)),
        dma((n_z,)),
        dma((n_z,)),
        dma((2, n_p)),
        dma((2, n_p)),
        dma((n_y,)),
        dma((n_y,)),
        dma((2 * CUTS, steps)),
        dma((2 * CUTS, steps)),
        dma((2 * CUTS, steps)),
        dma((2 * CUTS, steps)),
        dma,
    ]
    return pl.pallas_call(
        functools.partial(layer_kernel, sizes),
        out_shape=jax.ShapeDtypeStruct((rows_out, dim), BF),
        in_specs=[pl.BlockSpec(memory_space=pltpu.HBM)] * 11,
        out_specs=pl.BlockSpec(memory_space=pl.ANY),
        scratch_shapes=scratch,
        compiler_params=pltpu.CompilerParams(
            collective_id=0, has_side_effects=True, vmem_limit_bytes=40 << 20
        ),
        name="layer",
    )(*(pltpu.with_memory_space_constraint(v, pltpu.HBM) for v in (
        decay_codes,
        skip_gain,
        clip_start.reshape(n_ch, CH),
        norm_gain.reshape(1, width),
        inner_acts,
        gate_input,
        forward_keys,
        forward_queries,
        backward_keys,
        backward_queries,
        out_weight,
    )))


def solution(mesh):
    torus = Mesh(
        mesh.devices.reshape(8, 4, 2, mesh.shape["chan"]), ("seq_0", "seq_1", "seq_2", "chan")
    )
    return jax.shard_map(
        body,
        mesh=torus,
        in_specs=(
            P(SEQ, "chan"),
            P(SEQ, "chan"),
            P(SEQ, None),
            P(SEQ, None),
            P(SEQ, None),
            P(SEQ, None),
            P(None, SEQ, "chan"),
            P(SEQ),
            P("chan"),
            P("chan"),
            P("chan", None),
        ),
        out_specs=P(SEQ, None),
        check_vma=False,
    )
```
